32 devices in a mesh: dp: 8 (over z, y), tensor: 4 (over x, core).
Axes of the slice: x: 2, y: 2, z: 4, core: 2. Of those that a mesh axis runs over, the one named last changes fastest.
Arguments:
- tokens: bfloat16 [2, 16384, 768], P(None, ('dp', 'tensor')), may hold values from -6 to 6
- segments: int32 [2, 16384], P(None, 'dp'), may hold values from 0 to 15, never falling along the last dimension, each value on 1 to 2000 neighbouring positions
- timesteps: int32 [2, 8], P(None, 'dp'), may hold values from 0 to 999
- cotangent: bfloat16 [2, 16384, 768], P(None, ('dp', 'tensor')), may hold values from -6 to 6
- w_qkv: bfloat16 [768, 2304], P('dp', 'tensor'), may hold values from -0.21875 to 0.21875
- w_out: bfloat16 [768, 768], P('tensor', 'dp'), may hold values from -2.5 to 2.5
- w_up: bfloat16 [768, 3072], P('dp', 'tensor'), may hold values from -0.21875 to 0.21875
- w_down: bfloat16 [3072, 768], P('tensor', 'dp'), may hold values from -0.109375 to 0.109375
- w_ada: bfloat16 [256, 4608], P(('dp', 'tensor')), may hold values from -0.375 to 0.375
- b_ada: bfloat16 [4608], P(('dp', 'tensor')), may hold values from -3 to 3
Outputs:
- output: bfloat16 [2, 16384, 768], P(None, ('dp', 'tensor'))
- d_tokens: float32 [2, 16384, 768], P(None, ('dp', 'tensor'))
- g_qkv: float32 [768, 2304], P('dp', 'tensor')
- g_out: float32 [768, 768], P('tensor', 'dp')
- g_up: float32 [768, 3072], P('dp', 'tensor')
- g_down: float32 [3072, 768], P('tensor', 'dp')
- g_ada: float32 [256, 4608], P(('dp', 'tensor'))
- g_bias: float32 [4608], P(('dp', 'tensor'))
The draws below stay inside these ranges and needn't reach their ends.
Inputs may be any that keep to these rules, and one draw needn't show every extreme that they name: `segments`: along each micro-batch the numbers never fall; every document covers 1 to 2000 positions, one exactly 2000.
All inputs are finite; a program needn't handle non-finite values.
Results may differ from the reference program's by a relative error of at most 0.014.
The reference program's roundings to bfloat16 on the way count: a program that leaves them out, or rounds other values in their place, can miss the bound.
Values may be sent and summed in bfloat16 or wider, within the bound.
No kernel may reach another device: no remote copies, remote signals or barrier semaphores. Data moves between devices by JAX's collectives and lax.ppermute only.
A program may use at most 192 MiB of HBM per device.

```python
import math
import jax
import jax.numpy as jnp
import numpy as np
from jax import lax

D = 768
HEADS = 12
HD = 64
FF = 3072
TEMB = 256
MB = 2
DOC_MOST = 2000
SEQ_TOK = 16384
DOCS = 16
N_DP = 8


def plant(entries, own_key, low, top_value):
    shape = entries.shape
    spot = [jax.random.randint(jax.random.fold_in(own_key, axis), (), 0, shape[axis]) for axis in range(len(shape))]
    entries = entries.at[tuple(spot)].set(low)
    longest = shape.index(max(shape))
    spot[longest] = (spot[longest] + 1) % shape[longest]
    return entries.at[tuple(spot)].set(top_value)


def block_levels(rng, extent, cuts, low, top_value):
    factor_of, own = 1.0, jax.random.fold_in(rng, 6)
    for dim, parts in cuts:
        heights = jnp.exp(jax.random.uniform(jax.random.fold_in(own, dim), (parts,), jnp.float32, low / len(cuts), top_value / len(cuts)))
        factor_of = factor_of * jnp.repeat(heights, extent[dim] // parts).reshape([-1 if axis == dim else 1 for axis in range(len(extent))])
    return factor_of


def split_up(number_of, total, reach, lean):
    weights = [(1 << 20) // math.isqrt(rank ** lean) + 1 for rank in range(2, number_of + 1)]
    rest, holding = total - reach - (number_of - 1), [1] * (number_of - 1)
    while rest > 0:
        movable = [i for i in range(number_of - 1) if holding[i] < reach]
        pool, left = sum([weights[i] for i in movable]), rest
        for i in movable:
            more = min(reach - holding[i], max(1, left * weights[i] // pool), rest)
            holding[i] = holding[i] + more
            rest = rest - more
    return np.array([reach] + holding)


def uneven_parts(key, number_of, total, reach, skew):
    if number_of == 2:
        one = jax.random.randint(key, (), max(1, total - reach), min(reach, total - 1) + 1)
        return jnp.stack([one, total - one])
    sizes = jnp.asarray(split_up(number_of, total, reach, skew), jnp.int32)
    twos = (number_of - 1) // 2
    donor, taker = sizes[1:1 + 2 * twos:2], sizes[2:2 + 2 * twos:2]
    slack = jnp.minimum(donor - 1, reach - taker)
    shifted = jax.random.randint(jax.random.fold_in(key, 1), (twos,), 0, 1 << 20) % (slack + 1)
    sizes = sizes.at[1:1 + 2 * twos:2].set(donor - shifted).at[2:2 + 2 * twos:2].set(taker + shifted)
    return sizes[jax.random.permutation(jax.random.fold_in(key, 2), number_of)]


def normal_values(key, shape, scale, bound, cuts=(), kind=jnp.bfloat16):
    array = jax.random.normal(key, shape, jnp.float32) * scale
    if len(cuts) > 0:
        array = block_levels(key, shape, cuts, -0.22, 0.18) * array
    return jnp.clip(array, min=-bound, max=bound).astype(kind)


def setup_inputs(seed: int = 0) -> dict:
    streams_of = jax.random.split(jax.random.key(seed), 11)
    tokens = normal_values(streams_of[0], (MB, SEQ_TOK, D), 1.0, 6.0, ((1, 32),))
    segments = jax.vmap(lambda own: jnp.searchsorted(jnp.cumsum(uneven_parts(own, DOCS, SEQ_TOK, DOC_MOST, 0)), jnp.arange(SEQ_TOK), side="right"))(jax.random.split(streams_of[1], MB)).reshape((MB, SEQ_TOK)).astype(jnp.int32)
    timesteps = plant(jax.random.randint(streams_of[2], (MB, N_DP), 0, 1000), jax.random.fold_in(streams_of[2], 1), 0, 999).astype(jnp.int32)
    cotangent = normal_values(streams_of[3], (MB, SEQ_TOK, D), 1.0, 6.0, ((1, 32),))
    w_qkv = normal_values(streams_of[4], (D, 3 * D), D ** -0.5, 0.21875, ((0, 8), (1, 4)))
    w_out = normal_values(streams_of[5], (D, D), (D // 128) ** -0.5, 2.5, ((0, 4), (1, 8)))
    w_up = normal_values(streams_of[6], (D, FF), D ** -0.5, 0.21875, ((0, 8), (1, 4)))
    w_down = normal_values(streams_of[7], (FF, D), FF ** -0.5, 0.109375, ((0, 4), (1, 8)))
    w_ada = normal_values(streams_of[8], (TEMB, 6 * D), TEMB ** -0.5, 0.375, ((0, 32),))
    b_ada = normal_values(streams_of[9], (6 * D,), 0.5, 3.0, ((0, 32),))
    return dict(tokens=tokens, segments=segments, timesteps=timesteps, cotangent=cotangent, w_qkv=w_qkv, w_out=w_out, w_up=w_up, w_down=w_down, w_ada=w_ada, b_ada=b_ada)


EPSILON = 1e-06
MASKED = -1e+30

@jax.custom_vjp
def low(v):
    return lax.optimization_barrier(v.astype(jnp.bfloat16)).astype(jnp.float32)

@jax.custom_vjp
def low_back(v):
    return v

def low_keep(v):
    return (low(v), None)

def low_pass(kept, grad):
    return (grad,)

def back_keep(v):
    return (v, None)

def back_low(kept, grad):
    return (low(grad),)
low.defvjp(low_keep, low_pass)
low_back.defvjp(back_keep, back_low)

def time_features(stamps, feature_count):
    half = feature_count // 2
    freqs = jnp.exp(-math.log(10000.0) * jnp.arange(half, dtype=jnp.float32) / half)
    angles = stamps.astype(jnp.float32)[:, None] * freqs[None, :]
    return jnp.concatenate([jnp.cos(angles), jnp.sin(angles)], axis=1)

def rotate(matrix, turn):
    length = matrix.shape[0]
    half = matrix.shape[-1] // 2
    freqs = jnp.exp(-math.log(10000.0) * jnp.arange(half, dtype=jnp.float32) / half)
    angles = jnp.arange(length, dtype=jnp.float32)[:, None] * freqs[None, :]
    cosine = jnp.cos(angles)[:, None, :]
    sine = turn * jnp.sin(angles)[:, None, :]
    first = matrix[..., :half]
    second = matrix[..., half:]
    return jnp.concatenate([first * cosine - second * sine, first * sine + second * cosine], axis=-1)

def modulate(inputs, shift, stretch):
    center = inputs - lax.optimization_barrier(jnp.mean(inputs, axis=-1, keepdims=True))
    spread = lax.optimization_barrier(jnp.mean(center * center, axis=-1, keepdims=True))
    return center * lax.rsqrt(spread + EPSILON) * (1.0 + stretch) + shift

def attention(queries, key_heads, value_heads, doc_ids):
    length = queries.shape[0]
    block_rows = min(512, length)
    block_count = length // block_rows
    inv_root = 1.0 / math.sqrt(HD)

    def one_block(pieces):
        query_part, doc_part = pieces
        scores = low_back(inv_root * jnp.einsum('qhd,khd->hqk', query_part, key_heads, precision=lax.Precision.HIGHEST))
        allowed = (doc_part[:, None] == doc_ids[None, :])[None]
        scores = jnp.where(allowed, scores, MASKED)
        maximum = lax.optimization_barrier(jnp.max(scores, axis=-1, keepdims=True))
        expo = jnp.exp(scores - maximum)
        chances = low(expo / lax.optimization_barrier(jnp.sum(expo, axis=-1, keepdims=True)))
        return jnp.einsum('hqk,khd->qhd', chances, value_heads, precision=lax.Precision.HIGHEST)
    result = lax.map(jax.checkpoint(one_block), (queries.reshape(block_count, block_rows, HEADS, HD), doc_ids.reshape(block_count, block_rows)))
    return result.reshape(length, HEADS * HD)

def layer(inputs, doc_ids, stamp, w_qkv, w_out, w_up, w_down, w_ada, b_ada):
    highest = lax.Precision.HIGHEST
    cond = low(time_features(stamp[None], w_ada.shape[0]))[0]
    mods = jnp.dot(cond, w_ada, precision=highest) + b_ada
    shift_a, scale_a, gate_a, shift_m, scale_m, gate_m = jnp.split(mods, 6)
    length = inputs.shape[0]
    normed_a = low(modulate(inputs, shift_a, scale_a))
    packed = jnp.dot(normed_a, w_qkv, precision=highest).reshape(length, HEADS, 3, HD)
    queries = low(rotate(low_back(packed[:, :, 0]), 1.0))
    key_heads = low(rotate(low_back(packed[:, :, 1]), 1.0))
    value_heads = low(low_back(packed[:, :, 2]))
    attended = low(low_back(attention(queries, key_heads, value_heads, doc_ids)))
    branch_a = low_back(jnp.dot(attended, w_out, precision=highest))
    middle = inputs + gate_a * branch_a
    normed_m = low(modulate(middle, shift_m, scale_m))
    pre_act = low_back(jnp.dot(normed_m, w_up, precision=highest))
    hidden = low(jax.nn.gelu(pre_act, approximate=True))
    branch_m = low_back(jnp.dot(hidden, w_down, precision=highest))
    return middle + gate_m * branch_m

def reference(tokens, segments, timesteps, cotangent, w_qkv, w_out, w_up, w_down, w_ada, b_ada):
    micro_count, total_rows, feat_width = tokens.shape
    seq_count = micro_count * N_DP
    length = total_rows // N_DP
    inputs = tokens.astype(jnp.float32).reshape(seq_count, length, feat_width)
    doc_ids = segments.reshape(seq_count, length)
    stamps = timesteps.reshape(seq_count)
    weights = (w_qkv.astype(jnp.float32), w_out.astype(jnp.float32), w_up.astype(jnp.float32), w_down.astype(jnp.float32), w_ada.astype(jnp.float32), b_ada.astype(jnp.float32))

    def forward(inputs, wq, wo, wu, wd, wa, ba):

        def one_seq(pieces):
            seq_in, seq_ids, seq_stamp = pieces
            return layer(seq_in, seq_ids, seq_stamp, wq, wo, wu, wd, wa, ba)
        return lax.map(jax.checkpoint(one_seq), (inputs, doc_ids, stamps))
    result, backward = jax.vjp(forward, inputs, *weights)
    grads = backward(cotangent.astype(jnp.float32).reshape(seq_count, length, feat_width))
    return (result.reshape(micro_count, total_rows, feat_width).astype(jnp.bfloat16), grads[0].reshape(micro_count, total_rows, feat_width), grads[1], grads[2], grads[3], grads[4], grads[5], grads[6])
```

```python
import functools
import math

import jax
import jax.numpy as jnp
from jax import lax
from jax.experimental import pallas as pl
from jax.experimental.pallas import tpu as pltpu
from jax.sharding import PartitionSpec as P

HEADS = 12
HD = 64
HALF = HD // 2
EPSILON = 1e-06
MASKED = -1e30
F32 = jnp.float32
BF16 = jnp.bfloat16
NN = (((1,), (0,)), ((), ()))
NT = (((1,), (1,)), ((), ()))
TN = (((0,), (0,)), ((), ()))
TT = (((0,), (1,)), ((), ()))


def dot(left, right, dims=NN):
    return lax.dot_general(left, right, dims, preferred_element_type=F32)


def pick(bit, zero, one):
    return jnp.where(bit == 0, zero, one)


def swap_far(value):
    return lax.ppermute(value, "tensor", [(i, i ^ 2) for i in range(4)])


def swap_near(value):
    return lax.ppermute(value, "tensor", [(i, i ^ 1) for i in range(4)])


def swap_dp(value, bit):
    count = lax.axis_size("dp")
    return lax.ppermute(value, "dp", [(i, i ^ (1 << bit)) for i in range(count)])


def dp_bits():
    return lax.axis_size("dp").bit_length() - 1


def my_bit(bit):
    return (lax.axis_index("dp") >> bit) & 1


def gather_blocks(shard, bits):
    current, done = shard, []
    for bit in bits:
        arrived = swap_dp(current, bit)
        place = sum(1 for other in done if other > bit)
        mine = my_bit(bit)
        current = jnp.stack(
            [pick(mine, current, arrived), pick(mine, arrived, current)], axis=place
        )
        done.append(bit)
    return current.reshape(-1, shard.shape[-1])


def scatter_blocks(total, bits):
    count = dp_bits()
    current = total.reshape((2,) * count + (-1, total.shape[-1]))
    left = list(range(count - 1, -1, -1))
    for bit in bits:
        place = left.index(bit)
        first = lax.index_in_dim(current, 0, place, keepdims=False)
        second = lax.index_in_dim(current, 1, place, keepdims=False)
        mine = my_bit(bit)
        arrived = swap_dp(pick(mine, second, first).astype(BF16), bit)
        current = pick(mine, first, second) + arrived.astype(F32)
        left.remove(bit)
    return current


def gather_relative(value):
    current = value
    for bit in range(dp_bits()):
        current = jnp.stack([current, swap_dp(current, bit)])
    return current.reshape((-1,) + value.shape)


def scatter_relative(terms):
    count = dp_bits()
    current = terms.reshape((2,) * count + terms.shape[1:])
    for bit in range(count):
        place = count - 1 - bit
        first = lax.index_in_dim(current, 0, place, keepdims=False)
        second = lax.index_in_dim(current, 1, place, keepdims=False)
        current = first + swap_dp(second, bit)
    return current


def attend_kernel(
    bq, bk, heads, lo_ref, hi_ref, pk_ref, cs_ref, sn_ref, row_ref, col_ref,
    qkv_ref, att_ref, lse_ref, key_s, acc_s,
):
    length = pk_ref.shape[1]
    cosine = cs_ref[...]
    sine = sn_ref[...]
    for h in range(heads):
        base = 3 * HD * h

        def turned(row):
            a = pk_ref[row : row + HALF, :]
            b = pk_ref[row + HALF : row + HD, :]
            return jnp.concatenate([a * cosine - b * sine, a * sine + b * cosine], axis=0)

        qkv_ref[base : base + HD, :] = turned(base).astype(BF16)
        keys = turned(base + HD)
        qkv_ref[base + HD : base + 2 * HD, :] = keys.astype(BF16)
        key_s[h] = keys.T.astype(BF16)
        qkv_ref[base + 2 * HD : base + 3 * HD, :] = pk_ref[
            base + 2 * HD : base + 3 * HD, :
        ].astype(BF16)

    def query_block(i, _):
        columns = pl.ds(pl.multiple_of(i * bq, bq), bq)
        queries = [
            qkv_ref[3 * HD * h : 3 * HD * h + HD, columns] * jnp.asarray(0.125, BF16)
            for h in range(heads)
        ]
        query_docs = row_ref[0:1, columns]
        acc_s[...] = jnp.zeros_like(acc_s)

        def key_block(j, carry):
            rows = pl.ds(pl.multiple_of(j * bk, bk), bk)
            key_docs = jnp.concatenate([col_ref[rows, :]] * (bq // 128), axis=1)
            allowed = key_docs == query_docs
            result = []
            for h in range(heads):
                top, total = carry[2 * h], carry[2 * h + 1]
                scores = dot(key_s[h, rows, :], queries[h])
                scores = jnp.where(allowed, scores, MASKED)
                new_top = jnp.maximum(top, jnp.max(scores, axis=0, keepdims=True))
                fade = jnp.exp(top - new_top)
                chances = jnp.exp(scores - new_top)
                total = fade * total + jnp.sum(chances, axis=0, keepdims=True)
                acc_s[h] = acc_s[h] * fade + dot(
                    qkv_ref[3 * HD * h + 2 * HD : 3 * HD * h + 3 * HD, rows],
                    chances.astype(BF16),
                )
                result += [new_top, total]
            return tuple(result)

        start = (jnp.full((1, bq), MASKED, F32), jnp.zeros((1, bq), F32)) * heads
        carry = lax.fori_loop(lo_ref[i], hi_ref[i], key_block, start)
        for h in range(heads):
            top, total = carry[2 * h], carry[2 * h + 1]
            att_ref[HD * h : HD * h + HD, columns] = (acc_s[h] / total).astype(BF16)
            lse_ref[h, 0:1, columns] = top + jnp.log(total)
        return 0

    lax.fori_loop(0, length // bq, query_block, 0)


def attend_back_kernel(
    bq, bk, heads, lo_ref, hi_ref, qkv_ref, att_ref, dat_ref, lse_ref, cs_ref, sn_ref,
    row_ref, col_ref, out_ref, q_s, k_s, v_s, g_s, dq_s, dk_s, dv_s, inner_s,
):
    length = qkv_ref.shape[1]
    for h in range(heads):
        base = 3 * HD * h
        own = slice(HD * h, HD * h + HD)
        q_s[h] = qkv_ref[base : base + HD, :].T
        k_s[h] = qkv_ref[base + HD : base + 2 * HD, :].T
        v_s[h] = qkv_ref[base + 2 * HD : base + 3 * HD, :].T
        g_s[h] = dat_ref[own, :].T
        inner_s[h, 0:1, :] = jnp.sum(
            att_ref[own, :].astype(F32) * dat_ref[own, :].astype(F32), axis=0, keepdims=True
        )
    dq_s[...] = jnp.zeros_like(dq_s)

    def key_block(j, _):
        rows = pl.ds(pl.multiple_of(j * bk, bk), bk)
        key_docs = jnp.concatenate([col_ref[rows, :]] * (bq // 128), axis=1)
        dk_s[:, rows, :] = jnp.zeros((heads, bk, HD), F32)
        dv_s[:, rows, :] = jnp.zeros((heads, bk, HD), F32)

        def query_block(i, _):
            columns = pl.ds(pl.multiple_of(i * bq, bq), bq)
            allowed = key_docs == row_ref[0:1, columns]
            for h in range(heads):
                base = 3 * HD * h
                own = slice(HD * h, HD * h + HD)
                scores = dot(
                    k_s[h, rows, :] * jnp.asarray(0.125, BF16), qkv_ref[base : base + HD, columns]
                )
                chances = jnp.where(
                    allowed, jnp.exp(scores - lse_ref[h, 0:1, columns]), 0.0
                )
                d_chances = dot(v_s[h, rows, :], dat_ref[own, columns])
                d_scores = (chances * (d_chances - inner_s[h, 0:1, columns])).astype(BF16)
                dv_s[h, rows, :] += dot(chances.astype(BF16), g_s[h, columns, :])
                dk_s[h, rows, :] += dot(d_scores, q_s[h, columns, :])
                dq_s[own, columns] += dot(qkv_ref[base + HD : base + 2 * HD, rows], d_scores)
            return 0

        lax.fori_loop(lo_ref[j], hi_ref[j], query_block, 0)
        return 0

    lax.fori_loop(0, length // bk, key_block, 0)
    cosine = cs_ref[...] * 0.125
    sine = sn_ref[...] * 0.125

    def turned_back(row, value):
        a = value[0:HALF, :]
        b = value[HALF:HD, :]
        out_ref[row : row + HALF, :] = (a * cosine + b * sine).astype(BF16)
        out_ref[row + HALF : row + HD, :] = (b * cosine - a * sine).astype(BF16)

    for h in range(heads):
        base = 3 * HD * h
        turned_back(base, dq_s[HD * h : HD * h + HD, :])
        turned_back(base + HD, dk_s[h].T)
        out_ref[base + 2 * HD : base + 3 * HD, :] = dv_s[h].T.astype(BF16)


def whole(*shape):
    return pl.BlockSpec(shape, lambda i, *_: (0,) * len(shape))


def attend(packed, tables, docs, bounds, heads, bq, bk):
    length = packed.shape[1]
    return pl.pallas_call(
        functools.partial(attend_kernel, bq, bk, heads),
        grid_spec=pltpu.PrefetchScalarGridSpec(
            num_scalar_prefetch=2,
            grid=(1,),
            in_specs=[
                whole(3 * HD * heads, length),
                whole(HALF, length),
                whole(HALF, length),
                whole(1, length),
                whole(length, 128),
            ],
            out_specs=[
                whole(3 * HD * heads, length),
                whole(HD * heads, length),
                whole(heads, 1, length),
            ],
            scratch_shapes=[
                pltpu.VMEM((heads, length, HD), BF16),
                pltpu.VMEM((heads, HD, bq), F32),
            ],
        ),
        out_shape=[
            jax.ShapeDtypeStruct((3 * HD * heads, length), BF16),
            jax.ShapeDtypeStruct((HD * heads, length), BF16),
            jax.ShapeDtypeStruct((heads, 1, length), F32),
        ],
        cost_estimate=pl.CostEstimate(
            flops=heads * length * length * 512,
            bytes_accessed=packed.size * 8,
            transcendentals=heads * length * length // 2,
        ),
        name="attend",
    )(*bounds, packed, *tables, *docs)


def attend_back(qkv, attended, d_attended, lse, tables, docs, bounds, heads, bq, bk):
    length = qkv.shape[1]
    return pl.pallas_call(
        functools.partial(attend_back_kernel, bq, bk, heads),
        grid_spec=pltpu.PrefetchScalarGridSpec(
            num_scalar_prefetch=2,
            grid=(1,),
            in_specs=[
                whole(3 * HD * heads, length),
                whole(HD * heads, length),
                whole(HD * heads, length),
                whole(heads, 1, length),
                whole(HALF, length),
                whole(HALF, length),
                whole(1, length),
                whole(length, 128),
            ],
            out_specs=whole(3 * HD * heads, length),
            scratch_shapes=[pltpu.VMEM((heads, length, HD), BF16)] * 4
            + [
                pltpu.VMEM((heads * HD, length), F32),
                pltpu.VMEM((heads, length, HD), F32),
                pltpu.VMEM((heads, length, HD), F32),
                pltpu.VMEM((heads, 8, length), F32),
            ],
        ),
        out_shape=jax.ShapeDtypeStruct((3 * HD * heads, length), BF16),
        cost_estimate=pl.CostEstimate(
            flops=heads * length * length * 900,
            bytes_accessed=qkv.size * 8,
            transcendentals=heads * length * length // 2,
        ),
        name="attend_back",
    )(*bounds, qkv, attended, d_attended, lse, *tables, *docs)


def block_range(doc_ids, rows, columns):
    by_row = doc_ids.reshape(-1, rows)
    by_column = doc_ids.reshape(-1, columns)
    low = jnp.sum(by_column[:, -1][None, :] < by_row[:, 0][:, None], axis=1, dtype=jnp.int32)
    high = jnp.sum(by_column[:, 0][None, :] <= by_row[:, -1][:, None], axis=1, dtype=jnp.int32)
    return low, high


def turn_tables(length):
    freqs = jnp.exp(-math.log(10000.0) * jnp.arange(HALF, dtype=F32) / HALF)
    angles = freqs[:, None] * jnp.arange(length, dtype=F32)[None, :]
    return jnp.cos(angles), jnp.sin(angles)


def normalize(values):
    center = values - jnp.mean(values, axis=-1, keepdims=True)
    root = lax.rsqrt(jnp.mean(center * center, axis=-1, keepdims=True) + EPSILON)
    return center * root, root


def normalize_back(grad, unit, root, stretch):
    turned = grad * (1.0 + stretch)
    return root * (
        turned
        - jnp.mean(turned, axis=-1, keepdims=True)
        - unit * jnp.mean(turned * unit, axis=-1, keepdims=True)
    )


def gelu_pair(values):
    return jax.vjp(lambda v: jax.nn.gelu(v, approximate=True), values)


def per_device(tokens, segments, timesteps, cotangent, w_qkv, w_out, w_up, w_down, w_ada, b_ada):
    micro_count, rows, width = tokens.shape
    heads = HEADS // 4
    length = 4 * rows
    count = dp_bits()
    tensor = lax.axis_index("tensor")
    far, near = tensor // 2, tensor % 2
    device = lax.axis_index("dp") * 4 + tensor
    falling = list(range(count - 1, -1, -1))
    rising = list(range(count))

    full_tokens = []
    for m in range(micro_count):
        own = tokens[m]
        across = swap_far(own)
        pair = jnp.stack([pick(far, own, across), pick(far, across, own)])
        other = swap_near(pair)
        full_tokens.append(
            jnp.stack([pick(near, pair, other), pick(near, other, pair)], axis=1).reshape(
                length, width
            )
        )

    feature_rows = w_ada.shape[0]
    half = feature_rows * lax.axis_size("dp") * 4 // 2
    stamps = gather_relative(timesteps[:, 0].astype(F32))
    index = device * feature_rows + jnp.arange(feature_rows)
    freqs = jnp.exp(-math.log(10000.0) * (index % half).astype(F32) / half)
    angles = stamps[:, :, None] * freqs
    cond = jnp.where(index < half, jnp.cos(angles), jnp.sin(angles)).astype(BF16)
    cond = cond.reshape(-1, feature_rows)
    bias_size = b_ada.shape[0]
    slots = w_ada.shape[1] // bias_size
    bias = jnp.where(
        jnp.arange(slots)[:, None] == device, b_ada.astype(F32)[None, :], 0.0
    ).reshape(-1)
    terms = dot(cond, w_ada) + bias
    mods = scatter_relative(terms.reshape(-1, micro_count, terms.shape[1]))
    mods = mods + swap_far(mods)
    mods = mods + swap_near(mods)

    wq = gather_blocks(w_qkv, falling)
    wo_own = gather_blocks(w_out.T, falling)
    wo_far = swap_far(wo_own)
    wu_own = gather_blocks(w_up, falling)
    wu_far = swap_far(wu_own)
    down = w_down.T
    wd_own = gather_blocks(down, rising)
    wd_far = swap_far(wd_own)

    tables = turn_tables(length)
    fq, fk = min(512, length), min(512, length)
    rq, rk = min(512, length), min(256, length)

    outputs = []
    state = []
    for m in range(micro_count):
        shift_a, scale_a, gate_a, shift_m, scale_m, gate_m = jnp.split(mods[m], 6)
        doc_ids = segments[m]
        docs = (doc_ids[None, :], jnp.broadcast_to(doc_ids[:, None], (length, 128)))
        unit_full, _ = normalize(full_tokens[m].astype(F32))
        normed_a = (unit_full * (1.0 + scale_a) + shift_a).astype(BF16)
        packed = dot(wq, normed_a, TT)
        qkv, attended, lse = attend(
            packed, tables, docs, block_range(doc_ids, fq, fk), heads, fq, fk
        )
        half_length = length // 2
        first, second = attended[:, :half_length], attended[:, half_length:]
        att_own = pick(far, first, second)
        att_far = swap_far(pick(far, second, first))
        state.append((qkv, attended, lse, docs, doc_ids, normed_a, att_own, att_far))

    grads_up, grads_down, grads_out = [], [], []
    middles = []
    for m in range(micro_count):
        shift_a, scale_a, gate_a, shift_m, scale_m, gate_m = jnp.split(mods[m], 6)
        qkv, attended, lse, docs, doc_ids, normed_a, att_own, att_far = state[m]
        inputs = tokens[m].astype(F32)
        grad_out = cotangent[m].astype(F32)
        grad_m = (grad_out * gate_m).astype(BF16)
        grad_m2 = jnp.concatenate([grad_m, swap_near(grad_m)])
        branch = dot(att_own, wo_own, TT) + dot(att_far, wo_far, TT)
        first, second = branch[:rows], branch[rows:]
        branch_a = pick(near, first, second) + swap_near(pick(near, second, first))
        middle = inputs + gate_a * branch_a
        unit_m, root_m = normalize(middle)
        normed_m = (unit_m * (1.0 + scale_m) + shift_m).astype(BF16)
        normed_m2 = jnp.concatenate([normed_m, swap_near(normed_m)])
        hidden_own, back_own = gelu_pair(dot(normed_m2, wu_own))
        hidden_far, back_far = gelu_pair(dot(normed_m2, wu_far))
        hidden_own, hidden_far = hidden_own.astype(BF16), hidden_far.astype(BF16)
        branch = dot(hidden_own, wd_own, NT) + dot(hidden_far, wd_far, NT)
        branch_m = branch[:rows] + swap_near(branch[rows:])
        outputs.append((middle + gate_m * branch_m).astype(BF16))
        d_gate_m = jnp.sum(grad_out * branch_m, axis=0)
        d_pre_own = back_own(dot(grad_m2, wd_own))[0].astype(BF16)
        d_pre_far = back_far(dot(grad_m2, wd_far))[0].astype(BF16)
        grads_down.append((dot(grad_m2, hidden_own, TN), dot(grad_m2, hidden_far, TN)))
        grads_up.append((dot(normed_m2, d_pre_own, TN), dot(normed_m2, d_pre_far, TN)))
        branch = dot(d_pre_own, wu_own, NT) + dot(d_pre_far, wu_far, NT)
        d_normed_m = branch[:rows] + swap_near(branch[rows:])
        d_shift_m = jnp.sum(d_normed_m, axis=0)
        d_scale_m = jnp.sum(d_normed_m * unit_m, axis=0)
        d_middle = grad_out + normalize_back(d_normed_m, unit_m, root_m, scale_m)
        d_gate_a = jnp.sum(d_middle * branch_a, axis=0)
        grad_a = (d_middle * gate_a).astype(BF16)
        other = swap_near(grad_a)
        grad_a2 = jnp.concatenate([pick(near, grad_a, other), pick(near, other, grad_a)])
        d_att_own = dot(wo_own, grad_a2, TT).astype(BF16)
        d_att_far = swap_far(dot(wo_far, grad_a2, TT).astype(BF16))
        grads_out.append((dot(grad_a2, att_own, TT), dot(grad_a2, att_far, TT)))
        d_attended = jnp.concatenate(
            [pick(far, d_att_own, d_att_far), pick(far, d_att_far, d_att_own)], axis=1
        )
        middles.append((d_middle, d_attended, d_gate_a, d_shift_m, d_scale_m, d_gate_m))

    def reduced(grads):
        own = sum(pair[0] for pair in grads)
        away = sum(pair[1] for pair in grads)
        return scatter_blocks(own + swap_far(away.astype(BF16)).astype(F32), rising)

    g_down = reduced(grads_down).T
    g_up = reduced(grads_up)
    g_out = reduced(grads_out).T

    input_grads = []
    mod_grads = []
    g_qkv = []
    for m in range(micro_count):
        shift_a, scale_a, gate_a, shift_m, scale_m, gate_m = jnp.split(mods[m], 6)
        qkv, attended, lse, docs, doc_ids, normed_a, _, _ = state[m]
        d_middle, d_attended, d_gate_a, d_shift_m, d_scale_m, d_gate_m = middles[m]
        d_packed = attend_back(
            qkv, attended, d_attended, lse, tables, docs, block_range(doc_ids, rk, rq), heads, rq, rk
        )
        g_qkv.append(dot(normed_a, d_packed, TT))
        part = dot(d_packed, wq, TT).reshape(2, 2, rows, width)
        part = pick(near, part[:, 0], part[:, 1]) + swap_near(pick(near, part[:, 1], part[:, 0]))
        d_normed_a = pick(far, part[0], part[1]) + swap_far(
            pick(far, part[1], part[0]).astype(BF16)
        ).astype(F32)
        unit, root = normalize(tokens[m].astype(F32))
        d_shift_a = jnp.sum(d_normed_a, axis=0)
        d_scale_a = jnp.sum(d_normed_a * unit, axis=0)
        input_grads.append(d_middle + normalize_back(d_normed_a, unit, root, scale_a))
        mod_grads.append(
            jnp.concatenate([d_shift_a, d_scale_a, d_gate_a, d_shift_m, d_scale_m, d_gate_m])
        )
    g_qkv = scatter_blocks(sum(g_qkv), rising)

    d_mods = jnp.stack(mod_grads)
    d_mods = d_mods + swap_far(d_mods)
    d_mods = d_mods + swap_near(d_mods)
    all_mods = gather_relative(d_mods).reshape(-1, d_mods.shape[1])
    g_ada = lax.dot_general(
        cond.astype(F32),
        all_mods,
        TN,
        precision=lax.Precision.HIGHEST,
        preferred_element_type=F32,
    )
    g_bias = lax.dynamic_slice_in_dim(jnp.sum(all_mods, axis=0), device * bias_size, bias_size)
    return (
        jnp.stack(outputs),
        jnp.stack(input_grads),
        g_qkv,
        g_out,
        g_up,
        g_down,
        g_ada,
        g_bias,
    )


def solution(mesh):
    return jax.shard_map(
        per_device,
        mesh=mesh,
        in_specs=(
            P(None, ("dp", "tensor"), None),
            P(None, "dp"),
            P(None, "dp"),
            P(None, ("dp", "tensor"), None),
            P("dp", "tensor"),
            P("tensor", "dp"),
            P("dp", "tensor"),
            P("tensor", "dp"),
            P(("dp", "tensor"), None),
            P(("dp", "tensor")),
        ),
        out_specs=(
            P(None, ("dp", "tensor"), None),
            P(None, ("dp", "tensor"), None),
            P("dp", "tensor"),
            P("tensor", "dp"),
            P("dp", "tensor"),
            P("tensor", "dp"),
            P(("dp", "tensor"), None),
            P(("dp", "tensor")),
        ),
        check_vma=False,
    )
```

```python
import functools
import math

import jax
import jax.numpy as jnp
from jax import lax
from jax.experimental import pallas as pl
from jax.experimental.pallas import tpu as pltpu
from jax.sharding import PartitionSpec as P

HEADS = 12
HD = 64
HALF = HD // 2
EPSILON = 1e-06
MASKED = -1e30
F32 = jnp.float32
BF16 = jnp.bfloat16
NN = (((1,), (0,)), ((), ()))
NT = (((1,), (1,)), ((), ()))
TN = (((0,), (0,)), ((), ()))
TT = (((0,), (1,)), ((), ()))


def dot(left, right, dims=NN):
    return lax.dot_general(left, right, dims, preferred_element_type=F32)


def pick(bit, zero, one):
    return jnp.where(bit == 0, zero, one)


def swap_far(value):
    return lax.ppermute(value, "tensor", [(i, i ^ 2) for i in range(4)])


def swap_near(value):
    return lax.ppermute(value, "tensor", [(i, i ^ 1) for i in range(4)])


def swap_dp(value, bit):
    count = lax.axis_size("dp")
    return lax.ppermute(value, "dp", [(i, i ^ (1 << bit)) for i in range(count)])


def dp_bits():
    return lax.axis_size("dp").bit_length() - 1


def my_bit(bit):
    return (lax.axis_index("dp") >> bit) & 1


def gather_blocks(shard, bits):
    current, done = shard, []
    for bit in bits:
        arrived = swap_dp(current, bit)
        place = sum(1 for other in done if other > bit)
        mine = my_bit(bit)
        current = jnp.stack(
            [pick(mine, current, arrived), pick(mine, arrived, current)], axis=place
        )
        done.append(bit)
    return current.reshape(-1, shard.shape[-1])


def scatter_blocks(total, bits):
    count = dp_bits()
    current = total.reshape((2,) * count + (-1, total.shape[-1]))
    left = list(range(count - 1, -1, -1))
    for bit in bits:
        place = left.index(bit)
        first = lax.index_in_dim(current, 0, place, keepdims=False)
        second = lax.index_in_dim(current, 1, place, keepdims=False)
        mine = my_bit(bit)
        arrived = swap_dp(pick(mine, second, first).astype(BF16), bit)
        current = pick(mine, first, second) + arrived.astype(F32)
        left.remove(bit)
    return current


def gather_relative(value):
    current = value
    for bit in range(dp_bits()):
        current = jnp.stack([current, swap_dp(current, bit)])
    return current.reshape((-1,) + value.shape)


def scatter_relative(terms):
    count = dp_bits()
    current = terms.reshape((2,) * count + terms.shape[1:])
    for bit in range(count):
        place = count - 1 - bit
        first = lax.index_in_dim(current, 0, place, keepdims=False)
        second = lax.index_in_dim(current, 1, place, keepdims=False)
        current = first + swap_dp(second, bit)
    return current


def attend_kernel(
    bq, bk, heads, lo_ref, hi_ref, pk_ref, cs_ref, sn_ref, row_ref, col_ref,
    qkv_ref, att_ref, lse_ref, key_s, acc_s,
):
    length = pk_ref.shape[1]
    cosine = cs_ref[...]
    sine = sn_ref[...]
    for h in range(heads):
        base = 3 * HD * h

        def turned(row):
            a = pk_ref[row : row + HALF, :]
            b = pk_ref[row + HALF : row + HD, :]
            return jnp.concatenate([a * cosine - b * sine, a * sine + b * cosine], axis=0)

        qkv_ref[base : base + HD, :] = turned(base).astype(BF16)
        keys = turned(base + HD)
        qkv_ref[base + HD : base + 2 * HD, :] = keys.astype(BF16)
        key_s[h] = keys.T.astype(BF16)
        qkv_ref[base + 2 * HD : base + 3 * HD, :] = pk_ref[
            base + 2 * HD : base + 3 * HD, :
        ].astype(BF16)

    def query_block(i, _):
        columns = pl.ds(pl.multiple_of(i * bq, bq), bq)
        queries = [
            qkv_ref[3 * HD * h : 3 * HD * h + HD, columns] * jnp.asarray(0.125, BF16)
            for h in range(heads)
        ]
        query_docs = row_ref[0:1, columns]
        acc_s[...] = jnp.zeros_like(acc_s)

        def key_block(j, carry):
            rows = pl.ds(pl.multiple_of(j * bk, bk), bk)
            key_docs = jnp.concatenate([col_ref[rows, :]] * (bq // 128), axis=1)
            allowed = key_docs == query_docs
            result = []
            for h in range(heads):
                top, total = carry[2 * h], carry[2 * h + 1]
                scores = dot(key_s[h, rows, :], queries[h])
                scores = jnp.where(allowed, scores, MASKED)
                new_top = jnp.maximum(top, jnp.max(scores, axis=0, keepdims=True))
                fade = jnp.exp(top - new_top)
                chances = jnp.exp(scores - new_top)
                total = fade * total + jnp.sum(chances, axis=0, keepdims=True)
                acc_s[h] = acc_s[h] * fade + dot(
                    qkv_ref[3 * HD * h + 2 * HD : 3 * HD * h + 3 * HD, rows],
                    chances.astype(BF16),
                )
                result += [new_top, total]
            return tuple(result)

        start = (jnp.full((1, bq), MASKED, F32), jnp.zeros((1, bq), F32)) * heads
        carry = lax.fori_loop(lo_ref[i], hi_ref[i], key_block, start)
        for h in range(heads):
            top, total = carry[2 * h], carry[2 * h + 1]
            att_ref[HD * h : HD * h + HD, columns] = (acc_s[h] / total).astype(BF16)
            lse_ref[h, 0:1, columns] = top + jnp.log(total)
        return 0

    lax.fori_loop(0, length // bq, query_block, 0)


def attend_back_kernel(
    bq, bk, heads, lo_ref, hi_ref, qkv_ref, att_ref, dat_ref, lse_ref, cs_ref, sn_ref,
    row_ref, col_ref, out_ref, q_s, k_s, v_s, g_s, dq_s, dk_s, dv_s, inner_s,
):
    length = qkv_ref.shape[1]
    for h in range(heads):
        base = 3 * HD * h
        own = slice(HD * h, HD * h + HD)
        q_s[h] = qkv_ref[base : base + HD, :].T
        k_s[h] = qkv_ref[base + HD : base + 2 * HD, :].T
        v_s[h] = qkv_ref[base + 2 * HD : base + 3 * HD, :].T
        g_s[h] = dat_ref[own, :].T
        inner_s[h, 0:1, :] = jnp.sum(
            att_ref[own, :].astype(F32) * dat_ref[own, :].astype(F32), axis=0, keepdims=True
        )
    dq_s[...] = jnp.zeros_like(dq_s)

    def key_block(j, _):
        rows = pl.ds(pl.multiple_of(j * bk, bk), bk)
        key_docs = jnp.concatenate([col_ref[rows, :]] * (bq // 128), axis=1)
        dk_s[:, rows, :] = jnp.zeros((heads, bk, HD), F32)
        dv_s[:, rows, :] = jnp.zeros((heads, bk, HD), F32)

        def query_block(i, _):
            columns = pl.ds(pl.multiple_of(i * bq, bq), bq)
            allowed = key_docs == row_ref[0:1, columns]
            for h in range(heads):
                base = 3 * HD * h
                own = slice(HD * h, HD * h + HD)
                scores = dot(
                    k_s[h, rows, :] * jnp.asarray(0.125, BF16), qkv_ref[base : base + HD, columns]
                )
                chances = jnp.where(
                    allowed, jnp.exp(scores - lse_ref[h, 0:1, columns]), 0.0
                )
                d_chances = dot(v_s[h, rows, :], dat_ref[own, columns])
                d_scores = (chances * (d_chances - inner_s[h, 0:1, columns])).astype(BF16)
                dv_s[h, rows, :] += dot(chances.astype(BF16), g_s[h, columns, :])
                dk_s[h, rows, :] += dot(d_scores, q_s[h, columns, :])
                dq_s[own, columns] += dot(qkv_ref[base + HD : base + 2 * HD, rows], d_scores)
            return 0

        lax.fori_loop(lo_ref[j], hi_ref[j], query_block, 0)
        return 0

    lax.fori_loop(0, length // bk, key_block, 0)
    cosine = cs_ref[...] * 0.125
    sine = sn_ref[...] * 0.125

    def turned_back(row, value):
        a = value[0:HALF, :]
        b = value[HALF:HD, :]
        out_ref[row : row + HALF, :] = (a * cosine + b * sine).astype(BF16)
        out_ref[row + HALF : row + HD, :] = (b * cosine - a * sine).astype(BF16)

    for h in range(heads):
        base = 3 * HD * h
        turned_back(base, dq_s[HD * h : HD * h + HD, :])
        turned_back(base + HD, dk_s[h].T)
        out_ref[base + 2 * HD : base + 3 * HD, :] = dv_s[h].T.astype(BF16)


def whole(*shape):
    return pl.BlockSpec(shape, lambda i, *_: (0,) * len(shape))


def attend(packed, tables, docs, bounds, heads, bq, bk):
    length = packed.shape[1]
    return pl.pallas_call(
        functools.partial(attend_kernel, bq, bk, heads),
        grid_spec=pltpu.PrefetchScalarGridSpec(
            num_scalar_prefetch=2,
            grid=(1,),
            in_specs=[
                whole(3 * HD * heads, length),
                whole(HALF, length),
                whole(HALF, length),
                whole(1, length),
                whole(length, 128),
            ],
            out_specs=[
                whole(3 * HD * heads, length),
                whole(HD * heads, length),
                whole(heads, 1, length),
            ],
            scratch_shapes=[
                pltpu.VMEM((heads, length, HD), BF16),
                pltpu.VMEM((heads, HD, bq), F32),
            ],
        ),
        out_shape=[
            jax.ShapeDtypeStruct((3 * HD * heads, length), BF16),
            jax.ShapeDtypeStruct((HD * heads, length), BF16),
            jax.ShapeDtypeStruct((heads, 1, length), F32),
        ],
        cost_estimate=pl.CostEstimate(
            flops=heads * length * length * 512,
            bytes_accessed=packed.size * 8,
            transcendentals=heads * length * length // 2,
        ),
        name="attend",
    )(*bounds, packed, *tables, *docs)


def attend_back(qkv, attended, d_attended, lse, tables, docs, bounds, heads, bq, bk):
    length = qkv.shape[1]
    return pl.pallas_call(
        functools.partial(attend_back_kernel, bq, bk, heads),
        grid_spec=pltpu.PrefetchScalarGridSpec(
            num_scalar_prefetch=2,
            grid=(1,),
            in_specs=[
                whole(3 * HD * heads, length),
                whole(HD * heads, length),
                whole(HD * heads, length),
                whole(heads, 1, length),
                whole(HALF, length),
                whole(HALF, length),
                whole(1, length),
                whole(length, 128),
            ],
            out_specs=whole(3 * HD * heads, length),
            scratch_shapes=[pltpu.VMEM((heads, length, HD), BF16)] * 4
            + [
                pltpu.VMEM((heads * HD, length), F32),
                pltpu.VMEM((heads, length, HD), F32),
                pltpu.VMEM((heads, length, HD), F32),
                pltpu.VMEM((heads, 8, length), F32),
            ],
        ),
        out_shape=jax.ShapeDtypeStruct((3 * HD * heads, length), BF16),
        cost_estimate=pl.CostEstimate(
            flops=heads * length * length * 900,
            bytes_accessed=qkv.size * 8,
            transcendentals=heads * length * length // 2,
        ),
        name="attend_back",
    )(*bounds, qkv, attended, d_attended, lse, *tables, *docs)


def block_range(doc_ids, rows, columns):
    by_row = doc_ids.reshape(-1, rows)
    by_column = doc_ids.reshape(-1, columns)
    low = jnp.sum(by_column[:, -1][None, :] < by_row[:, 0][:, None], axis=1, dtype=jnp.int32)
    high = jnp.sum(by_column[:, 0][None, :] <= by_row[:, -1][:, None], axis=1, dtype=jnp.int32)
    return low, high


def turn_tables(length):
    freqs = jnp.exp(-math.log(10000.0) * jnp.arange(HALF, dtype=F32) / HALF)
    angles = freqs[:, None] * jnp.arange(length, dtype=F32)[None, :]
    return jnp.cos(angles), jnp.sin(angles)


def normalize(values):
    center = values - jnp.mean(values, axis=-1, keepdims=True)
    root = lax.rsqrt(jnp.mean(center * center, axis=-1, keepdims=True) + EPSILON)
    return center * root, root


def normalize_back(grad, unit, root, stretch):
    turned = grad * (1.0 + stretch)
    return root * (
        turned
        - jnp.mean(turned, axis=-1, keepdims=True)
        - unit * jnp.mean(turned * unit, axis=-1, keepdims=True)
    )


def gelu_pair(values):
    square = values * values
    bend = jnp.tanh(0.7978845608028654 * (values + 0.044715 * (square * values)))
    slope = 0.7978845608028654 * (1.0 + 3 * 0.044715 * square)
    hidden = 0.5 * values * (1.0 + bend)
    return hidden, 0.5 * (1.0 + bend) + 0.5 * values * (1.0 - bend * bend) * slope


def per_device(tokens, segments, timesteps, cotangent, w_qkv, w_out, w_up, w_down, w_ada, b_ada):
    micro_count, rows, width = tokens.shape
    heads = HEADS // 4
    length = 4 * rows
    count = dp_bits()
    tensor = lax.axis_index("tensor")
    far, near = tensor // 2, tensor % 2
    device = lax.axis_index("dp") * 4 + tensor
    falling = list(range(count - 1, -1, -1))
    rising = list(range(count))

    full_tokens = []
    for m in range(micro_count):
        own = tokens[m]
        across = swap_far(own)
        pair = jnp.stack([pick(far, own, across), pick(far, across, own)])
        other = swap_near(pair)
        full_tokens.append(
            jnp.stack([pick(near, pair, other), pick(near, other, pair)], axis=1).reshape(
                length, width
            )
        )

    feature_rows = w_ada.shape[0]
    half = feature_rows * lax.axis_size("dp") * 4 // 2
    stamps = gather_relative(timesteps[:, 0].astype(F32))
    index = device * feature_rows + jnp.arange(feature_rows)
    freqs = jnp.exp(-math.log(10000.0) * (index % half).astype(F32) / half)
    angles = stamps[:, :, None] * freqs
    cond = jnp.where(index < half, jnp.cos(angles), jnp.sin(angles)).astype(BF16)
    cond = cond.reshape(-1, feature_rows)
    bias_size = b_ada.shape[0]
    slots = w_ada.shape[1] // bias_size
    bias = jnp.where(
        jnp.arange(slots)[:, None] == device, b_ada.astype(F32)[None, :], 0.0
    ).reshape(-1)
    terms = dot(cond, w_ada) + bias
    mods = scatter_relative(terms.reshape(-1, micro_count, terms.shape[1]))
    mods = mods + swap_far(mods)
    mods = mods + swap_near(mods)

    wq = gather_blocks(w_qkv, falling)
    pack = jnp.concatenate([w_up, w_down.T, w_out.T], axis=1)
    groups = [
        [4 * i + 2 * j + c for i in range(lax.axis_size("dp")) for j in range(2)] for c in range(2)
    ]
    pack = lax.all_gather(pack, ("dp", "tensor"), axis_index_groups=groups)
    pack = pack.reshape((-1, 2) + pack.shape[1:])
    hid = w_up.shape[1]
    part = w_out.shape[0]

    def both(start, size):
        piece = pack[..., start : start + size]
        return piece.transpose(0, 2, 1, 3).reshape(width, 2 * size)

    wu = both(0, hid)
    wd = both(hid, hid)
    wo = both(2 * hid, part)

    tables = turn_tables(length)
    fq, fk = min(512, length), min(512, length)
    rq, rk = min(512, length), min(256, length)

    outputs = []
    state = []
    for m in range(micro_count):
        shift_a, scale_a, gate_a, shift_m, scale_m, gate_m = jnp.split(mods[m], 6)
        doc_ids = segments[m]
        docs = (doc_ids[None, :], jnp.broadcast_to(doc_ids[:, None], (length, 128)))
        unit_full, _ = normalize(full_tokens[m].astype(F32))
        normed_a = (unit_full * (1.0 + scale_a) + shift_a).astype(BF16)
        packed = dot(wq, normed_a, TT)
        qkv, attended, lse = attend(
            packed, tables, docs, block_range(doc_ids, fq, fk), heads, fq, fk
        )
        half_length = length // 2
        first, second = attended[:, :half_length], attended[:, half_length:]
        att_own = pick(far, first, second)
        att_far = swap_far(pick(far, second, first))
        att = jnp.concatenate([pick(far, att_own, att_far), pick(far, att_far, att_own)])
        state.append((qkv, attended, lse, docs, doc_ids, normed_a, att))

    grads_up, grads_down, grads_out = [], [], []
    middles = []
    for m in range(micro_count):
        shift_a, scale_a, gate_a, shift_m, scale_m, gate_m = jnp.split(mods[m], 6)
        qkv, attended, lse, docs, doc_ids, normed_a, att = state[m]
        inputs = tokens[m].astype(F32)
        grad_out = cotangent[m].astype(F32)
        grad_m = (grad_out * gate_m).astype(BF16)
        grad_m2 = jnp.concatenate([grad_m, swap_near(grad_m)])
        branch = dot(att, wo, TT)
        first, second = branch[:rows], branch[rows:]
        branch_a = pick(near, first, second) + swap_near(pick(near, second, first))
        middle = inputs + gate_a * branch_a
        unit_m, root_m = normalize(middle)
        normed_m = (unit_m * (1.0 + scale_m) + shift_m).astype(BF16)
        normed_m2 = jnp.concatenate([normed_m, swap_near(normed_m)])
        hidden, slope = gelu_pair(dot(normed_m2, wu))
        hidden = hidden.astype(BF16)
        branch = dot(hidden, wd, NT)
        branch_m = branch[:rows] + swap_near(branch[rows:])
        outputs.append((middle + gate_m * branch_m).astype(BF16))
        d_gate_m = jnp.sum(grad_out * branch_m, axis=0)
        d_pre = (dot(grad_m2, wd) * slope).astype(BF16)
        grads_down.append(dot(grad_m2, hidden, TN))
        grads_up.append(dot(normed_m2, d_pre, TN))
        branch = dot(d_pre, wu, NT)
        d_normed_m = branch[:rows] + swap_near(branch[rows:])
        d_shift_m = jnp.sum(d_normed_m, axis=0)
        d_scale_m = jnp.sum(d_normed_m * unit_m, axis=0)
        d_middle = grad_out + normalize_back(d_normed_m, unit_m, root_m, scale_m)
        d_gate_a = jnp.sum(d_middle * branch_a, axis=0)
        grad_a = (d_middle * gate_a).astype(BF16)
        other = swap_near(grad_a)
        grad_a2 = jnp.concatenate([pick(near, grad_a, other), pick(near, other, grad_a)])
        d_att = dot(wo, grad_a2, TT).astype(BF16)
        grads_out.append(dot(grad_a2, att, TT))
        first, second = d_att[: d_att.shape[0] // 2], d_att[d_att.shape[0] // 2 :]
        d_att_own = pick(far, first, second)
        d_att_far = swap_far(pick(far, second, first))
        d_attended = jnp.concatenate(
            [pick(far, d_att_own, d_att_far), pick(far, d_att_far, d_att_own)], axis=1
        )
        middles.append((d_middle, d_attended, d_gate_a, d_shift_m, d_scale_m, d_gate_m))

    total = jnp.concatenate([sum(grads_up), sum(grads_down), sum(grads_out)], axis=1)
    total = lax.psum_scatter(total.astype(BF16), "dp", scatter_dimension=0, tiled=True)
    sides = [
        jnp.split(total[:, start : start + 2 * size], 2, axis=1)
        for start, size in ((0, hid), (2 * hid, hid), (4 * hid, part))
    ]
    mine = jnp.concatenate([pick(far, first, second) for first, second in sides], axis=1)
    away = jnp.concatenate([pick(far, second, first) for first, second in sides], axis=1)
    total = mine.astype(F32) + swap_far(away).astype(F32)
    g_up = total[:, :hid]
    g_down = total[:, hid : 2 * hid].T
    g_out = total[:, 2 * hid :].T

    input_grads = []
    mod_grads = []
    g_qkv = []
    for m in range(micro_count):
        shift_a, scale_a, gate_a, shift_m, scale_m, gate_m = jnp.split(mods[m], 6)
        qkv, attended, lse, docs, doc_ids, normed_a, _ = state[m]
        d_middle, d_attended, d_gate_a, d_shift_m, d_scale_m, d_gate_m = middles[m]
        d_packed = attend_back(
            qkv, attended, d_attended, lse, tables, docs, block_range(doc_ids, rk, rq), heads, rq, rk
        )
        g_qkv.append(dot(normed_a, d_packed, TT))
        partial = dot(d_packed, wq, TT)
        halves = partial.reshape(2, 2, rows, width)
        halves = pick(near, halves[:, 0], halves[:, 1]) + swap_near(
            pick(near, halves[:, 1], halves[:, 0])
        )
        d_normed_a = pick(far, halves[0], halves[1]) + swap_far(
            pick(far, halves[1], halves[0]).astype(BF16)
        ).astype(F32)
        unit, root = normalize(tokens[m].astype(F32))
        if m + 1 < micro_count:
            d_shift_a = jnp.sum(d_normed_a, axis=0)
            d_scale_a = jnp.sum(d_normed_a * unit, axis=0)
        else:
            unit_full, _ = normalize(full_tokens[m].astype(F32))
            d_shift_a = jnp.sum(partial, axis=0)
            d_scale_a = jnp.sum(partial * unit_full, axis=0)
        input_grads.append(d_middle + normalize_back(d_normed_a, unit, root, scale_a))
        mod_grads.append(
            jnp.concatenate([d_shift_a, d_scale_a, d_gate_a, d_shift_m, d_scale_m, d_gate_m])
        )
    g_qkv = scatter_blocks(sum(g_qkv), rising)

    d_mods = jnp.stack(mod_grads)
    d_mods = d_mods + swap_far(d_mods)
    d_mods = d_mods + swap_near(d_mods)
    all_mods = gather_relative(d_mods).reshape(-1, d_mods.shape[1])
    g_ada = lax.dot_general(
        cond.astype(F32),
        all_mods,
        TN,
        precision=lax.Precision.HIGHEST,
        preferred_element_type=F32,
    )
    g_bias = lax.dynamic_slice_in_dim(jnp.sum(all_mods, axis=0), device * bias_size, bias_size)
    return (
        jnp.stack(outputs),
        jnp.stack(input_grads),
        g_qkv,
        g_out,
        g_up,
        g_down,
        g_ada,
        g_bias,
    )


def solution(mesh):
    return jax.shard_map(
        per_device,
        mesh=mesh,
        in_specs=(
            P(None, ("dp", "tensor"), None),
            P(None, "dp"),
            P(None, "dp"),
            P(None, ("dp", "tensor"), None),
            P("dp", "tensor"),
            P("tensor", "dp"),
            P("dp", "tensor"),
            P("tensor", "dp"),
            P(("dp", "tensor"), None),
            P(("dp", "tensor")),
        ),
        out_specs=(
            P(None, ("dp", "tensor"), None),
            P(None, ("dp", "tensor"), None),
            P("dp", "tensor"),
            P("tensor", "dp"),
            P("dp", "tensor"),
            P("tensor", "dp"),
            P(("dp", "tensor"), None),
            P(("dp", "tensor")),
        ),
        check_vma=False,
    )
```

```python
import functools
import math

import jax
import jax.numpy as jnp
from jax import lax
from jax.experimental import pallas as pl
from jax.experimental.pallas import tpu as pltpu
from jax.sharding import PartitionSpec as P

HEADS = 12
HD = 64
HALF = HD // 2
EPSILON = 1e-06
MASKED = -1e30
F32 = jnp.float32
BF16 = jnp.bfloat16
NN = (((1,), (0,)), ((), ()))
NT = (((1,), (1,)), ((), ()))
TN = (((0,), (0,)), ((), ()))
TT = (((0,), (1,)), ((), ()))


def dot(left, right, dims=NN):
    return lax.dot_general(left, right, dims, preferred_element_type=F32)


def pick(bit, zero, one):
    return jnp.where(bit == 0, zero, one)


def swap_far(value):
    return lax.ppermute(value, "tensor", [(i, i ^ 2) for i in range(4)])


def swap_near(value):
    return lax.ppermute(value, "tensor", [(i, i ^ 1) for i in range(4)])


def swap_dp(value, bit):
    count = lax.axis_size("dp")
    return lax.ppermute(value, "dp", [(i, i ^ (1 << bit)) for i in range(count)])


def after(value, other):
    return lax.optimization_barrier((value, other))[0]


def dp_bits():
    return lax.axis_size("dp").bit_length() - 1


def my_bit(bit):
    return (lax.axis_index("dp") >> bit) & 1


def gather_blocks(shard, bits):
    current, done = shard, []
    for bit in bits:
        arrived = swap_dp(current, bit)
        place = sum(1 for other in done if other > bit)
        mine = my_bit(bit)
        current = jnp.stack(
            [pick(mine, current, arrived), pick(mine, arrived, current)], axis=place
        )
        done.append(bit)
        yield current


def scatter_blocks(total, bits, ready=lambda value, bit: value):
    count = dp_bits()
    current = total.reshape((2,) * count + (-1, total.shape[-1]))
    left = list(range(count - 1, -1, -1))
    for bit in bits:
        current = ready(current, bit)
        place = left.index(bit)
        first = lax.index_in_dim(current, 0, place, keepdims=False)
        second = lax.index_in_dim(current, 1, place, keepdims=False)
        mine = my_bit(bit)
        arrived = swap_dp(pick(mine, second, first).astype(BF16), bit)
        current = pick(mine, first, second) + arrived.astype(F32)
        left.remove(bit)
    return current


def gather_relative(value, first=lambda value, bit: value):
    current = value
    for bit in range(dp_bits()):
        current = first(current, bit)
        current = jnp.stack([current, swap_dp(current, bit)])
    return current.reshape((-1,) + value.shape)


def scatter_relative(terms, first=lambda value, bit: value):
    count = dp_bits()
    current = terms.reshape((2,) * count + terms.shape[1:])
    for bit in range(count):
        current = first(current, bit)
        place = count - 1 - bit
        kept = lax.index_in_dim(current, 0, place, keepdims=False)
        sent = lax.index_in_dim(current, 1, place, keepdims=False)
        current = kept + swap_dp(sent, bit)
    return current


def document_columns(row_ref, col_s):
    for start in range(0, row_ref.shape[1], 128):
        tile = jnp.broadcast_to(row_ref[0:1, start : start + 128], (128, 128))
        col_s[start : start + 128, :] = tile.T


def token_copies(refs, place, tok_s, sems):
    rows = tok_s.shape[0] // 4
    return [
        pltpu.make_async_copy(
            ref,
            tok_s.at[pl.ds(pl.multiple_of(jnp.bitwise_xor(place, r) * rows, rows), rows), :],
            sems.at[r],
        )
        for r, ref in enumerate(refs)
    ]


def same_documents(row_ref, col_s, rows, columns, size):
    return jnp.concatenate([col_s[rows, :]] * (size // 128), axis=1) == row_ref[0:1, columns]


def attend_kernel(
    m, bq, bk, heads, lo_ref, hi_ref, place_ref, t0, t1, t2, t3, mods_ref, wq_ref, cs_ref, sn_ref,
    row_ref, normed_hbm, qkv_ref, own_ref, far_ref, lse_ref,
    tok_s, normed_s, wq_s, key_s, acc_s, att_s, col_s, sem, token_sems,
):
    length, width = tok_s.shape
    rows = length // 4
    place = place_ref[0]
    copies = token_copies((t0, t1, t2, t3), place, tok_s, token_sems)
    for copy in copies:
        copy.start()
    wq_s[...] = wq_ref[...].T
    document_columns(row_ref, col_s)
    for copy in copies:
        copy.wait()
    shift = mods_ref[m : m + 1, 0:width]
    stretch = 1.0 + mods_ref[m : m + 1, width : 2 * width]
    step = min(256, rows)

    def project(i, _):
        piece = pl.ds(pl.multiple_of(i * step, step), step)
        unit, _ = normalize(tok_s[piece, :].astype(F32))
        normed = (unit * stretch + shift).astype(BF16)
        normed_s[piece, :] = normed
        packed = dot(wq_s[...], normed, NT)
        cosine = cs_ref[:, piece]
        sine = sn_ref[:, piece]
        for h in range(heads):
            base = 3 * HD * h

            def turned(row):
                a = packed[row : row + HALF]
                b = packed[row + HALF : row + HD]
                return jnp.concatenate([a * cosine - b * sine, a * sine + b * cosine], axis=0)

            qkv_ref[base : base + HD, piece] = turned(base).astype(BF16)
            keys = turned(base + HD)
            qkv_ref[base + HD : base + 2 * HD, piece] = keys.astype(BF16)
            key_s[h, piece, :] = keys.T.astype(BF16)
            qkv_ref[base + 2 * HD : base + 3 * HD, piece] = packed[
                base + 2 * HD : base + 3 * HD
            ].astype(BF16)
        return 0

    lax.fori_loop(0, length // step, project, 0)
    copy = pltpu.make_async_copy(normed_s, normed_hbm, sem)
    copy.start()

    def query_block(i, _):
        columns = pl.ds(pl.multiple_of(i * bq, bq), bq)
        queries = [
            qkv_ref[3 * HD * h : 3 * HD * h + HD, columns] * jnp.asarray(0.125, BF16)
            for h in range(heads)
        ]
        acc_s[...] = jnp.zeros_like(acc_s)

        def key_block(j, carry):
            keys = pl.ds(pl.multiple_of(j * bk, bk), bk)
            allowed = same_documents(row_ref, col_s, keys, columns, bq)
            scores = [dot(key_s[h, keys, :], queries[h]) for h in range(heads)]
            result, fades, lows = [], [], []
            for h in range(heads):
                top, total = carry[2 * h], carry[2 * h + 1]
                masked = jnp.where(allowed, scores[h], MASKED)
                new_top = jnp.maximum(top, jnp.max(masked, axis=0, keepdims=True))
                fade = jnp.exp(top - new_top)
                chances = jnp.exp(masked - new_top)
                total = fade * total + jnp.sum(chances, axis=0, keepdims=True)
                lows.append(chances.astype(BF16))
                fades.append(fade)
                result += [new_top, total]
            for h in range(heads):
                values = qkv_ref[3 * HD * h + 2 * HD : 3 * HD * h + 3 * HD, keys]
                acc_s[h] = acc_s[h] * fades[h] + dot(values, lows[h])
            return tuple(result)

        start = (jnp.full((1, bq), MASKED, F32), jnp.zeros((1, bq), F32)) * heads
        carry = lax.fori_loop(lo_ref[i], hi_ref[i], key_block, start)
        for h in range(heads):
            top, total = carry[2 * h], carry[2 * h + 1]
            att_s[HD * h : HD * h + HD, columns] = (acc_s[h] / total).astype(BF16)
            lse_ref[h, 0:1, columns] = top + jnp.log(total)
        return 0

    lax.fori_loop(0, length // bq, query_block, 0)
    half = length // 2
    mine = pl.multiple_of(place // 2 * half, half)
    away = pl.multiple_of(half - mine, half)
    own_ref[...] = att_s[:, pl.ds(mine, half)]
    far_ref[...] = att_s[:, pl.ds(away, half)]
    copy.wait()


def attend_back_kernel(
    bq, bk, heads, lo_ref, hi_ref, place_ref, qkv_ref, own_ref, far_ref, d_own_ref, d_far_ref,
    lse_ref, cs_ref, sn_ref, row_ref, wq_hbm, t0, t1, t2, t3,
    keep_ref, send_ref, back_s, sums_ref, q_s, k_s, v_s, g_s, dat_s, dq_s, dk_s, dv_s, inner_s,
    col_s, wq_s, tok_s, sems, token_sems,
):
    place = place_ref[0]
    copies = [
        pltpu.make_async_copy(wq_hbm, wq_s, sems),
        *token_copies((t0, t1, t2, t3), place, tok_s, token_sems),
    ]
    for copy in copies:
        copy.start()
    length = qkv_ref.shape[1]
    half = length // 2
    rows = length // 4
    document_columns(row_ref, col_s)
    mine = pl.multiple_of(place // 2 * half, half)
    away = pl.multiple_of(half - mine, half)
    for start, att_ref, d_ref in ((mine, own_ref, d_own_ref), (away, far_ref, d_far_ref)):
        piece = pl.ds(start, half)
        dat_s[:, piece] = d_ref[...]
        for h in range(heads):
            head = slice(HD * h, HD * h + HD)
            inner_s[h, 0:1, piece] = jnp.sum(
                att_ref[head, :].astype(F32) * d_ref[head, :].astype(F32), axis=0, keepdims=True
            )
            g_s[h, piece, :] = d_ref[head, :].T
    for h in range(heads):
        base = 3 * HD * h
        q_s[h] = qkv_ref[base : base + HD, :].T
        k_s[h] = qkv_ref[base + HD : base + 2 * HD, :].T
        v_s[h] = qkv_ref[base + 2 * HD : base + 3 * HD, :].T
    dq_s[...] = jnp.zeros_like(dq_s)

    def key_block(j, _):
        keys = pl.ds(pl.multiple_of(j * bk, bk), bk)
        dk_s[:, keys, :] = jnp.zeros((heads, bk, HD), F32)
        dv_s[:, keys, :] = jnp.zeros((heads, bk, HD), F32)

        def query_block(i, _):
            columns = pl.ds(pl.multiple_of(i * bq, bq), bq)
            allowed = same_documents(row_ref, col_s, keys, columns, bq)
            scores = [
                dot(
                    k_s[h, keys, :] * jnp.asarray(0.125, BF16),
                    qkv_ref[3 * HD * h : 3 * HD * h + HD, columns],
                )
                for h in range(heads)
            ]
            d_chances = [
                dot(v_s[h, keys, :], dat_s[HD * h : HD * h + HD, columns]) for h in range(heads)
            ]
            lows, d_lows = [], []
            for h in range(heads):
                chances = jnp.where(
                    allowed, jnp.exp(scores[h] - lse_ref[h, 0:1, columns]), 0.0
                )
                lows.append(chances.astype(BF16))
                d_lows.append((chances * (d_chances[h] - inner_s[h, 0:1, columns])).astype(BF16))
            for h in range(heads):
                base = 3 * HD * h
                dv_s[h, keys, :] += dot(lows[h], g_s[h, columns, :])
                dk_s[h, keys, :] += dot(d_lows[h], q_s[h, columns, :])
                dq_s[HD * h : HD * h + HD, columns] += dot(
                    qkv_ref[base + HD : base + 2 * HD, keys], d_lows[h]
                )
            return 0

        lax.fori_loop(lo_ref[j], hi_ref[j], query_block, 0)
        return 0

    lax.fori_loop(0, length // bk, key_block, 0)
    for copy in copies:
        copy.wait()
    step = min(256, rows)

    sums_ref[...] = jnp.zeros_like(sums_ref)
    for r, (ref, entry) in enumerate(
        ((keep_ref, 0), (send_ref, 0), (keep_ref, 1), (send_ref, 1))
    ):

        def finish(i, _):
            start = jnp.bitwise_xor(place, r) * rows + i * step
            piece = pl.ds(pl.multiple_of(start, step), step)
            cosine = cs_ref[:, piece] * 0.125
            sine = sn_ref[:, piece] * 0.125

            def turned_back(row, value):
                a = value[0:HALF, :]
                b = value[HALF:HD, :]
                back_s[row : row + HALF, piece] = (a * cosine + b * sine).astype(BF16)
                back_s[row + HALF : row + HD, piece] = (b * cosine - a * sine).astype(BF16)

            for h in range(heads):
                base = 3 * HD * h
                turned_back(base, dq_s[HD * h : HD * h + HD, piece])
                turned_back(base + HD, dk_s[h, piece, :].T)
                back_s[base + 2 * HD : base + 3 * HD, piece] = dv_s[h, piece, :].T.astype(BF16)
            part = dot(back_s[:, piece].T, wq_s[...], NT)
            unit, _ = normalize(tok_s[piece, :].astype(F32))
            sums_ref[0:1, :] += jnp.sum(part, axis=0, keepdims=True)
            sums_ref[1:2, :] += jnp.sum(part * unit, axis=0, keepdims=True)
            ref[entry, pl.ds(pl.multiple_of(i * step, step), step), :] = part.astype(ref.dtype)
            return 0

        lax.fori_loop(0, rows // step, finish, 0)

def project_grad_kernel(add, normed_ref, back_ref, *rest):
    if add:
        before_ref, *rest = rest
    out_ref, total_s = rest
    step = pl.program_id(0)

    @pl.when(step == 0)
    def _():
        total_s[...] = jnp.zeros_like(total_s)

    total_s[...] += dot(back_ref[...], normed_ref[...])

    @pl.when(step == pl.num_programs(0) - 1)
    def _():
        total = total_s[...].T
        out_ref[...] = total + before_ref[...] if add else total


def project_grad(normed, back, before):
    length, width = normed.shape
    size = back.shape[0]
    add = before is not None
    step = length // 4
    block = pl.BlockSpec((width, size), lambda i: (0, 0))
    return pl.pallas_call(
        functools.partial(project_grad_kernel, add),
        grid=(4,),
        in_specs=[
            pl.BlockSpec((step, width), lambda i: (i, 0)),
            pl.BlockSpec((size, step), lambda i: (0, i)),
        ]
        + [block] * add,
        out_specs=block,
        out_shape=jax.ShapeDtypeStruct((width, size), F32),
        scratch_shapes=[pltpu.VMEM((size, width), F32)],
        cost_estimate=pl.CostEstimate(
            flops=40 * length * width * size, bytes_accessed=length * width * 4, transcendentals=0
        ),
        name="project_grad",
    )(normed, back, *[before] * add)


def held(*shape):
    return pl.BlockSpec(shape, lambda i, *_: (0,) * len(shape), pipeline_mode=pl.Buffered(1))


ANYWHERE = pl.BlockSpec(memory_space=pl.ANY)


def attend(m, blocks, mods, wq, tables, doc_row, bounds, place, heads, bq, bk):
    rows, width = blocks[0].shape
    length = 4 * rows
    size = 3 * HD * heads
    return pl.pallas_call(
        functools.partial(attend_kernel, m, bq, bk, heads),
        grid_spec=pltpu.PrefetchScalarGridSpec(
            num_scalar_prefetch=3,
            grid=(1,),
            in_specs=[ANYWHERE] * 4
            + [
                held(*mods.shape),
                held(width, size),
                held(HALF, length),
                held(HALF, length),
                held(1, length),
            ],
            out_specs=[
                ANYWHERE,
                held(size, length),
                held(HD * heads, length // 2),
                held(HD * heads, length // 2),
                held(heads, 1, length),
            ],
            scratch_shapes=[
                pltpu.VMEM((length, width), BF16),
                pltpu.VMEM((length, width), BF16),
                pltpu.VMEM((size, width), BF16),
                pltpu.VMEM((heads, length, HD), BF16),
                pltpu.VMEM((heads, HD, bq), F32),
                pltpu.VMEM((HD * heads, length), BF16),
                pltpu.VMEM((length, 128), F32),
                pltpu.SemaphoreType.DMA(()),
                pltpu.SemaphoreType.DMA((4,)),
            ],
        ),
        out_shape=[
            jax.ShapeDtypeStruct((length, width), BF16),
            jax.ShapeDtypeStruct((size, length), BF16),
            jax.ShapeDtypeStruct((HD * heads, length // 2), BF16),
            jax.ShapeDtypeStruct((HD * heads, length // 2), BF16),
            jax.ShapeDtypeStruct((heads, 1, length), F32),
        ],
        cost_estimate=pl.CostEstimate(
            flops=heads * length * length * 2400,
            bytes_accessed=length * width * 8,
            transcendentals=heads * length * length // 2,
        ),
        name="attend",
    )(*bounds, place, *blocks, mods, wq, *tables, doc_row)


def attend_back(
    blocks, qkv, att, d_att, lse, tables, doc_row, bounds, place, wq, heads, bq, bk
):
    size, length = qkv.shape
    width = wq.shape[0]
    rows = length // 4
    half = held(HD * heads, length // 2)
    return pl.pallas_call(
        functools.partial(attend_back_kernel, bq, bk, heads),
        grid_spec=pltpu.PrefetchScalarGridSpec(
            num_scalar_prefetch=3,
            grid=(1,),
            in_specs=[
                held(size, length),
                half,
                half,
                half,
                half,
                held(heads, 1, length),
                held(HALF, length),
                held(HALF, length),
                held(1, length),
            ]
            + [ANYWHERE] * 5,
            out_specs=[
                held(2, rows, width),
                held(2, rows, width),
                held(size, length),
                held(2, width),
            ],
            scratch_shapes=[pltpu.VMEM((heads, length, HD), BF16)] * 4
            + [
                pltpu.VMEM((heads * HD, length), BF16),
                pltpu.VMEM((heads * HD, length), F32),
                pltpu.VMEM((heads, length, HD), F32),
                pltpu.VMEM((heads, length, HD), F32),
                pltpu.VMEM((heads, 8, length), F32),
                pltpu.VMEM((length, 128), F32),
                pltpu.VMEM((width, size), BF16),
                pltpu.VMEM((length, width), BF16),
                pltpu.SemaphoreType.DMA(()),
                pltpu.SemaphoreType.DMA((4,)),
            ],
        ),
        out_shape=[
            jax.ShapeDtypeStruct((2, rows, width), F32),
            jax.ShapeDtypeStruct((2, rows, width), BF16),
            jax.ShapeDtypeStruct((size, length), BF16),
            jax.ShapeDtypeStruct((2, width), F32),
        ],
        cost_estimate=pl.CostEstimate(
            flops=heads * length * length * 3600,
            bytes_accessed=length * width * 8,
            transcendentals=heads * length * length // 2,
        ),
        name="attend_back",
    )(*bounds, place, qkv, *att, *d_att, lse, *tables, doc_row, wq, *blocks)


def gelu_pair(values):
    square = values * values
    bend = jnp.tanh(0.7978845608028654 * (values + 0.044715 * (square * values)))
    slope = 0.7978845608028654 * (1.0 + 3 * 0.044715 * square)
    hidden = 0.5 * values * (1.0 + bend)
    return hidden, 0.5 * (1.0 + bend) + 0.5 * values * (1.0 - bend * bend) * slope


def feed_kernel(parts, add, n0, n1, g0, g1, up_ref, down_ref, *rest):
    if add:
        before_ref, *rest = rest
    b0, b1, d0, d1, g_ref, n_s, g_s, n_t, g_t, hidden_s, pre_s = rest
    rows = n0.shape[0]
    up = up_ref[...].reshape(-1, up_ref.shape[-1])
    down = down_ref[...].reshape(-1, down_ref.shape[-1])

    @pl.when(pl.program_id(0) == 0)
    def _():
        for piece, n, g in ((slice(0, rows), n0, g0), (slice(rows, 2 * rows), n1, g1)):
            n_s[piece, :] = n[...]
            g_s[piece, :] = g[...]
            n_t[:, piece] = n[...].T
            g_t[:, piece] = g[...].T
        for ref in (b0, b1, d0, d1):
            ref[...] = jnp.zeros_like(ref)

    step = 2 * rows // parts
    for p in range(parts):
        piece = slice(p * step, (p + 1) * step)
        hidden, slope = gelu_pair(dot(n_s[piece, :], up))
        hidden_s[piece, :] = hidden.astype(BF16)
        pre_s[piece, :] = (dot(g_s[piece, :], down) * slope).astype(BF16)
    for first, b_ref, d_ref in ((0, b0, d0), (rows, b1, d1)):
        for start in range(0, rows, step):
            piece = slice(first + start, first + start + step)
            b_ref[start : start + step, :] += dot(hidden_s[piece, :], down, NT)
            d_ref[start : start + step, :] += dot(pre_s[piece, :], up, NT)
    chunk = up.shape[1]
    for start, left, right in ((0, n_t, pre_s), (chunk, g_t, hidden_s)):
        columns = slice(start, start + chunk)
        grad = dot(left[...], right[...])
        if add:
            grad = grad + before_ref[:, columns]
        g_ref[:, columns] = grad.astype(g_ref.dtype)


CHUNK = 256


def feed(normed, grads, pack, hid, before, kind):
    rows, width = normed[0].shape
    count, _, height, _ = pack.shape
    chunk = CHUNK
    steps = hid // chunk
    add = before is not None

    def weight(first):
        return pl.BlockSpec(
            (count, 1, height, chunk), lambda i: (0, i // steps, 0, first * steps + i % steps)
        )

    block = pl.BlockSpec((rows, width), lambda i: (0, 0))
    columns = pl.BlockSpec((width, 2 * chunk), lambda i: (0, i))
    total = 2 * rows
    return pl.pallas_call(
        functools.partial(feed_kernel, 4, add),
        grid=(2 * steps,),
        in_specs=[block] * 4 + [weight(0), weight(1)] + [columns] * add,
        out_specs=[block] * 4 + [columns],
        out_shape=[jax.ShapeDtypeStruct((rows, width), F32)] * 4
        + [jax.ShapeDtypeStruct((width, 4 * hid), kind)],
        scratch_shapes=[pltpu.VMEM((total, width), BF16)] * 2
        + [pltpu.VMEM((width, total), BF16)] * 2
        + [pltpu.VMEM((total, chunk), BF16)] * 2,
        cost_estimate=pl.CostEstimate(
            flops=24 * total * width * hid,
            bytes_accessed=8 * width * hid + 12 * total * width,
            transcendentals=2 * total * hid,
        ),
        name="feed",
    )(*normed, *grads, pack, pack, *[before] * add)


def block_range(doc_ids, rows, columns):
    by_row = doc_ids.reshape(-1, rows)
    by_column = doc_ids.reshape(-1, columns)
    low = jnp.sum(by_column[:, -1][None, :] < by_row[:, 0][:, None], axis=1, dtype=jnp.int32)
    high = jnp.sum(by_column[:, 0][None, :] <= by_row[:, -1][:, None], axis=1, dtype=jnp.int32)
    return low, high


def turn_tables(length):
    freqs = jnp.exp(-math.log(10000.0) * jnp.arange(HALF, dtype=F32) / HALF)
    angles = freqs[:, None] * jnp.arange(length, dtype=F32)[None, :]
    return jnp.cos(angles), jnp.sin(angles)


def normalize(values):
    center = values - jnp.mean(values, axis=-1, keepdims=True)
    root = lax.rsqrt(jnp.mean(center * center, axis=-1, keepdims=True) + EPSILON)
    return center * root, root


def normalize_back(grad, unit, root, stretch):
    turned = grad * (1.0 + stretch)
    return root * (
        turned
        - jnp.mean(turned, axis=-1, keepdims=True)
        - unit * jnp.mean(turned * unit, axis=-1, keepdims=True)
    )


def per_device(tokens, segments, timesteps, cotangent, w_qkv, w_out, w_up, w_down, w_ada, b_ada):
    micro_count, rows, width = tokens.shape
    heads = HEADS // 4
    length = 4 * rows
    count = dp_bits()
    tensor = lax.axis_index("tensor")
    far, near = tensor // 2, tensor % 2
    device = lax.axis_index("dp") * 4 + tensor
    falling = list(range(count - 1, -1, -1))
    rising = list(range(count))

    gathering = gather_blocks(w_qkv, falling)
    states = []

    def advance(value, step):
        while len(states) <= step:
            states.append(next(gathering))
        return after(value, states[step])

    blocks = []

    def with_stamps(value, bit):
        if bit == 1:
            ready = after(tokens, value)
            for m in range(micro_count):
                across = swap_far(ready[m])
                pair = (ready[m], swap_near(ready[m]), across)
                blocks.append(pair if m > 0 else (*pair, swap_near(across)))
        return advance(value, bit - 2) if bit >= 2 else value

    def with_terms(value, bit):
        return advance(value, count - 2) if bit == count - 1 else value

    feature_rows = w_ada.shape[0]
    half = feature_rows * lax.axis_size("dp") * 4 // 2
    stamps = gather_relative(timesteps[:, 0].astype(F32), with_stamps)
    index = device * feature_rows + jnp.arange(feature_rows)
    freqs = jnp.exp(-math.log(10000.0) * (index % half).astype(F32) / half)
    angles = stamps[:, :, None] * freqs
    cond = jnp.where(index < half, jnp.cos(angles), jnp.sin(angles)).astype(BF16)
    cond = cond.reshape(-1, feature_rows)
    bias_size = b_ada.shape[0]
    slots = w_ada.shape[1] // bias_size
    bias = jnp.where(
        jnp.arange(slots)[:, None] == device, b_ada.astype(F32)[None, :], 0.0
    ).reshape(-1)
    terms = dot(cond, w_ada) + bias
    mods = scatter_relative(terms.reshape(-1, micro_count, terms.shape[1]), with_terms)

    mods = after(advance(mods, count - 1), blocks[0][3])
    mods = mods + swap_far(mods)
    mods = mods + swap_near(mods)

    wq = states[-1].reshape(width, -1)
    pack = after(jnp.concatenate([w_up, w_down.T, w_out.T], axis=1), stamps)
    groups = [
        [4 * i + 2 * j + c for i in range(lax.axis_size("dp")) for j in range(2)] for c in range(2)
    ]
    pack = lax.all_gather(pack, ("dp", "tensor"), axis_index_groups=groups)
    pack = pack.reshape((-1, 2) + pack.shape[1:])
    hid = w_up.shape[1]
    part = w_out.shape[0]
    wo = pack[..., 2 * hid :].reshape(-1, 2, w_out.shape[1], part)
    wo = pick(far, wo, wo[:, ::-1]).transpose(0, 2, 1, 3).reshape(width, 2 * part)
    if w_up.shape[0] % 16:
        pack = pack.transpose(1, 0, 2, 3).reshape(1, 2, width, -1)

    tables = turn_tables(length)
    place = tensor.astype(jnp.int32).reshape(1)
    fq, fk = min(512, length), min(512, length)
    rq, rk = min(512, length), min(256, length)
    doc_rows = segments.astype(F32)

    state = []
    for m in range(micro_count):
        if m > 0:
            own, near_own, across = blocks[m]
            across = after(across, state[-1][3])
            blocks[m] = (own, near_own, across, swap_near(across))
        normed_a, qkv, att_own, att_away, lse = attend(
            m, blocks[m], mods, wq, tables, doc_rows[m : m + 1],
            block_range(segments[m], fq, fk), place, heads, fq, fk,
        )
        state.append((normed_a, qkv, (att_own, att_away), lse))

    outputs = []
    grads_out = []
    grads_feed = None
    middles = []
    for m in range(micro_count):
        shift_a, scale_a, gate_a, shift_m, scale_m, gate_m = jnp.split(mods[m], 6)
        att_own, att_away = state[m][2]
        arrived = swap_far(att_away)
        if m + 1 < micro_count:
            arrived = after(arrived, state[m + 1][2][0])
        if m > 0:
            arrived = after(arrived, branch_own)
        att = jnp.concatenate([att_own, arrived])
        inputs = tokens[m].astype(F32)
        grad_out = cotangent[m].astype(F32)
        grad_m = (grad_out * gate_m).astype(BF16)
        branch = dot(att, wo, TT)
        first, second = branch[:rows], branch[rows:]
        branch_a = pick(near, first, second) + swap_near(pick(near, second, first))
        middle = inputs + gate_a * branch_a
        unit_m, root_m = normalize(middle)
        normed_m = (unit_m * (1.0 + scale_m) + shift_m).astype(BF16)
        branch_own, branch_near, d_own, d_near, grads_feed = feed(
            (normed_m, swap_near(normed_m)),
            (grad_m, swap_near(grad_m)),
            pack,
            hid,
            grads_feed,
            BF16 if m + 1 == micro_count else F32,
        )

        branch_m = branch_own + swap_near(branch_near)
        outputs.append((middle + gate_m * branch_m).astype(BF16))
        d_gate_m = jnp.sum(grad_out * branch_m, axis=0)
        d_normed_m = d_own + swap_near(d_near)
        d_shift_m = jnp.sum(d_normed_m, axis=0)
        d_scale_m = jnp.sum(d_normed_m * unit_m, axis=0)
        d_middle = grad_out + normalize_back(d_normed_m, unit_m, root_m, scale_m)
        d_gate_a = jnp.sum(d_middle * branch_a, axis=0)
        grad_a = (d_middle * gate_a).astype(BF16)
        other = swap_near(grad_a)
        grad_a2 = jnp.concatenate([pick(near, grad_a, other), pick(near, other, grad_a)])
        d_att = dot(wo, grad_a2, TT).astype(BF16)
        grads_out.append(dot(grad_a2, att, TT))
        if m > 0:
            middles[m - 1][1][1] = after(middles[m - 1][1][1], d_att)
        d_att = [d_att[:part], swap_far(d_att[part:])]
        middles.append((d_middle, d_att, d_gate_a, d_shift_m, d_scale_m, d_gate_m))

    feed_total = lax.psum_scatter(grads_feed, "dp", scatter_dimension=0, tiled=True)
    out_total = lax.psum_scatter(
        sum(grads_out).astype(BF16), "dp", scatter_dimension=0, tiled=True
    )

    input_grads = []
    mod_grads = []
    g_qkv = None
    backs = []
    for m in range(micro_count):
        normed_a, qkv, att, lse = state[m]
        keep, send, back, sums = attend_back(
            blocks[m], qkv, att, middles[m][1], lse, tables, doc_rows[m : m + 1],
            block_range(segments[m], rk, rq), place, wq, heads, rq, rk,
        )
        arrived = swap_near(send).astype(F32)
        crossing = (keep[1] + arrived[1]).astype(BF16)
        crossed = swap_far(crossing)
        g_qkv = project_grad(normed_a, back, g_qkv)
        if m + 1 < micro_count:
            middles[m + 1][1][1] = after(middles[m + 1][1][1], (crossing, g_qkv))
        if m > 0:
            backs[m - 1][1] = after(backs[m - 1][1], sums)
        backs.append([keep[0] + arrived[0], crossed])
        _, _, d_gate_a, d_shift_m, d_scale_m, d_gate_m = middles[m]
        mod_grads.append(
            jnp.concatenate([sums[0], sums[1], d_gate_a, d_shift_m, d_scale_m, d_gate_m])
        )
    for m in range(micro_count):
        scale_a = jnp.split(mods[m], 6)[1]
        d_normed_a = backs[m][0] + backs[m][1].astype(F32)
        unit, root = normalize(tokens[m].astype(F32))
        input_grads.append(middles[m][0] + normalize_back(d_normed_a, unit, root, scale_a))
    height = feed_total.shape[0]
    sides = feed_total.reshape(height, 2, hid // CHUNK, 2, CHUNK)
    sides = [sides[:, side].transpose(0, 2, 1, 3).reshape(height, 2 * hid) for side in range(2)]
    mine = jnp.concatenate([pick(far, sides[0], sides[1]), out_total[:, :part]], axis=1)
    away = jnp.concatenate([pick(far, sides[1], sides[0]), out_total[:, part:]], axis=1)
    total = mine.astype(F32) + swap_far(after(away, backs[-1][1])).astype(F32)
    g_up = total[:, :hid]
    g_down = total[:, hid : 2 * hid].T
    g_out = total[:, 2 * hid :].T

    g_last = after(g_qkv, crossing)
    g_qkv = scatter_blocks(
        g_last,
        rising,
        lambda value, bit: after(value, backs[-1][1]) if bit == 1 else value,
    )

    d_mods = jnp.stack(mod_grads)
    d_mods = after(d_mods + swap_far(d_mods), g_last)
    d_mods = d_mods + swap_near(d_mods)
    all_mods = gather_relative(d_mods).reshape(-1, d_mods.shape[1])
    g_ada = lax.dot_general(
        cond.astype(F32),
        all_mods,
        TN,
        precision=lax.Precision.HIGHEST,
        preferred_element_type=F32,
    )
    g_bias = lax.dynamic_slice_in_dim(jnp.sum(all_mods, axis=0), device * bias_size, bias_size)
    return (
        jnp.stack(outputs),
        jnp.stack(input_grads),
        g_qkv,
        g_out,
        g_up,
        g_down,
        g_ada,
        g_bias,
    )


def solution(mesh):
    return jax.shard_map(
        per_device,
        mesh=mesh,
        in_specs=(
            P(None, ("dp", "tensor"), None),
            P(None, "dp"),
            P(None, "dp"),
            P(None, ("dp", "tensor"), None),
            P("dp", "tensor"),
            P("tensor", "dp"),
            P("dp", "tensor"),
            P("tensor", "dp"),
            P(("dp", "tensor"), None),
            P(("dp", "tensor")),
        ),
        out_specs=(
            P(None, ("dp", "tensor"), None),
            P(None, ("dp", "tensor"), None),
            P("dp", "tensor"),
            P("tensor", "dp"),
            P("dp", "tensor"),
            P("tensor", "dp"),
            P(("dp", "tensor"), None),
            P(("dp", "tensor")),
        ),
        check_vma=False,
    )
```

```python
import functools
import math

import jax
import jax.numpy as jnp
from jax import lax
from jax.experimental import pallas as pl
from jax.experimental.pallas import tpu as pltpu
from jax.sharding import PartitionSpec as P

HEADS = 12
HD = 64
HALF = HD // 2
EPSILON = 1e-06
MASKED = -1e30
F32 = jnp.float32
BF16 = jnp.bfloat16
NN = (((1,), (0,)), ((), ()))
NT = (((1,), (1,)), ((), ()))
TN = (((0,), (0,)), ((), ()))
TT = (((0,), (1,)), ((), ()))


def dot(left, right, dims=NN):
    return lax.dot_general(left, right, dims, preferred_element_type=F32)


def pick(bit, zero, one):
    return jnp.where(bit == 0, zero, one)


def swap_far(value):
    return lax.ppermute(value, "tensor", [(i, i ^ 2) for i in range(4)])


def swap_near(value):
    return lax.ppermute(value, "tensor", [(i, i ^ 1) for i in range(4)])


def swap_dp(value, bit):
    count = lax.axis_size("dp")
    return lax.ppermute(value, "dp", [(i, i ^ (1 << bit)) for i in range(count)])


def after(value, other):
    return lax.optimization_barrier((value, other))[0]


def dp_bits():
    return lax.axis_size("dp").bit_length() - 1


def my_bit(bit):
    return (lax.axis_index("dp") >> bit) & 1


def gather_block(current, bit, done, arrival=lambda value: value):
    arrived = arrival(swap_dp(current, bit))
    place = sum(1 for other in done if other > bit)
    mine = my_bit(bit)
    return jnp.stack([pick(mine, current, arrived), pick(mine, arrived, current)], axis=place)


def halves(current, bit, left):
    place = left.index(bit)
    first = lax.index_in_dim(current, 0, place, keepdims=False)
    second = lax.index_in_dim(current, 1, place, keepdims=False)
    mine = my_bit(bit)
    return pick(mine, first, second), pick(mine, second, first).astype(BF16)


def by_bits(total):
    return total.reshape((2,) * dp_bits() + (-1, total.shape[-1]))


def gather_relative(value, first=lambda value, bit: value):
    current = value
    for bit in range(dp_bits()):
        current = first(current, bit)
        current = jnp.stack([current, swap_dp(current, bit)])
    return current.reshape((-1,) + value.shape)


def scatter_relative(terms, first=lambda value, bit: value):
    count = dp_bits()
    current = terms.reshape((2,) * count + terms.shape[1:])
    for bit in range(count):
        current = first(current, bit)
        place = count - 1 - bit
        kept = lax.index_in_dim(current, 0, place, keepdims=False)
        sent = lax.index_in_dim(current, 1, place, keepdims=False)
        current = kept + swap_dp(sent, bit)
    return current


def document_columns(row_ref, col_s):
    for start in range(0, row_ref.shape[1], 128):
        tile = jnp.broadcast_to(row_ref[0:1, start : start + 128], (128, 128))
        col_s[start : start + 128, :] = tile.T


def token_copies(refs, place, tok_s, sems):
    rows = tok_s.shape[0] // 4
    return [
        pltpu.make_async_copy(
            ref,
            tok_s.at[pl.ds(pl.multiple_of(jnp.bitwise_xor(place, r) * rows, rows), rows), :],
            sems.at[r],
        )
        for r, ref in enumerate(refs)
    ]


def same_documents(row_ref, col_s, rows, columns, size):
    return jnp.concatenate([col_s[rows, :]] * (size // 128), axis=1) == row_ref[0:1, columns]


def attend_kernel(
    m, bq, bk, heads, lo_ref, hi_ref, place_ref, t0, t1, t2, t3, mods_ref, wq_ref, cs_ref, sn_ref,
    row_ref, normed_hbm, qkv_ref, own_ref, far_ref, lse_ref,
    tok_s, normed_s, wq_s, key_s, acc_s, att_s, col_s, sem, token_sems,
):
    length, width = tok_s.shape
    rows = length // 4
    place = place_ref[0]
    copies = token_copies((t0, t1, t2, t3), place, tok_s, token_sems)
    for copy in copies:
        copy.start()
    wq_s[...] = wq_ref[...].T
    document_columns(row_ref, col_s)
    for copy in copies:
        copy.wait()
    shift = mods_ref[m : m + 1, 0:width]
    stretch = 1.0 + mods_ref[m : m + 1, width : 2 * width]
    step = min(256, rows)

    def project(i, _):
        piece = pl.ds(pl.multiple_of(i * step, step), step)
        unit, _ = normalize(tok_s[piece, :].astype(F32))
        normed = (unit * stretch + shift).astype(BF16)
        normed_s[piece, :] = normed
        packed = dot(wq_s[...], normed, NT)
        cosine = cs_ref[:, piece]
        sine = sn_ref[:, piece]
        for h in range(heads):
            base = 3 * HD * h

            def turned(row):
                a = packed[row : row + HALF]
                b = packed[row + HALF : row + HD]
                return jnp.concatenate([a * cosine - b * sine, a * sine + b * cosine], axis=0)

            qkv_ref[base : base + HD, piece] = turned(base).astype(BF16)
            keys = turned(base + HD)
            qkv_ref[base + HD : base + 2 * HD, piece] = keys.astype(BF16)
            key_s[h, piece, :] = keys.T.astype(BF16)
            qkv_ref[base + 2 * HD : base + 3 * HD, piece] = packed[
                base + 2 * HD : base + 3 * HD
            ].astype(BF16)
        return 0

    lax.fori_loop(0, length // step, project, 0)
    copy = pltpu.make_async_copy(normed_s, normed_hbm, sem)
    copy.start()

    def query_block(i, _):
        columns = pl.ds(pl.multiple_of(i * bq, bq), bq)
        queries = [
            qkv_ref[3 * HD * h : 3 * HD * h + HD, columns] * jnp.asarray(0.125, BF16)
            for h in range(heads)
        ]
        acc_s[...] = jnp.zeros_like(acc_s)

        def key_block(j, carry):
            keys = pl.ds(pl.multiple_of(j * bk, bk), bk)
            allowed = same_documents(row_ref, col_s, keys, columns, bq)
            scores = [dot(key_s[h, keys, :], queries[h]) for h in range(heads)]
            result, fades, lows = [], [], []
            for h in range(heads):
                top, total = carry[2 * h], carry[2 * h + 1]
                masked = jnp.where(allowed, scores[h], MASKED)
                new_top = jnp.maximum(top, jnp.max(masked, axis=0, keepdims=True))
                fade = jnp.exp(top - new_top)
                chances = jnp.exp(masked - new_top)
                total = fade * total + jnp.sum(chances, axis=0, keepdims=True)
                lows.append(chances.astype(BF16))
                fades.append(fade)
                result += [new_top, total]
            for h in range(heads):
                values = qkv_ref[3 * HD * h + 2 * HD : 3 * HD * h + 3 * HD, keys]
                acc_s[h] = acc_s[h] * fades[h] + dot(values, lows[h])
            return tuple(result)

        start = (jnp.full((1, bq), MASKED, F32), jnp.zeros((1, bq), F32)) * heads
        carry = lax.fori_loop(lo_ref[i], hi_ref[i], key_block, start)
        for h in range(heads):
            top, total = carry[2 * h], carry[2 * h + 1]
            att_s[HD * h : HD * h + HD, columns] = (acc_s[h] / total).astype(BF16)
            lse_ref[h, 0:1, columns] = top + jnp.log(total)
        return 0

    lax.fori_loop(0, length // bq, query_block, 0)
    half = length // 2
    mine = pl.multiple_of(place // 2 * half, half)
    away = pl.multiple_of(half - mine, half)
    own_ref[...] = att_s[:, pl.ds(mine, half)]
    far_ref[...] = att_s[:, pl.ds(away, half)]
    copy.wait()


def attend_back_kernel(
    bq, bk, heads, lo_ref, hi_ref, place_ref, qkv_ref, own_ref, far_ref, d_own_ref, d_far_ref,
    lse_ref, cs_ref, sn_ref, row_ref, wq_hbm, t0, t1, t2, t3,
    keep_ref, send_ref, back_s, sums_ref, q_s, k_s, v_s, g_s, dat_s, dq_s, dk_s, dv_s, inner_s,
    col_s, wq_s, tok_s, sems, token_sems,
):
    place = place_ref[0]
    copies = [
        pltpu.make_async_copy(wq_hbm, wq_s, sems),
        *token_copies((t0, t1, t2, t3), place, tok_s, token_sems),
    ]
    for copy in copies:
        copy.start()
    length = qkv_ref.shape[1]
    half = length // 2
    rows = length // 4
    document_columns(row_ref, col_s)
    mine = pl.multiple_of(place // 2 * half, half)
    away = pl.multiple_of(half - mine, half)
    for start, att_ref, d_ref in ((mine, own_ref, d_own_ref), (away, far_ref, d_far_ref)):
        piece = pl.ds(start, half)
        dat_s[:, piece] = d_ref[...]
        for h in range(heads):
            head = slice(HD * h, HD * h + HD)
            inner_s[h, 0:1, piece] = jnp.sum(
                att_ref[head, :].astype(F32) * d_ref[head, :].astype(F32), axis=0, keepdims=True
            )
            g_s[h, piece, :] = d_ref[head, :].T
    for h in range(heads):
        base = 3 * HD * h
        q_s[h] = qkv_ref[base : base + HD, :].T
        k_s[h] = qkv_ref[base + HD : base + 2 * HD, :].T
        v_s[h] = qkv_ref[base + 2 * HD : base + 3 * HD, :].T
    dq_s[...] = jnp.zeros_like(dq_s)

    def key_block(j, _):
        keys = pl.ds(pl.multiple_of(j * bk, bk), bk)
        dk_s[:, keys, :] = jnp.zeros((heads, bk, HD), F32)
        dv_s[:, keys, :] = jnp.zeros((heads, bk, HD), F32)

        def query_block(i, _):
            columns = pl.ds(pl.multiple_of(i * bq, bq), bq)
            allowed = same_documents(row_ref, col_s, keys, columns, bq)
            scores = [
                dot(
                    k_s[h, keys, :] * jnp.asarray(0.125, BF16),
                    qkv_ref[3 * HD * h : 3 * HD * h + HD, columns],
                )
                for h in range(heads)
            ]
            d_chances = [
                dot(v_s[h, keys, :], dat_s[HD * h : HD * h + HD, columns]) for h in range(heads)
            ]
            lows, d_lows = [], []
            for h in range(heads):
                chances = jnp.where(
                    allowed, jnp.exp(scores[h] - lse_ref[h, 0:1, columns]), 0.0
                )
                lows.append(chances.astype(BF16))
                d_lows.append((chances * (d_chances[h] - inner_s[h, 0:1, columns])).astype(BF16))
            for h in range(heads):
                base = 3 * HD * h
                dv_s[h, keys, :] += dot(lows[h], g_s[h, columns, :])
                dk_s[h, keys, :] += dot(d_lows[h], q_s[h, columns, :])
                dq_s[HD * h : HD * h + HD, columns] += dot(
                    qkv_ref[base + HD : base + 2 * HD, keys], d_lows[h]
                )
            return 0

        lax.fori_loop(lo_ref[j], hi_ref[j], query_block, 0)
        return 0

    lax.fori_loop(0, length // bk, key_block, 0)
    for copy in copies:
        copy.wait()
    step = min(256, rows)

    sums_ref[...] = jnp.zeros_like(sums_ref)
    for r, (ref, entry) in enumerate(
        ((keep_ref, 0), (send_ref, 0), (keep_ref, 1), (send_ref, 1))
    ):

        def finish(i, _):
            start = jnp.bitwise_xor(place, r) * rows + i * step
            piece = pl.ds(pl.multiple_of(start, step), step)
            cosine = cs_ref[:, piece] * 0.125
            sine = sn_ref[:, piece] * 0.125

            def turned_back(row, value):
                a = value[0:HALF, :]
                b = value[HALF:HD, :]
                back_s[row : row + HALF, piece] = (a * cosine + b * sine).astype(BF16)
                back_s[row + HALF : row + HD, piece] = (b * cosine - a * sine).astype(BF16)

            for h in range(heads):
                base = 3 * HD * h
                turned_back(base, dq_s[HD * h : HD * h + HD, piece])
                turned_back(base + HD, dk_s[h, piece, :].T)
                back_s[base + 2 * HD : base + 3 * HD, piece] = dv_s[h, piece, :].T.astype(BF16)
            part = dot(back_s[:, piece].T, wq_s[...], NT)
            unit, _ = normalize(tok_s[piece, :].astype(F32))
            sums_ref[0:1, :] += jnp.sum(part, axis=0, keepdims=True)
            sums_ref[1:2, :] += jnp.sum(part * unit, axis=0, keepdims=True)
            ref[entry, pl.ds(pl.multiple_of(i * step, step), step), :] = part.astype(ref.dtype)
            return 0

        lax.fori_loop(0, rows // step, finish, 0)

def project_grad_kernel(add, normed_ref, back_ref, *rest):
    if add:
        before_ref, *rest = rest
    out_ref, total_s = rest
    step = pl.program_id(0)

    @pl.when(step == 0)
    def _():
        total_s[...] = jnp.zeros_like(total_s)

    total_s[...] += dot(back_ref[...], normed_ref[...])

    @pl.when(step == pl.num_programs(0) - 1)
    def _():
        total = total_s[...].T
        out_ref[...] = total + before_ref[...] if add else total


def project_grad(normed, back, before):
    length, width = normed.shape
    size = back.shape[0]
    add = before is not None
    step = length // 4
    block = pl.BlockSpec((width, size), lambda i: (0, 0))
    return pl.pallas_call(
        functools.partial(project_grad_kernel, add),
        grid=(4,),
        in_specs=[
            pl.BlockSpec((step, width), lambda i: (i, 0)),
            pl.BlockSpec((size, step), lambda i: (0, i)),
        ]
        + [block] * add,
        out_specs=block,
        out_shape=jax.ShapeDtypeStruct((width, size), F32),
        scratch_shapes=[pltpu.VMEM((size, width), F32)],
        cost_estimate=pl.CostEstimate(
            flops=40 * length * width * size, bytes_accessed=length * width * 4, transcendentals=0
        ),
        name="project_grad",
    )(normed, back, *[before] * add)


def held(*shape):
    return pl.BlockSpec(shape, lambda i, *_: (0,) * len(shape), pipeline_mode=pl.Buffered(1))


ANYWHERE = pl.BlockSpec(memory_space=pl.ANY)


def attend(m, blocks, mods, wq, tables, doc_row, bounds, place, heads, bq, bk):
    rows, width = blocks[0].shape
    length = 4 * rows
    size = 3 * HD * heads
    return pl.pallas_call(
        functools.partial(attend_kernel, m, bq, bk, heads),
        grid_spec=pltpu.PrefetchScalarGridSpec(
            num_scalar_prefetch=3,
            grid=(1,),
            in_specs=[ANYWHERE] * 4
            + [
                held(*mods.shape),
                held(width, size),
                held(HALF, length),
                held(HALF, length),
                held(1, length),
            ],
            out_specs=[
                ANYWHERE,
                held(size, length),
                held(HD * heads, length // 2),
                held(HD * heads, length // 2),
                held(heads, 1, length),
            ],
            scratch_shapes=[
                pltpu.VMEM((length, width), BF16),
                pltpu.VMEM((length, width), BF16),
                pltpu.VMEM((size, width), BF16),
                pltpu.VMEM((heads, length, HD), BF16),
                pltpu.VMEM((heads, HD, bq), F32),
                pltpu.VMEM((HD * heads, length), BF16),
                pltpu.VMEM((length, 128), F32),
                pltpu.SemaphoreType.DMA(()),
                pltpu.SemaphoreType.DMA((4,)),
            ],
        ),
        out_shape=[
            jax.ShapeDtypeStruct((length, width), BF16),
            jax.ShapeDtypeStruct((size, length), BF16),
            jax.ShapeDtypeStruct((HD * heads, length // 2), BF16),
            jax.ShapeDtypeStruct((HD * heads, length // 2), BF16),
            jax.ShapeDtypeStruct((heads, 1, length), F32),
        ],
        cost_estimate=pl.CostEstimate(
            flops=heads * length * length * 2400,
            bytes_accessed=length * width * 8,
            transcendentals=heads * length * length // 2,
        ),
        compiler_params=pltpu.CompilerParams(vmem_limit_bytes=46 * 2**20),
        name="attend",
    )(*bounds, place, *blocks, mods, wq, *tables, doc_row)


def attend_back(
    blocks, qkv, att, d_att, lse, tables, doc_row, bounds, place, wq, heads, bq, bk
):
    size, length = qkv.shape
    width = wq.shape[0]
    rows = length // 4
    half = held(HD * heads, length // 2)
    return pl.pallas_call(
        functools.partial(attend_back_kernel, bq, bk, heads),
        grid_spec=pltpu.PrefetchScalarGridSpec(
            num_scalar_prefetch=3,
            grid=(1,),
            in_specs=[
                held(size, length),
                half,
                half,
                half,
                half,
                held(heads, 1, length),
                held(HALF, length),
                held(HALF, length),
                held(1, length),
            ]
            + [ANYWHERE] * 5,
            out_specs=[
                held(2, rows, width),
                held(2, rows, width),
                held(size, length),
                held(2, width),
            ],
            scratch_shapes=[pltpu.VMEM((heads, length, HD), BF16)] * 4
            + [
                pltpu.VMEM((heads * HD, length), BF16),
                pltpu.VMEM((heads * HD, length), F32),
                pltpu.VMEM((heads, length, HD), F32),
                pltpu.VMEM((heads, length, HD), F32),
                pltpu.VMEM((heads, 8, length), F32),
                pltpu.VMEM((length, 128), F32),
                pltpu.VMEM((width, size), BF16),
                pltpu.VMEM((length, width), BF16),
                pltpu.SemaphoreType.DMA(()),
                pltpu.SemaphoreType.DMA((4,)),
            ],
        ),
        out_shape=[
            jax.ShapeDtypeStruct((2, rows, width), F32),
            jax.ShapeDtypeStruct((2, rows, width), BF16),
            jax.ShapeDtypeStruct((size, length), BF16),
            jax.ShapeDtypeStruct((2, width), F32),
        ],
        cost_estimate=pl.CostEstimate(
            flops=heads * length * length * 3600,
            bytes_accessed=length * width * 8,
            transcendentals=heads * length * length // 2,
        ),
        compiler_params=pltpu.CompilerParams(vmem_limit_bytes=50 * 2**20),
        name="attend_back",
    )(*bounds, place, qkv, *att, *d_att, lse, *tables, doc_row, wq, *blocks)


def gelu_pair(values):
    square = values * values
    bend = jnp.tanh(0.7978845608028654 * (values + 0.044715 * (square * values)))
    slope = 0.7978845608028654 * (1.0 + 3 * 0.044715 * square)
    hidden = 0.5 * values * (1.0 + bend)
    return hidden, 0.5 * (1.0 + bend) + 0.5 * values * (1.0 - bend * bend) * slope


def feed_kernel(parts, add, n0, n1, g0, g1, up_ref, down_ref, *rest):
    if add:
        before_ref, *rest = rest
    b0, b1, d0, d1, g_ref, n_s, g_s, n_t, g_t, hidden_s, pre_s, b1_s, d1_s = rest
    rows = n0.shape[0]
    up = up_ref[...].reshape(-1, up_ref.shape[-1])
    down = down_ref[...].reshape(-1, down_ref.shape[-1])

    @pl.when(pl.program_id(0) == 0)
    def _():
        for piece, n, g in ((slice(0, rows), n0, g0), (slice(rows, 2 * rows), n1, g1)):
            n_s[piece, :] = n[...]
            g_s[piece, :] = g[...]
            n_t[:, piece] = n[...].T
            g_t[:, piece] = g[...].T
        for ref in (b0, b1_s, d0, d1_s):
            ref[...] = jnp.zeros_like(ref)

    step = 2 * rows // parts
    for p in range(parts):
        piece = slice(p * step, (p + 1) * step)
        hidden, slope = gelu_pair(dot(n_s[piece, :], up))
        hidden_s[piece, :] = hidden.astype(BF16)
        pre_s[piece, :] = (dot(g_s[piece, :], down) * slope).astype(BF16)
    for first, b_ref, d_ref in ((0, b0, d0), (rows, b1_s, d1_s)):
        for start in range(0, rows, step):
            piece = slice(first + start, first + start + step)
            b_ref[start : start + step, :] += dot(hidden_s[piece, :], down, NT)
            d_ref[start : start + step, :] += dot(pre_s[piece, :], up, NT)
    chunk = up.shape[1]
    for start, left, right in ((0, n_t, pre_s), (chunk, g_t, hidden_s)):
        columns = slice(start, start + chunk)
        grad = dot(left[...], right[...])
        if add:
            grad = grad + before_ref[:, columns]
        g_ref[:, columns] = grad.astype(g_ref.dtype)

    @pl.when(pl.program_id(0) == pl.num_programs(0) - 1)
    def _():
        b1[...] = b1_s[...].astype(BF16)
        d1[...] = d1_s[...].astype(BF16)


CHUNK = 256


def feed(normed, grads, pack, hid, before, kind):
    rows, width = normed[0].shape
    count, _, height, _ = pack.shape
    chunk = CHUNK
    steps = hid // chunk
    add = before is not None

    def weight(first):
        return pl.BlockSpec(
            (count, 1, height, chunk), lambda i: (0, i // steps, 0, first * steps + i % steps)
        )

    block = pl.BlockSpec((rows, width), lambda i: (0, 0))
    columns = pl.BlockSpec((width, 2 * chunk), lambda i: (0, i))
    total = 2 * rows
    return pl.pallas_call(
        functools.partial(feed_kernel, 4, add),
        grid=(2 * steps,),
        in_specs=[block] * 4 + [weight(0), weight(1)] + [columns] * add,
        out_specs=[block] * 4 + [columns],
        out_shape=[jax.ShapeDtypeStruct((rows, width), kind) for kind in (F32, BF16, F32, BF16)]
        + [jax.ShapeDtypeStruct((width, 4 * hid), kind)],
        scratch_shapes=[pltpu.VMEM((total, width), BF16)] * 2
        + [pltpu.VMEM((width, total), BF16)] * 2
        + [pltpu.VMEM((total, chunk), BF16)] * 2
        + [pltpu.VMEM((rows, width), F32)] * 2,
        cost_estimate=pl.CostEstimate(
            flops=24 * total * width * hid,
            bytes_accessed=8 * width * hid + 12 * total * width,
            transcendentals=2 * total * hid,
        ),
        compiler_params=pltpu.CompilerParams(vmem_limit_bytes=46 * 2**20),
        name="feed",
    )(*normed, *grads, pack, pack, *[before] * add)


def terms_kernel(cond_ref, w_ref, bias_ref, out_ref):
    total = bias_ref[...] + jnp.zeros_like(out_ref)
    for r in range(w_ref.shape[0]):
        total = total + cond_ref[:, r : r + 1] * w_ref[r : r + 1, :].astype(F32)
    out_ref[...] = total


def mod_terms(cond, w_ada, bias):
    return pl.pallas_call(
        terms_kernel,
        out_shape=jax.ShapeDtypeStruct((cond.shape[0], w_ada.shape[1]), F32),
        cost_estimate=pl.CostEstimate(
            flops=2 * cond.size * w_ada.shape[1],
            bytes_accessed=4 * cond.shape[0] * w_ada.shape[1],
            transcendentals=0,
        ),
        name="mod_terms",
    )(cond.astype(F32), w_ada, bias[None, :])


def part_of(mods_ref, m, k, width):
    return mods_ref[m : m + 1, k * width : (k + 1) * width]


def out_weights(pack_ref, side, size):
    return pack_ref[:, pl.ds(side, 1), :, 0:size].reshape(-1, size)


def out_kernel(place_ref, own_ref, far_ref, pack_ref, keep_ref, send_ref):
    size, total = own_ref.shape
    rows = total // 2
    side, near = place_ref[0] // 2, place_ref[0] % 2
    own_w = out_weights(pack_ref, side, size)
    far_w = out_weights(pack_ref, 1 - side, size)
    for ref, half in ((keep_ref, near), (send_ref, 1 - near)):
        piece = pl.ds(pl.multiple_of(half * rows, rows), rows)
        ref[...] = (
            dot(own_ref[:, piece].T, own_w, NT) + dot(far_ref[:, piece].T, far_w, NT)
        ).astype(ref.dtype)


def pack_tail(pack):
    count, _, height, columns = pack.shape
    return pl.BlockSpec((count, 2, height, CHUNK), lambda i, *_: (0, 0, 0, columns // CHUNK))


def out_project(place, own, away, pack):
    size, total = own.shape
    rows, width = total // 2, pack.shape[0] * pack.shape[2]
    return pl.pallas_call(
        out_kernel,
        grid_spec=pltpu.PrefetchScalarGridSpec(
            num_scalar_prefetch=1,
            grid=(1,),
            in_specs=[held(size, total), held(size, total), pack_tail(pack)],
            out_specs=[held(rows, width), held(rows, width)],
        ),
        out_shape=[
            jax.ShapeDtypeStruct((rows, width), F32),
            jax.ShapeDtypeStruct((rows, width), BF16),
        ],
        cost_estimate=pl.CostEstimate(
            flops=8 * total * width * size, bytes_accessed=total * width * 4, transcendentals=0
        ),
        compiler_params=pltpu.CompilerParams(vmem_limit_bytes=20 * 2**20),
        name="out_project",
    )(place, own, away, pack)


def out_back_kernel(add, place_ref, g0_ref, g1_ref, own_ref, far_ref, pack_ref, *rest):
    if add:
        *before_refs, = rest[:2]
        rest = rest[2:]
    d_own_ref, d_far_ref, *grad_refs = rest
    size, total = own_ref.shape
    rows = total // 2
    side, near = place_ref[0] // 2, place_ref[0] % 2
    pieces = [
        pl.ds(pl.multiple_of(half * rows, rows), rows) for half in (near, 1 - near)
    ]
    grads = [g0_ref[...], g1_ref[...]]
    turned = [grad.T for grad in grads]
    for k, (att_ref, d_ref, which) in enumerate(
        ((own_ref, d_own_ref, side), (far_ref, d_far_ref, 1 - side))
    ):
        weights = out_weights(pack_ref, which, size).T
        total_grad = 0.0
        for grad, flipped, piece in zip(grads, turned, pieces):
            d_ref[:, piece] = dot(weights, grad, NT).astype(BF16)
            total_grad = total_grad + dot(flipped, att_ref[:, piece], NT)
        if add:
            total_grad = total_grad + before_refs[k][...]
        grad_refs[k][...] = total_grad.astype(grad_refs[k].dtype)


def out_back(place, grads, own, away, pack, before, last):
    size, total = own.shape
    rows, width = grads[0].shape
    add = before is not None
    half = held(size, total)
    return pl.pallas_call(
        functools.partial(out_back_kernel, add),
        grid_spec=pltpu.PrefetchScalarGridSpec(
            num_scalar_prefetch=1,
            grid=(1,),
            in_specs=[held(rows, width)] * 2
            + [half, half, pack_tail(pack)]
            + [held(width, size)] * (2 * add),
            out_specs=[half, half, held(width, size), held(width, size)],
        ),
        out_shape=[jax.ShapeDtypeStruct((size, total), BF16)] * 2
        + [
            jax.ShapeDtypeStruct((width, size), F32),
            jax.ShapeDtypeStruct((width, size), BF16 if last else F32),
        ],
        cost_estimate=pl.CostEstimate(
            flops=16 * total * width * size, bytes_accessed=total * width * 4, transcendentals=0
        ),
        compiler_params=pltpu.CompilerParams(vmem_limit_bytes=24 * 2**20),
        name="out_back",
    )(place, *grads, own, away, pack, *(before if add else ()))


def before_feed_kernel(m, mods_ref, tok_ref, cot_ref, keep_ref, arr_ref, br_ref, n_ref, g_ref):
    width = keep_ref.shape[1]
    branch = keep_ref[...] + arr_ref[...].astype(F32)
    br_ref[...] = branch
    middle = tok_ref[0].astype(F32) + part_of(mods_ref, m, 2, width) * branch
    unit, _ = normalize(middle)
    n_ref[...] = (
        unit * (1.0 + part_of(mods_ref, m, 4, width)) + part_of(mods_ref, m, 3, width)
    ).astype(BF16)
    g_ref[...] = (cot_ref[0].astype(F32) * part_of(mods_ref, m, 5, width)).astype(BF16)


def after_feed_kernel(
    m, mods_ref, tok_ref, cot_ref, br_ref, b0_ref, b1_ref, d0_ref, d1_ref, *rest
):
    out_ref, d_ref, g_ref, sums_ref = rest[-4:]
    width = br_ref.shape[1]
    branch_a = br_ref[...]
    middle = tok_ref[0].astype(F32) + part_of(mods_ref, m, 2, width) * branch_a
    unit, root = normalize(middle)
    branch_m = b0_ref[...] + b1_ref[...].astype(F32)
    out_ref[0] = (middle + part_of(mods_ref, m, 5, width) * branch_m).astype(BF16)
    d_normed = d0_ref[...] + d1_ref[...].astype(F32)
    grad = cot_ref[0].astype(F32)
    d_middle = grad + normalize_back(d_normed, unit, root, part_of(mods_ref, m, 4, width))
    d_ref[...] = d_middle
    g_ref[...] = (d_middle * part_of(mods_ref, m, 2, width)).astype(BF16)

    @pl.when(pl.program_id(0) == 0)
    def _():
        sums_ref[...] = jnp.zeros_like(sums_ref)

    for k, term in enumerate((d_middle * branch_a, d_normed, d_normed * unit, grad * branch_m)):
        sums_ref[k : k + 1, :] += jnp.sum(term, axis=0, keepdims=True)


def finish_kernel(m, mods_ref, tok_ref, keep_ref, arr_ref, crossed_ref, d_ref, *rest):
    out_ref = rest[-1]
    width = d_ref.shape[1]
    unit, root = normalize(tok_ref[0].astype(F32))
    grad = keep_ref[0] + arr_ref[0].astype(F32) + crossed_ref[...].astype(F32)
    out_ref[0] = d_ref[...] + normalize_back(grad, unit, root, part_of(mods_ref, m, 1, width))


def by_rows(name, kernel, m, mods, inputs, outputs, before=None, sums=0, weight=40):
    rows, width = inputs[-1].shape
    step = min(256, rows)
    flat = pl.BlockSpec((step, width), lambda i: (i, 0))
    entry = pl.BlockSpec((1, step, width), lambda i: (m, i, 0))
    first = pl.BlockSpec((1, step, width), lambda i: (0, i, 0))
    in_specs = [pl.BlockSpec(mods.shape, lambda i: (0, 0))]
    for value, whole_set in inputs[:-1]:
        in_specs.append(flat if value.ndim == 2 else entry if whole_set else first)
    values = [value for value, _ in inputs[:-1]] + [inputs[-1]]
    in_specs.append(flat)
    extra = [] if before is None else [before]
    in_specs += [ANYWHERE] * len(extra)
    out_specs = [flat if len(shape.shape) == 2 else entry for shape in outputs]
    if sums:
        outputs = [*outputs, jax.ShapeDtypeStruct((sums, width), F32)]
        out_specs.append(pl.BlockSpec((sums, width), lambda i: (0, 0)))
    return pl.pallas_call(
        functools.partial(kernel, m),
        grid=(rows // step,),
        in_specs=in_specs,
        out_specs=out_specs,
        out_shape=outputs,
        input_output_aliases={1 + len(values): 0} if extra else {},
        cost_estimate=pl.CostEstimate(
            flops=weight * rows * width, bytes_accessed=32 * rows * width, transcendentals=rows
        ),
        compiler_params=pltpu.CompilerParams(vmem_limit_bytes=16 * 2**20),
        name=name,
    )(mods, *values, *extra)


def block_range(doc_ids, rows, columns):
    by_row = doc_ids.reshape(-1, rows)
    by_column = doc_ids.reshape(-1, columns)
    low = jnp.sum(by_column[:, -1][None, :] < by_row[:, 0][:, None], axis=1, dtype=jnp.int32)
    high = jnp.sum(by_column[:, 0][None, :] <= by_row[:, -1][:, None], axis=1, dtype=jnp.int32)
    return low, high


def turn_tables(length):
    freqs = jnp.exp(-math.log(10000.0) * jnp.arange(HALF, dtype=F32) / HALF)
    angles = freqs[:, None] * jnp.arange(length, dtype=F32)[None, :]
    return jnp.cos(angles), jnp.sin(angles)


def normalize(values):
    center = values - jnp.mean(values, axis=-1, keepdims=True)
    root = lax.rsqrt(jnp.mean(center * center, axis=-1, keepdims=True) + EPSILON)
    return center * root, root


def normalize_back(grad, unit, root, stretch):
    turned = grad * (1.0 + stretch)
    return root * (
        turned
        - jnp.mean(turned, axis=-1, keepdims=True)
        - unit * jnp.mean(turned * unit, axis=-1, keepdims=True)
    )


def per_device(tokens, segments, timesteps, cotangent, w_qkv, w_out, w_up, w_down, w_ada, b_ada):
    micro_count, rows, width = tokens.shape
    heads = HEADS // 4
    length = 4 * rows
    count = dp_bits()
    tensor = lax.axis_index("tensor")
    far, near = tensor // 2, tensor % 2
    device = lax.axis_index("dp") * 4 + tensor
    falling = list(range(count - 1, -1, -1))
    rising = list(range(count))

    fq, fk = min(512, length), min(512, length)
    rq, rk = min(512, length), min(256, length)
    doc_rows = segments.astype(F32)
    bounds = [
        (block_range(segments[m], fq, fk), block_range(segments[m], rk, rq))
        for m in range(micro_count)
    ]
    tables = turn_tables(length)
    pack = jnp.concatenate([w_up, w_down.T, w_out.T], axis=1)

    states = []

    def advance(value, step):
        while len(states) <= step:
            done = falling[: len(states)]
            states.append(
                gather_block(states[-1] if states else w_qkv, falling[len(done)], done)
            )
        return after(value, states[step])

    def with_stamps(value, bit):
        if bit == count - 1:
            return after(value, (tables, doc_rows, bounds, pack))
        return advance(value, bit - 1) if bit >= 1 else value

    ready = tokens[0]
    across = swap_far(ready)
    blocks = [(ready, swap_near(ready), across, swap_near(across))]

    feature_rows = w_ada.shape[0]
    half = feature_rows * lax.axis_size("dp") * 4 // 2
    stamps = gather_relative(timesteps[:, 0].astype(F32), with_stamps)
    index = device * feature_rows + jnp.arange(feature_rows)
    freqs = jnp.exp(-math.log(10000.0) * (index % half).astype(F32) / half)
    angles = stamps[:, :, None] * freqs
    cond = jnp.where(index < half, jnp.cos(angles), jnp.sin(angles)).astype(BF16)
    cond = cond.reshape(-1, feature_rows)
    bias_size = b_ada.shape[0]
    slots = w_ada.shape[1] // bias_size
    bias = jnp.where(
        jnp.arange(slots)[:, None] == device, b_ada.astype(F32)[None, :], 0.0
    ).reshape(-1)
    terms = mod_terms(advance(after(cond, across), count - 2), w_ada, bias)
    mods = scatter_relative(terms.reshape(-1, micro_count, terms.shape[1]))

    begun = mods
    mods = after(advance(mods, count - 1), blocks[0][3])
    wq = states[-1].reshape(width, -1)
    mods = mods + swap_far(mods)
    mods = mods + swap_near(mods)

    pack = after(pack, begun)
    groups = [
        [4 * i + 2 * j + c for i in range(lax.axis_size("dp")) for j in range(2)] for c in range(2)
    ]
    pack = lax.all_gather(pack, ("dp", "tensor"), axis_index_groups=groups)
    pack = pack.reshape((-1, 2) + pack.shape[1:])
    hid = w_up.shape[1]
    part = w_out.shape[0]
    if w_up.shape[0] % 16:
        pack = pack.transpose(1, 0, 2, 3).reshape(1, 2, width, -1)

    place = tensor.astype(jnp.int32).reshape(1)
    state = []
    for m in range(micro_count):
        if m > 0:
            own = after(tokens, mods)[m]
            across = after(swap_far(own), state[-1][3])
            blocks.append((own, swap_near(own), across, swap_near(across)))
        normed_a, qkv, att_own, att_away, lse = attend(
            m, blocks[m], mods, wq, tables, doc_rows[m : m + 1],
            bounds[m][0], place, heads, fq, fk,
        )
        state.append((normed_a, qkv, (att_own, att_away), lse))

    every = jax.ShapeDtypeStruct(tokens.shape, BF16)
    wide = jax.ShapeDtypeStruct((rows, width), F32)
    low = jax.ShapeDtypeStruct((rows, width), BF16)
    output = None
    grads_out = None
    grads_feed = None
    middles = []
    for m in range(micro_count):
        last = m + 1 == micro_count
        att_own, att_away = state[m][2]
        if m == 0:
            crossing = [swap_far(state[k][2][1]) for k in range(micro_count)]
        att_far = crossing[m]
        if not last:
            att_far = after(att_far, state[m + 1][2][0])
        keep, send = out_project(place, att_own, att_far, pack)
        branch_a, normed_m, grad_m = by_rows(
            "before_feed",
            before_feed_kernel,
            m,
            mods,
            [(tokens, True), (cotangent, True), (keep, False), swap_near(send)],
            [wide, low, low],
        )
        if m > 0:
            normed_m = after(normed_m, middles[-1][3])
        branch_own, branch_near, d_own, d_near, grads_feed = feed(
            (normed_m, swap_near(normed_m)),
            (grad_m, swap_near(grad_m)),
            pack,
            hid,
            grads_feed,
            BF16 if last else F32,
        )
        if not last:
            (branch_own, branch_near, d_own, d_near), crossing[m + 1] = lax.optimization_barrier(
                ((branch_own, branch_near, d_own, d_near), crossing[m + 1])
            )
        if m > 0:
            (branch_own, branch_near, d_own, d_near), middles[m - 1][1][1] = (
                lax.optimization_barrier(
                    ((branch_own, branch_near, d_own, d_near), middles[m - 1][1][1])
                )
            )
        output, d_middle, grad_a, sums = by_rows(
            "after_feed",
            after_feed_kernel,
            m,
            mods,
            [
                (tokens, True),
                (cotangent, True),
                (branch_a, False),
                (branch_own, False),
                (swap_near(branch_near), False),
                (d_own, False),
                swap_near(d_near),
            ],
            [every, wide, low],
            before=output,
            sums=4,
        )
        d_att_own, d_att_far, *grads_out = out_back(
            place, (grad_a, swap_near(grad_a)), att_own, att_far, pack, grads_out,
            last,
        )
        if m > 0:
            middles[m - 1][1][0] = after(middles[m - 1][1][0], d_att_far)
        middles.append([d_middle, [d_att_own, swap_far(d_att_far)], sums, d_att_far])

    feed_total = lax.psum_scatter(grads_feed, "dp", scatter_dimension=0, tiled=True)
    out_far = swap_far(grads_out[1])

    mod_grads = []
    g_qkv = None
    backs = []
    for m in range(micro_count):
        normed_a, qkv, att, lse = state[m]
        keep, send, back, sums = attend_back(
            blocks[m], qkv, att, middles[m][1], lse, tables, doc_rows[m : m + 1],
            bounds[m][1], place, wq, heads, rq, rk,
        )
        if m > 0:
            (keep, send, back, sums), (backs[m - 1][2], out_half) = lax.optimization_barrier(
                ((keep, send, back, sums), (backs[m - 1][2], out_half))
            )
        elif m == 0:
            (keep, send, back, sums), out_far = lax.optimization_barrier(
                ((keep, send, back, sums), out_far)
            )
            out_keep, out_send = halves(
                by_bits(grads_out[0] + out_far.astype(F32)), 0, falling
            )
            out_half = swap_dp(out_send, 0)
        arrived = swap_near(send)
        crossing = (keep[1] + arrived[1].astype(F32)).astype(BF16)
        crossed = swap_far(crossing)
        g_qkv = project_grad(normed_a, back, g_qkv)
        if m + 1 < micro_count:
            middles[m + 1][1][0] = after(
                middles[m + 1][1][0], (crossing, g_qkv, out_send)
            )
            middles[m + 1][1][1] = after(middles[m + 1][1][1], sums)
        backs.append([keep, arrived, crossed])
        mod_grads.append(jnp.concatenate([sums.reshape(-1), middles[m][2].reshape(-1)]))
    g_last = after(g_qkv, crossing)
    middles[0][0] = after(middles[0][0], g_last)
    d_tokens = None
    wide_set = jax.ShapeDtypeStruct(tokens.shape, F32)
    for m in range(micro_count):
        keep, arrived, crossed = backs[m]
        (d_tokens,) = by_rows(
            "finish",
            finish_kernel,
            m,
            mods,
            [(tokens, True), (keep, False), (arrived, False), (crossed, False), middles[m][0]],
            [wide_set],
            before=d_tokens,
        )
    sides = feed_total[:, : 2 * hid], feed_total[:, 2 * hid :]
    feed_far = swap_far(after(pick(far, sides[1], sides[0]), crossed))
    total = pick(far, sides[0], sides[1]).astype(F32) + feed_far.astype(F32)
    pieces = jnp.split(total, 2 * hid // CHUNK, axis=1)
    g_up = jnp.concatenate(pieces[0::2], axis=1)
    g_down = jnp.concatenate(pieces[1::2], axis=1).T
    current, sent = halves(by_bits(g_last), 0, falling)
    swapped = swap_dp(sent, 0)
    current = jnp.concatenate(
        [out_keep + out_half.astype(F32), current + swapped.astype(F32)], axis=-1
    )
    for bit in rising[1:]:
        if bit == count - 1:
            current = after(current, crossed)
        current, sent = halves(current, bit, falling[: count - bit])
        current = current + swap_dp(sent, bit).astype(F32)
    g_out = current[:, :part].T
    g_qkv = current[:, part:]

    d_mods = jnp.stack(mod_grads)
    d_mods = after(d_mods + swap_far(d_mods), g_last)
    d_mods = d_mods + swap_near(d_mods)
    all_mods = gather_relative(
        d_mods, lambda value, bit: after(value, swapped) if bit == 1 else value
    ).reshape(-1, d_mods.shape[1])
    g_ada = lax.dot_general(
        cond.astype(F32),
        all_mods,
        TN,
        precision=lax.Precision.HIGHEST,
        preferred_element_type=F32,
    )
    g_bias = lax.dynamic_slice_in_dim(jnp.sum(all_mods, axis=0), device * bias_size, bias_size)
    return (
        output,
        d_tokens,
        g_qkv,
        g_out,
        g_up,
        g_down,
        g_ada,
        g_bias,
    )


def solution(mesh):
    return jax.shard_map(
        per_device,
        mesh=mesh,
        in_specs=(
            P(None, ("dp", "tensor"), None),
            P(None, "dp"),
            P(None, "dp"),
            P(None, ("dp", "tensor"), None),
            P("dp", "tensor"),
            P("tensor", "dp"),
            P("dp", "tensor"),
            P("tensor", "dp"),
            P(("dp", "tensor"), None),
            P(("dp", "tensor")),
        ),
        out_specs=(
            P(None, ("dp", "tensor"), None),
            P(None, ("dp", "tensor"), None),
            P("dp", "tensor"),
            P("tensor", "dp"),
            P("dp", "tensor"),
            P("tensor", "dp"),
            P(("dp", "tensor"), None),
            P(("dp", "tensor")),
        ),
        check_vma=False,
    )
```

```python
import functools
import math

import jax
import jax.numpy as jnp
from jax import lax
from jax.experimental import pallas as pl
from jax.experimental.pallas import tpu as pltpu
from jax.sharding import PartitionSpec as P

HEADS = 12
HD = 64
HALF = HD // 2
EPSILON = 1e-06
MASKED = -1e30
F32 = jnp.float32
BF16 = jnp.bfloat16
NN = (((1,), (0,)), ((), ()))
NT = (((1,), (1,)), ((), ()))
TN = (((0,), (0,)), ((), ()))
TT = (((0,), (1,)), ((), ()))


def dot(left, right, dims=NN):
    return lax.dot_general(left, right, dims, preferred_element_type=F32)


def pick(bit, zero, one):
    return jnp.where(bit == 0, zero, one)


def swap_far(value):
    return lax.ppermute(value, "tensor", [(i, i ^ 2) for i in range(4)])


def swap_near(value):
    return lax.ppermute(value, "tensor", [(i, i ^ 1) for i in range(4)])


def swap_dp(value, bit):
    count = lax.axis_size("dp")
    return lax.ppermute(value, "dp", [(i, i ^ (1 << bit)) for i in range(count)])


def after(value, other):
    return lax.optimization_barrier((value, other))[0]


def dp_bits():
    return lax.axis_size("dp").bit_length() - 1


def my_bit(bit):
    return (lax.axis_index("dp") >> bit) & 1


def gather_block(current, bit, done, arrival=lambda value: value):
    arrived = arrival(swap_dp(current, bit))
    place = sum(1 for other in done if other > bit)
    mine = my_bit(bit)
    return jnp.stack([pick(mine, current, arrived), pick(mine, arrived, current)], axis=place)


def halves(current, bit, left):
    place = left.index(bit)
    first = lax.index_in_dim(current, 0, place, keepdims=False)
    second = lax.index_in_dim(current, 1, place, keepdims=False)
    mine = my_bit(bit)
    return pick(mine, first, second), pick(mine, second, first).astype(BF16)


def by_bits(total):
    return total.reshape((2,) * dp_bits() + (-1, total.shape[-1]))


def gather_relative(value, first=lambda value, bit: value):
    current = value
    for bit in range(dp_bits()):
        current = first(current, bit)
        current = jnp.stack([current, swap_dp(current, bit)])
    return current.reshape((-1,) + value.shape)


def scatter_relative(terms, first=lambda value, bit: value):
    count = dp_bits()
    current = terms.reshape((2,) * count + terms.shape[1:])
    for bit in range(count):
        current = first(current, bit)
        place = count - 1 - bit
        kept = lax.index_in_dim(current, 0, place, keepdims=False)
        sent = lax.index_in_dim(current, 1, place, keepdims=False)
        current = kept + swap_dp(sent, bit)
    return current


def document_columns(row_ref, col_s):
    for start in range(0, row_ref.shape[1], 128):
        tile = jnp.broadcast_to(row_ref[0:1, start : start + 128], (128, 128))
        col_s[start : start + 128, :] = tile.T


def token_copies(refs, place, tok_s, sems):
    rows = tok_s.shape[0] // 4
    return [
        pltpu.make_async_copy(
            ref,
            tok_s.at[pl.ds(pl.multiple_of(jnp.bitwise_xor(place, r) * rows, rows), rows), :],
            sems.at[r],
        )
        for r, ref in enumerate(refs)
    ]


def same_documents(row_ref, col_s, rows, columns, size):
    return jnp.concatenate([col_s[rows, :]] * (size // 128), axis=1) == row_ref[0:1, columns]


def attend_kernel(
    m, bq, bk, heads, lo_ref, hi_ref, place_ref, t0, t1, t2, t3, mods_ref, wq_ref, cs_ref, sn_ref,
    row_ref, normed_hbm, qkv_ref, own_ref, far_ref, lse_ref,
    tok_s, normed_s, wq_s, key_s, acc_s, att_s, col_s, sem, token_sems,
):
    length, width = tok_s.shape
    rows = length // 4
    place = place_ref[0]
    copies = token_copies((t0, t1, t2, t3), place, tok_s, token_sems)
    for copy in copies:
        copy.start()
    wq_s[...] = wq_ref[...].T
    document_columns(row_ref, col_s)
    for copy in copies:
        copy.wait()
    shift = mods_ref[m : m + 1, 0:width]
    stretch = 1.0 + mods_ref[m : m + 1, width : 2 * width]
    step = min(256, rows)

    def project(i, _):
        piece = pl.ds(pl.multiple_of(i * step, step), step)
        unit, _ = normalize(tok_s[piece, :].astype(F32))
        normed = (unit * stretch + shift).astype(BF16)
        normed_s[piece, :] = normed
        packed = dot(wq_s[...], normed, NT)
        cosine = cs_ref[:, piece]
        sine = sn_ref[:, piece]
        for h in range(heads):
            base = 3 * HD * h

            def turned(row):
                a = packed[row : row + HALF]
                b = packed[row + HALF : row + HD]
                return jnp.concatenate([a * cosine - b * sine, a * sine + b * cosine], axis=0)

            qkv_ref[base : base + HD, piece] = turned(base).astype(BF16)
            keys = turned(base + HD)
            qkv_ref[base + HD : base + 2 * HD, piece] = keys.astype(BF16)
            key_s[h, piece, :] = keys.T.astype(BF16)
            qkv_ref[base + 2 * HD : base + 3 * HD, piece] = packed[
                base + 2 * HD : base + 3 * HD
            ].astype(BF16)
        return 0

    lax.fori_loop(0, length // step, project, 0)
    copy = pltpu.make_async_copy(normed_s, normed_hbm, sem)
    copy.start()

    def query_block(i, _):
        columns = pl.ds(pl.multiple_of(i * bq, bq), bq)
        queries = [
            qkv_ref[3 * HD * h : 3 * HD * h + HD, columns] * jnp.asarray(0.125, BF16)
            for h in range(heads)
        ]
        acc_s[...] = jnp.zeros_like(acc_s)

        def key_block(j, carry):
            keys = pl.ds(pl.multiple_of(j * bk, bk), bk)
            allowed = same_documents(row_ref, col_s, keys, columns, bq)
            scores = [dot(key_s[h, keys, :], queries[h]) for h in range(heads)]
            result, fades, lows = [], [], []
            for h in range(heads):
                top, total = carry[2 * h], carry[2 * h + 1]
                masked = jnp.where(allowed, scores[h], MASKED)
                new_top = jnp.maximum(top, jnp.max(masked, axis=0, keepdims=True))
                fade = jnp.exp(top - new_top)
                chances = jnp.exp(masked - new_top)
                total = fade * total + jnp.sum(chances, axis=0, keepdims=True)
                lows.append(chances.astype(BF16))
                fades.append(fade)
                result += [new_top, total]
            for h in range(heads):
                values = qkv_ref[3 * HD * h + 2 * HD : 3 * HD * h + 3 * HD, keys]
                acc_s[h] = acc_s[h] * fades[h] + dot(values, lows[h])
            return tuple(result)

        start = (jnp.full((1, bq), MASKED, F32), jnp.zeros((1, bq), F32)) * heads
        carry = lax.fori_loop(lo_ref[i], hi_ref[i], key_block, start)
        for h in range(heads):
            top, total = carry[2 * h], carry[2 * h + 1]
            att_s[HD * h : HD * h + HD, columns] = (acc_s[h] / total).astype(BF16)
            lse_ref[h, 0:1, columns] = top + jnp.log(total)
        return 0

    lax.fori_loop(0, length // bq, query_block, 0)
    half = length // 2
    mine = pl.multiple_of(place // 2 * half, half)
    away = pl.multiple_of(half - mine, half)
    own_ref[...] = att_s[:, pl.ds(mine, half)]
    far_ref[...] = att_s[:, pl.ds(away, half)]
    copy.wait()


def attend_back_kernel(
    bq, bk, heads, lo_ref, hi_ref, place_ref, qkv_ref, own_ref, far_ref, d_own_ref, d_far_ref,
    lse_ref, cs_ref, sn_ref, row_ref, wq_hbm, t0, t1, t2, t3,
    keep_ref, send_ref, back_s, sums_ref, q_s, k_s, v_s, g_s, dat_s, dq_s, dk_s, dv_s, inner_s,
    col_s, wq_s, tok_s, sems, token_sems,
):
    place = place_ref[0]
    copies = [
        pltpu.make_async_copy(wq_hbm, wq_s, sems),
        *token_copies((t0, t1, t2, t3), place, tok_s, token_sems),
    ]
    for copy in copies:
        copy.start()
    length = qkv_ref.shape[1]
    half = length // 2
    rows = length // 4
    document_columns(row_ref, col_s)
    mine = pl.multiple_of(place // 2 * half, half)
    away = pl.multiple_of(half - mine, half)
    for start, att_ref, d_ref in ((mine, own_ref, d_own_ref), (away, far_ref, d_far_ref)):
        piece = pl.ds(start, half)
        dat_s[:, piece] = d_ref[...]
        for h in range(heads):
            head = slice(HD * h, HD * h + HD)
            inner_s[h, 0:1, piece] = jnp.sum(
                att_ref[head, :].astype(F32) * d_ref[head, :].astype(F32), axis=0, keepdims=True
            )
            g_s[h, piece, :] = d_ref[head, :].T
    for h in range(heads):
        base = 3 * HD * h
        q_s[h] = qkv_ref[base : base + HD, :].T
        k_s[h] = qkv_ref[base + HD : base + 2 * HD, :].T
        v_s[h] = qkv_ref[base + 2 * HD : base + 3 * HD, :].T
    dq_s[...] = jnp.zeros_like(dq_s)

    def key_block(j, _):
        keys = pl.ds(pl.multiple_of(j * bk, bk), bk)
        dk_s[:, keys, :] = jnp.zeros((heads, bk, HD), F32)
        dv_s[:, keys, :] = jnp.zeros((heads, bk, HD), F32)

        def query_block(i, _):
            columns = pl.ds(pl.multiple_of(i * bq, bq), bq)
            allowed = same_documents(row_ref, col_s, keys, columns, bq)
            for h in range(heads):
                base = 3 * HD * h
                head = slice(HD * h, HD * h + HD)
                scores = dot(
                    k_s[h, keys, :] * jnp.asarray(0.125, BF16), qkv_ref[base : base + HD, columns]
                )
                chances = jnp.where(
                    allowed, jnp.exp(scores - lse_ref[h, 0:1, columns]), 0.0
                )
                d_chances = dot(v_s[h, keys, :], dat_s[head, columns])
                d_scores = (chances * (d_chances - inner_s[h, 0:1, columns])).astype(BF16)
                dv_s[h, keys, :] += dot(chances.astype(BF16), g_s[h, columns, :])
                dk_s[h, keys, :] += dot(d_scores, q_s[h, columns, :])
                dq_s[head, columns] += dot(qkv_ref[base + HD : base + 2 * HD, keys], d_scores)
            return 0

        lax.fori_loop(lo_ref[j], hi_ref[j], query_block, 0)
        return 0

    lax.fori_loop(0, length // bk, key_block, 0)
    for copy in copies:
        copy.wait()
    step = min(256, rows)

    sums_ref[...] = jnp.zeros_like(sums_ref)
    for r, (ref, entry) in enumerate(
        ((keep_ref, 0), (send_ref, 0), (keep_ref, 1), (send_ref, 1))
    ):

        def finish(i, _):
            start = jnp.bitwise_xor(place, r) * rows + i * step
            piece = pl.ds(pl.multiple_of(start, step), step)
            cosine = cs_ref[:, piece] * 0.125
            sine = sn_ref[:, piece] * 0.125

            def turned_back(row, value):
                a = value[0:HALF, :]
                b = value[HALF:HD, :]
                back_s[row : row + HALF, piece] = (a * cosine + b * sine).astype(BF16)
                back_s[row + HALF : row + HD, piece] = (b * cosine - a * sine).astype(BF16)

            for h in range(heads):
                base = 3 * HD * h
                turned_back(base, dq_s[HD * h : HD * h + HD, piece])
                turned_back(base + HD, dk_s[h, piece, :].T)
                back_s[base + 2 * HD : base + 3 * HD, piece] = dv_s[h, piece, :].T.astype(BF16)
            part = dot(back_s[:, piece].T, wq_s[...], NT)
            unit, _ = normalize(tok_s[piece, :].astype(F32))
            sums_ref[0:1, :] += jnp.sum(part, axis=0, keepdims=True)
            sums_ref[1:2, :] += jnp.sum(part * unit, axis=0, keepdims=True)
            ref[entry, pl.ds(pl.multiple_of(i * step, step), step), :] = part.astype(ref.dtype)
            return 0

        lax.fori_loop(0, rows // step, finish, 0)

def project_grad_kernel(add, normed_ref, back_ref, *rest):
    if add:
        before_ref, *rest = rest
    out_ref, total_s = rest
    step = pl.program_id(0)

    @pl.when(step == 0)
    def _():
        total_s[...] = jnp.zeros_like(total_s)

    total_s[...] += dot(back_ref[...], normed_ref[...])

    @pl.when(step == pl.num_programs(0) - 1)
    def _():
        total = total_s[...].T
        out_ref[...] = total + before_ref[...] if add else total


def project_grad(normed, back, before):
    length, width = normed.shape
    size = back.shape[0]
    add = before is not None
    step = length // 4
    block = pl.BlockSpec((width, size), lambda i: (0, 0))
    return pl.pallas_call(
        functools.partial(project_grad_kernel, add),
        grid=(4,),
        in_specs=[
            pl.BlockSpec((step, width), lambda i: (i, 0)),
            pl.BlockSpec((size, step), lambda i: (0, i)),
        ]
        + [block] * add,
        out_specs=block,
        out_shape=jax.ShapeDtypeStruct((width, size), F32),
        scratch_shapes=[pltpu.VMEM((size, width), F32)],
        cost_estimate=pl.CostEstimate(
            flops=40 * length * width * size, bytes_accessed=length * width * 4, transcendentals=0
        ),
        name="project_grad",
    )(normed, back, *[before] * add)


def held(*shape):
    return pl.BlockSpec(shape, lambda i, *_: (0,) * len(shape), pipeline_mode=pl.Buffered(1))


ANYWHERE = pl.BlockSpec(memory_space=pl.ANY)


def attend(m, blocks, mods, wq, tables, doc_row, bounds, place, heads, bq, bk):
    rows, width = blocks[0].shape
    length = 4 * rows
    size = 3 * HD * heads
    return pl.pallas_call(
        functools.partial(attend_kernel, m, bq, bk, heads),
        grid_spec=pltpu.PrefetchScalarGridSpec(
            num_scalar_prefetch=3,
            grid=(1,),
            in_specs=[ANYWHERE] * 4
            + [
                held(*mods.shape),
                held(width, size),
                held(HALF, length),
                held(HALF, length),
                held(1, length),
            ],
            out_specs=[
                ANYWHERE,
                held(size, length),
                held(HD * heads, length // 2),
                held(HD * heads, length // 2),
                held(heads, 1, length),
            ],
            scratch_shapes=[
                pltpu.VMEM((length, width), BF16),
                pltpu.VMEM((length, width), BF16),
                pltpu.VMEM((size, width), BF16),
                pltpu.VMEM((heads, length, HD), BF16),
                pltpu.VMEM((heads, HD, bq), F32),
                pltpu.VMEM((HD * heads, length), BF16),
                pltpu.VMEM((length, 128), F32),
                pltpu.SemaphoreType.DMA(()),
                pltpu.SemaphoreType.DMA((4,)),
            ],
        ),
        out_shape=[
            jax.ShapeDtypeStruct((length, width), BF16),
            jax.ShapeDtypeStruct((size, length), BF16),
            jax.ShapeDtypeStruct((HD * heads, length // 2), BF16),
            jax.ShapeDtypeStruct((HD * heads, length // 2), BF16),
            jax.ShapeDtypeStruct((heads, 1, length), F32),
        ],
        cost_estimate=pl.CostEstimate(
            flops=heads * length * length * 2400,
            bytes_accessed=length * width * 8,
            transcendentals=heads * length * length // 2,
        ),
        compiler_params=pltpu.CompilerParams(vmem_limit_bytes=46 * 2**20),
        name="attend",
    )(*bounds, place, *blocks, mods, wq, *tables, doc_row)


def attend_back(
    blocks, qkv, att, d_att, lse, tables, doc_row, bounds, place, wq, heads, bq, bk
):
    size, length = qkv.shape
    width = wq.shape[0]
    rows = length // 4
    half = held(HD * heads, length // 2)
    return pl.pallas_call(
        functools.partial(attend_back_kernel, bq, bk, heads),
        grid_spec=pltpu.PrefetchScalarGridSpec(
            num_scalar_prefetch=3,
            grid=(1,),
            in_specs=[
                held(size, length),
                half,
                half,
                half,
                half,
                held(heads, 1, length),
                held(HALF, length),
                held(HALF, length),
                held(1, length),
            ]
            + [ANYWHERE] * 5,
            out_specs=[
                held(2, rows, width),
                held(2, rows, width),
                held(size, length),
                held(2, width),
            ],
            scratch_shapes=[pltpu.VMEM((heads, length, HD), BF16)] * 4
            + [
                pltpu.VMEM((heads * HD, length), BF16),
                pltpu.VMEM((heads * HD, length), F32),
                pltpu.VMEM((heads, length, HD), F32),
                pltpu.VMEM((heads, length, HD), F32),
                pltpu.VMEM((heads, 8, length), F32),
                pltpu.VMEM((length, 128), F32),
                pltpu.VMEM((width, size), BF16),
                pltpu.VMEM((length, width), BF16),
                pltpu.SemaphoreType.DMA(()),
                pltpu.SemaphoreType.DMA((4,)),
            ],
        ),
        out_shape=[
            jax.ShapeDtypeStruct((2, rows, width), F32),
            jax.ShapeDtypeStruct((2, rows, width), BF16),
            jax.ShapeDtypeStruct((size, length), BF16),
            jax.ShapeDtypeStruct((2, width), F32),
        ],
        cost_estimate=pl.CostEstimate(
            flops=heads * length * length * 3600,
            bytes_accessed=length * width * 8,
            transcendentals=heads * length * length // 2,
        ),
        compiler_params=pltpu.CompilerParams(vmem_limit_bytes=50 * 2**20),
        name="attend_back",
    )(*bounds, place, qkv, *att, *d_att, lse, *tables, doc_row, wq, *blocks)


def gelu_pair(values):
    square = values * values
    bend = jnp.tanh(0.7978845608028654 * (values + 0.044715 * (square * values)))
    slope = 0.7978845608028654 * (1.0 + 3 * 0.044715 * square)
    hidden = 0.5 * values * (1.0 + bend)
    return hidden, 0.5 * (1.0 + bend) + 0.5 * values * (1.0 - bend * bend) * slope


def feed_kernel(parts, add, n0, n1, g0, g1, up_ref, down_ref, *rest):
    if add:
        before_ref, *rest = rest
    b0, b1, d0, d1, g_ref, n_s, g_s, n_t, g_t, hidden_s, pre_s, b1_s, d1_s = rest
    rows = n0.shape[0]
    up = up_ref[...].reshape(-1, up_ref.shape[-1])
    down = down_ref[...].reshape(-1, down_ref.shape[-1])

    @pl.when(pl.program_id(0) == 0)
    def _():
        for piece, n, g in ((slice(0, rows), n0, g0), (slice(rows, 2 * rows), n1, g1)):
            n_s[piece, :] = n[...]
            g_s[piece, :] = g[...]
            n_t[:, piece] = n[...].T
            g_t[:, piece] = g[...].T
        for ref in (b0, b1_s, d0, d1_s):
            ref[...] = jnp.zeros_like(ref)

    step = 2 * rows // parts
    for p in range(parts):
        piece = slice(p * step, (p + 1) * step)
        hidden, slope = gelu_pair(dot(n_s[piece, :], up))
        hidden_s[piece, :] = hidden.astype(BF16)
        pre_s[piece, :] = (dot(g_s[piece, :], down) * slope).astype(BF16)
    for first, b_ref, d_ref in ((0, b0, d0), (rows, b1_s, d1_s)):
        for start in range(0, rows, step):
            piece = slice(first + start, first + start + step)
            b_ref[start : start + step, :] += dot(hidden_s[piece, :], down, NT)
            d_ref[start : start + step, :] += dot(pre_s[piece, :], up, NT)
    chunk = up.shape[1]
    for start, left, right in ((0, n_t, pre_s), (chunk, g_t, hidden_s)):
        columns = slice(start, start + chunk)
        grad = dot(left[...], right[...])
        if add:
            grad = grad + before_ref[:, columns]
        g_ref[:, columns] = grad.astype(g_ref.dtype)

    @pl.when(pl.program_id(0) == pl.num_programs(0) - 1)
    def _():
        b1[...] = b1_s[...].astype(BF16)
        d1[...] = d1_s[...].astype(BF16)


CHUNK = 256


def feed(normed, grads, pack, hid, before, kind):
    rows, width = normed[0].shape
    count, _, height, _ = pack.shape
    chunk = CHUNK
    steps = hid // chunk
    add = before is not None

    def weight(first):
        return pl.BlockSpec(
            (count, 1, height, chunk), lambda i: (0, i // steps, 0, first * steps + i % steps)
        )

    block = pl.BlockSpec((rows, width), lambda i: (0, 0))
    columns = pl.BlockSpec((width, 2 * chunk), lambda i: (0, i))
    total = 2 * rows
    return pl.pallas_call(
        functools.partial(feed_kernel, 4, add),
        grid=(2 * steps,),
        in_specs=[block] * 4 + [weight(0), weight(1)] + [columns] * add,
        out_specs=[block] * 4 + [columns],
        out_shape=[jax.ShapeDtypeStruct((rows, width), kind) for kind in (F32, BF16, F32, BF16)]
        + [jax.ShapeDtypeStruct((width, 4 * hid), kind)],
        scratch_shapes=[pltpu.VMEM((total, width), BF16)] * 2
        + [pltpu.VMEM((width, total), BF16)] * 2
        + [pltpu.VMEM((total, chunk), BF16)] * 2
        + [pltpu.VMEM((rows, width), F32)] * 2,
        cost_estimate=pl.CostEstimate(
            flops=24 * total * width * hid,
            bytes_accessed=8 * width * hid + 12 * total * width,
            transcendentals=2 * total * hid,
        ),
        compiler_params=pltpu.CompilerParams(vmem_limit_bytes=46 * 2**20),
        name="feed",
    )(*normed, *grads, pack, pack, *[before] * add)


def terms_kernel(cond_ref, w_ref, bias_ref, out_ref):
    total = bias_ref[...] + jnp.zeros_like(out_ref)
    for r in range(w_ref.shape[0]):
        total = total + cond_ref[:, r : r + 1] * w_ref[r : r + 1, :].astype(F32)
    out_ref[...] = total


def mod_terms(cond, w_ada, bias):
    return pl.pallas_call(
        terms_kernel,
        out_shape=jax.ShapeDtypeStruct((cond.shape[0], w_ada.shape[1]), F32),
        cost_estimate=pl.CostEstimate(
            flops=2 * cond.size * w_ada.shape[1],
            bytes_accessed=4 * cond.shape[0] * w_ada.shape[1],
            transcendentals=0,
        ),
        name="mod_terms",
    )(cond.astype(F32), w_ada, bias[None, :])


def part_of(mods_ref, m, k, width):
    return mods_ref[m : m + 1, k * width : (k + 1) * width]


def out_weights(pack_ref, side, size):
    return pack_ref[:, pl.ds(side, 1), :, :].reshape(-1, size)


def out_kernel(place_ref, own_ref, far_ref, pack_ref, keep_ref, send_ref):
    size, total = own_ref.shape
    rows = total // 2
    side, near = place_ref[0] // 2, place_ref[0] % 2
    own_w = out_weights(pack_ref, side, size)
    far_w = out_weights(pack_ref, 1 - side, size)
    for ref, half in ((keep_ref, near), (send_ref, 1 - near)):
        piece = pl.ds(pl.multiple_of(half * rows, rows), rows)
        ref[...] = (
            dot(own_ref[:, piece].T, own_w, NT) + dot(far_ref[:, piece].T, far_w, NT)
        ).astype(ref.dtype)


def out_project(place, own, away, pack):
    size, total = own.shape
    rows, width = total // 2, pack.shape[0] * pack.shape[2]
    return pl.pallas_call(
        out_kernel,
        grid_spec=pltpu.PrefetchScalarGridSpec(
            num_scalar_prefetch=1,
            grid=(1,),
            in_specs=[held(size, total), held(size, total), held(*pack.shape)],
            out_specs=[held(rows, width), held(rows, width)],
        ),
        out_shape=[
            jax.ShapeDtypeStruct((rows, width), F32),
            jax.ShapeDtypeStruct((rows, width), BF16),
        ],
        cost_estimate=pl.CostEstimate(
            flops=8 * total * width * size, bytes_accessed=total * width * 4, transcendentals=0
        ),
        compiler_params=pltpu.CompilerParams(vmem_limit_bytes=20 * 2**20),
        name="out_project",
    )(place, own, away, pack)


def out_back_kernel(add, place_ref, g0_ref, g1_ref, own_ref, far_ref, pack_ref, *rest):
    if add:
        *before_refs, = rest[:2]
        rest = rest[2:]
    d_own_ref, d_far_ref, *grad_refs = rest
    size, total = own_ref.shape
    rows = total // 2
    side, near = place_ref[0] // 2, place_ref[0] % 2
    pieces = [
        pl.ds(pl.multiple_of(half * rows, rows), rows) for half in (near, 1 - near)
    ]
    grads = [g0_ref[...], g1_ref[...]]
    turned = [grad.T for grad in grads]
    for k, (att_ref, d_ref, which) in enumerate(
        ((own_ref, d_own_ref, side), (far_ref, d_far_ref, 1 - side))
    ):
        weights = out_weights(pack_ref, which, size).T
        total_grad = 0.0
        for grad, flipped, piece in zip(grads, turned, pieces):
            d_ref[:, piece] = dot(weights, grad, NT).astype(BF16)
            total_grad = total_grad + dot(flipped, att_ref[:, piece], NT)
        if add:
            total_grad = total_grad + before_refs[k][...]
        grad_refs[k][...] = total_grad.astype(grad_refs[k].dtype)


def out_back(place, grads, own, away, pack, before, last):
    size, total = own.shape
    rows, width = grads[0].shape
    add = before is not None
    half = held(size, total)
    return pl.pallas_call(
        functools.partial(out_back_kernel, add),
        grid_spec=pltpu.PrefetchScalarGridSpec(
            num_scalar_prefetch=1,
            grid=(1,),
            in_specs=[held(rows, width)] * 2
            + [half, half, held(*pack.shape)]
            + [held(width, size)] * (2 * add),
            out_specs=[half, half, held(width, size), held(width, size)],
        ),
        out_shape=[jax.ShapeDtypeStruct((size, total), BF16)] * 2
        + [
            jax.ShapeDtypeStruct((width, size), F32),
            jax.ShapeDtypeStruct((width, size), BF16 if last else F32),
        ],
        cost_estimate=pl.CostEstimate(
            flops=16 * total * width * size, bytes_accessed=total * width * 4, transcendentals=0
        ),
        compiler_params=pltpu.CompilerParams(vmem_limit_bytes=24 * 2**20),
        name="out_back",
    )(place, *grads, own, away, pack, *(before if add else ()))


def before_feed_kernel(m, mods_ref, tok_ref, cot_ref, keep_ref, arr_ref, br_ref, n_ref, g_ref):
    width = keep_ref.shape[1]
    branch = keep_ref[...] + arr_ref[...].astype(F32)
    br_ref[...] = branch
    middle = tok_ref[0].astype(F32) + part_of(mods_ref, m, 2, width) * branch
    unit, _ = normalize(middle)
    n_ref[...] = (
        unit * (1.0 + part_of(mods_ref, m, 4, width)) + part_of(mods_ref, m, 3, width)
    ).astype(BF16)
    g_ref[...] = (cot_ref[0].astype(F32) * part_of(mods_ref, m, 5, width)).astype(BF16)


def after_feed_kernel(
    m, mods_ref, tok_ref, cot_ref, br_ref, b0_ref, b1_ref, d0_ref, d1_ref, *rest
):
    out_ref, d_ref, g_ref, sums_ref = rest[-4:]
    width = br_ref.shape[1]
    branch_a = br_ref[...]
    middle = tok_ref[0].astype(F32) + part_of(mods_ref, m, 2, width) * branch_a
    unit, root = normalize(middle)
    branch_m = b0_ref[...] + b1_ref[...].astype(F32)
    out_ref[0] = (middle + part_of(mods_ref, m, 5, width) * branch_m).astype(BF16)
    d_normed = d0_ref[...] + d1_ref[...].astype(F32)
    grad = cot_ref[0].astype(F32)
    d_middle = grad + normalize_back(d_normed, unit, root, part_of(mods_ref, m, 4, width))
    d_ref[...] = d_middle
    g_ref[...] = (d_middle * part_of(mods_ref, m, 2, width)).astype(BF16)

    @pl.when(pl.program_id(0) == 0)
    def _():
        sums_ref[...] = jnp.zeros_like(sums_ref)

    for k, term in enumerate((d_middle * branch_a, d_normed, d_normed * unit, grad * branch_m)):
        sums_ref[k : k + 1, :] += jnp.sum(term, axis=0, keepdims=True)


def finish_kernel(m, mods_ref, tok_ref, keep_ref, arr_ref, crossed_ref, d_ref, *rest):
    out_ref = rest[-1]
    width = d_ref.shape[1]
    unit, root = normalize(tok_ref[0].astype(F32))
    grad = keep_ref[0] + arr_ref[0].astype(F32) + crossed_ref[...].astype(F32)
    out_ref[0] = d_ref[...] + normalize_back(grad, unit, root, part_of(mods_ref, m, 1, width))


def by_rows(name, kernel, m, mods, inputs, outputs, before=None, sums=0, weight=40):
    rows, width = inputs[-1].shape
    step = min(256, rows)
    flat = pl.BlockSpec((step, width), lambda i: (i, 0))
    entry = pl.BlockSpec((1, step, width), lambda i: (m, i, 0))
    first = pl.BlockSpec((1, step, width), lambda i: (0, i, 0))
    in_specs = [pl.BlockSpec(mods.shape, lambda i: (0, 0))]
    for value, whole_set in inputs[:-1]:
        in_specs.append(flat if value.ndim == 2 else entry if whole_set else first)
    values = [value for value, _ in inputs[:-1]] + [inputs[-1]]
    in_specs.append(flat)
    extra = [] if before is None else [before]
    in_specs += [ANYWHERE] * len(extra)
    out_specs = [flat if len(shape.shape) == 2 else entry for shape in outputs]
    if sums:
        outputs = [*outputs, jax.ShapeDtypeStruct((sums, width), F32)]
        out_specs.append(pl.BlockSpec((sums, width), lambda i: (0, 0)))
    return pl.pallas_call(
        functools.partial(kernel, m),
        grid=(rows // step,),
        in_specs=in_specs,
        out_specs=out_specs,
        out_shape=outputs,
        input_output_aliases={1 + len(values): 0} if extra else {},
        cost_estimate=pl.CostEstimate(
            flops=weight * rows * width, bytes_accessed=32 * rows * width, transcendentals=rows
        ),
        compiler_params=None
        if name == "finish"
        else pltpu.CompilerParams(vmem_limit_bytes=16 * 2**20),
        name=name,
    )(mods, *values, *extra)


def block_range(doc_ids, rows, columns):
    by_row = doc_ids.reshape(-1, rows)
    by_column = doc_ids.reshape(-1, columns)
    low = jnp.sum(by_column[:, -1][None, :] < by_row[:, 0][:, None], axis=1, dtype=jnp.int32)
    high = jnp.sum(by_column[:, 0][None, :] <= by_row[:, -1][:, None], axis=1, dtype=jnp.int32)
    return low, high


def turn_tables(length):
    freqs = jnp.exp(-math.log(10000.0) * jnp.arange(HALF, dtype=F32) / HALF)
    angles = freqs[:, None] * jnp.arange(length, dtype=F32)[None, :]
    return jnp.cos(angles), jnp.sin(angles)


def normalize(values):
    center = values - jnp.mean(values, axis=-1, keepdims=True)
    root = lax.rsqrt(jnp.mean(center * center, axis=-1, keepdims=True) + EPSILON)
    return center * root, root


def normalize_back(grad, unit, root, stretch):
    turned = grad * (1.0 + stretch)
    return root * (
        turned
        - jnp.mean(turned, axis=-1, keepdims=True)
        - unit * jnp.mean(turned * unit, axis=-1, keepdims=True)
    )


def per_device(tokens, segments, timesteps, cotangent, w_qkv, w_out, w_up, w_down, w_ada, b_ada):
    micro_count, rows, width = tokens.shape
    heads = HEADS // 4
    length = 4 * rows
    count = dp_bits()
    tensor = lax.axis_index("tensor")
    far, near = tensor // 2, tensor % 2
    device = lax.axis_index("dp") * 4 + tensor
    falling = list(range(count - 1, -1, -1))
    rising = list(range(count))

    fq, fk = min(512, length), min(512, length)
    rq, rk = min(512, length), min(256, length)
    doc_rows = segments.astype(F32)
    bounds = [
        (block_range(segments[m], fq, fk), block_range(segments[m], rk, rq))
        for m in range(micro_count)
    ]
    tables = turn_tables(length)
    pack = jnp.concatenate([w_up, w_down.T, w_out.T], axis=1)

    states = []

    def advance(value, step):
        while len(states) <= step:
            done = falling[: len(states)]
            states.append(
                gather_block(states[-1] if states else w_qkv, falling[len(done)], done)
            )
        return after(value, states[step])

    def with_stamps(value, bit):
        return advance(value, bit - 1) if bit >= 1 else value

    begun = []

    def with_terms(value, bit):
        if bit == 0:
            begun.append(value)
        return value

    ready = tokens[0]
    across = swap_far(ready)
    blocks = [(ready, swap_near(ready), across, swap_near(across))]

    feature_rows = w_ada.shape[0]
    half = feature_rows * lax.axis_size("dp") * 4 // 2
    stamps = gather_relative(timesteps[:, 0].astype(F32), with_stamps)
    index = device * feature_rows + jnp.arange(feature_rows)
    freqs = jnp.exp(-math.log(10000.0) * (index % half).astype(F32) / half)
    angles = stamps[:, :, None] * freqs
    cond = jnp.where(index < half, jnp.cos(angles), jnp.sin(angles)).astype(BF16)
    cond = cond.reshape(-1, feature_rows)
    bias_size = b_ada.shape[0]
    slots = w_ada.shape[1] // bias_size
    bias = jnp.where(
        jnp.arange(slots)[:, None] == device, b_ada.astype(F32)[None, :], 0.0
    ).reshape(-1)
    terms = mod_terms(advance(after(cond, across), count - 2), w_ada, bias)
    mods = scatter_relative(terms.reshape(-1, micro_count, terms.shape[1]), with_terms)

    mods = after(advance(mods, count - 1), (blocks[0][3], tables, doc_rows, bounds))
    wq = states[-1].reshape(width, -1)
    mods = mods + swap_far(mods)
    mods = mods + swap_near(mods)

    pack = after(pack, begun[0])
    groups = [
        [4 * i + 2 * j + c for i in range(lax.axis_size("dp")) for j in range(2)] for c in range(2)
    ]
    pack = lax.all_gather(pack, ("dp", "tensor"), axis_index_groups=groups)
    pack = pack.reshape((-1, 2) + pack.shape[1:])
    hid = w_up.shape[1]
    part = w_out.shape[0]
    if w_up.shape[0] % 16:
        pack = pack.transpose(1, 0, 2, 3).reshape(1, 2, width, -1)

    place = tensor.astype(jnp.int32).reshape(1)
    state = []
    for m in range(micro_count):
        if m > 0:
            own = after(tokens, mods)[m]
            across = after(swap_far(own), state[-1][3])
            blocks.append((own, swap_near(own), across, swap_near(across)))
        normed_a, qkv, att_own, att_away, lse = attend(
            m, blocks[m], mods, wq, tables, doc_rows[m : m + 1],
            bounds[m][0], place, heads, fq, fk,
        )
        state.append((normed_a, qkv, (att_own, att_away), lse))

    out_pack = pack[..., 2 * hid :]
    every = jax.ShapeDtypeStruct(tokens.shape, BF16)
    wide = jax.ShapeDtypeStruct((rows, width), F32)
    low = jax.ShapeDtypeStruct((rows, width), BF16)
    output = None
    grads_out = None
    grads_feed = None
    middles = []
    for m in range(micro_count):
        last = m + 1 == micro_count
        att_own, att_away = state[m][2]
        if m == 0:
            crossing = [swap_far(state[k][2][1]) for k in range(micro_count)]
        att_far = crossing[m]
        if not last:
            att_far = after(att_far, state[m + 1][2][0])
        keep, send = out_project(place, att_own, att_far, out_pack)
        branch_a, normed_m, grad_m = by_rows(
            "before_feed",
            before_feed_kernel,
            m,
            mods,
            [(tokens, True), (cotangent, True), (keep, False), swap_near(send)],
            [wide, low, low],
        )
        if m > 0:
            normed_m = after(normed_m, middles[-1][3])
        branch_own, branch_near, d_own, d_near, grads_feed = feed(
            (normed_m, swap_near(normed_m)),
            (grad_m, swap_near(grad_m)),
            pack,
            hid,
            grads_feed,
            BF16 if last else F32,
        )
        if not last:
            (branch_own, branch_near, d_own, d_near), crossing[m + 1] = lax.optimization_barrier(
                ((branch_own, branch_near, d_own, d_near), crossing[m + 1])
            )
        if m > 0:
            (branch_own, branch_near, d_own, d_near), middles[m - 1][1][1] = (
                lax.optimization_barrier(
                    ((branch_own, branch_near, d_own, d_near), middles[m - 1][1][1])
                )
            )
        output, d_middle, grad_a, sums = by_rows(
            "after_feed",
            after_feed_kernel,
            m,
            mods,
            [
                (tokens, True),
                (cotangent, True),
                (branch_a, False),
                (branch_own, False),
                (swap_near(branch_near), False),
                (d_own, False),
                swap_near(d_near),
            ],
            [every, wide, low],
            before=output,
            sums=4,
        )
        d_att_own, d_att_far, *grads_out = out_back(
            place, (grad_a, swap_near(grad_a)), att_own, att_far, out_pack, grads_out,
            last,
        )
        if m > 0:
            middles[m - 1][1][0] = after(middles[m - 1][1][0], d_att_far)
        middles.append([d_middle, [d_att_own, swap_far(d_att_far)], sums, d_att_far])

    feed_total = lax.psum_scatter(grads_feed, "dp", scatter_dimension=0, tiled=True)
    out_far = swap_far(grads_out[1])

    mod_grads = []
    g_qkv = None
    backs = []
    for m in range(micro_count):
        normed_a, qkv, att, lse = state[m]
        keep, send, back, sums = attend_back(
            blocks[m], qkv, att, middles[m][1], lse, tables, doc_rows[m : m + 1],
            bounds[m][1], place, wq, heads, rq, rk,
        )
        if m > 0:
            (keep, send, back, sums), (backs[m - 1][2], out_half) = lax.optimization_barrier(
                ((keep, send, back, sums), (backs[m - 1][2], out_half))
            )
        elif m == 0:
            (keep, send, back, sums), out_far = lax.optimization_barrier(
                ((keep, send, back, sums), out_far)
            )
            out_keep, out_send = halves(
                by_bits(grads_out[0] + out_far.astype(F32)), 0, falling
            )
            out_half = swap_dp(out_send, 0)
        arrived = swap_near(send)
        crossing = (keep[1] + arrived[1].astype(F32)).astype(BF16)
        crossed = swap_far(crossing)
        g_qkv = project_grad(normed_a, back, g_qkv)
        if m + 1 < micro_count:
            middles[m + 1][1][0] = after(
                middles[m + 1][1][0], (crossing, g_qkv, out_send)
            )
            middles[m + 1][1][1] = after(middles[m + 1][1][1], sums)
        backs.append([keep, arrived, crossed])
        mod_grads.append(jnp.concatenate([sums.reshape(-1), middles[m][2].reshape(-1)]))
    g_last = after(g_qkv, crossing)
    middles[0][0] = after(middles[0][0], g_last)
    d_tokens = None
    wide_set = jax.ShapeDtypeStruct(tokens.shape, F32)
    for m in range(micro_count):
        keep, arrived, crossing = backs[m]
        (d_tokens,) = by_rows(
            "finish",
            finish_kernel,
            m,
            mods,
            [(tokens, True), (keep, False), (arrived, False), (crossing, False), middles[m][0]],
            [wide_set],
            before=d_tokens,
        )
        if m == 0:
            d_tokens, backs[-1][2] = lax.optimization_barrier((d_tokens, backs[-1][2]))
            first_done, crossed = d_tokens, backs[-1][2]
    sides = feed_total[:, : 2 * hid], feed_total[:, 2 * hid :]
    feed_far = swap_far(after(pick(far, sides[1], sides[0]), crossed))
    total = pick(far, sides[0], sides[1]).astype(F32) + feed_far.astype(F32)
    pieces = jnp.split(total, 2 * hid // CHUNK, axis=1)
    g_up = jnp.concatenate(pieces[0::2], axis=1)
    g_down = jnp.concatenate(pieces[1::2], axis=1).T
    current, sent = halves(by_bits(g_last), 0, falling)
    swapped = after(swap_dp(sent, 0), first_done)
    current = jnp.concatenate(
        [out_keep + out_half.astype(F32), current + swapped.astype(F32)], axis=-1
    )
    for bit in rising[1:]:
        if bit == 1:
            current = after(current, crossed)
        current, sent = halves(current, bit, falling[: count - bit])
        current = current + swap_dp(sent, bit).astype(F32)
    g_out = current[:, :part].T
    g_qkv = current[:, part:]

    d_mods = jnp.stack(mod_grads)
    d_mods = after(d_mods + swap_far(d_mods), g_last)
    d_mods = d_mods + swap_near(d_mods)
    all_mods = gather_relative(
        d_mods, lambda value, bit: after(value, swapped) if bit == 1 else value
    ).reshape(-1, d_mods.shape[1])
    g_ada = lax.dot_general(
        cond.astype(F32),
        all_mods,
        TN,
        precision=lax.Precision.HIGHEST,
        preferred_element_type=F32,
    )
    g_bias = lax.dynamic_slice_in_dim(jnp.sum(all_mods, axis=0), device * bias_size, bias_size)
    return (
        output,
        d_tokens,
        g_qkv,
        g_out,
        g_up,
        g_down,
        g_ada,
        g_bias,
    )


def solution(mesh):
    return jax.shard_map(
        per_device,
        mesh=mesh,
        in_specs=(
            P(None, ("dp", "tensor"), None),
            P(None, "dp"),
            P(None, "dp"),
            P(None, ("dp", "tensor"), None),
            P("dp", "tensor"),
            P("tensor", "dp"),
            P("dp", "tensor"),
            P("tensor", "dp"),
            P(("dp", "tensor"), None),
            P(("dp", "tensor")),
        ),
        out_specs=(
            P(None, ("dp", "tensor"), None),
            P(None, ("dp", "tensor"), None),
            P("dp", "tensor"),
            P("tensor", "dp"),
            P("dp", "tensor"),
            P("tensor", "dp"),
            P(("dp", "tensor"), None),
            P(("dp", "tensor")),
        ),
        check_vma=False,
    )
```

```python
import functools
import math

import jax
import jax.numpy as jnp
from jax import lax
from jax.experimental import pallas as pl
from jax.experimental.pallas import tpu as pltpu
from jax.sharding import PartitionSpec as P

HEADS = 12
HD = 64
HALF = HD // 2
EPSILON = 1e-06
MASKED = -1e30
F32 = jnp.float32
BF16 = jnp.bfloat16
NN = (((1,), (0,)), ((), ()))
NT = (((1,), (1,)), ((), ()))
TN = (((0,), (0,)), ((), ()))
TT = (((0,), (1,)), ((), ()))


def dot(left, right, dims=NN):
    return lax.dot_general(left, right, dims, preferred_element_type=F32)


def pick(bit, zero, one):
    return jnp.where(bit == 0, zero, one)


def swap_far(value):
    return lax.ppermute(value, "tensor", [(i, i ^ 2) for i in range(4)])


def swap_near(value):
    return lax.ppermute(value, "tensor", [(i, i ^ 1) for i in range(4)])


def swap_by(value, mask):
    return lax.ppermute(value, "dp", [(i, i ^ mask) for i in range(lax.axis_size("dp"))])


def swap_dp(value, bit):
    return swap_by(value, 1 << bit)


def after(value, other):
    return lax.optimization_barrier((value, other))[0]


def dp_bits():
    return lax.axis_size("dp").bit_length() - 1


def my_bit(bit):
    return (lax.axis_index("dp") >> bit) & 1


def gather_block(current, bit, done, arrival=lambda value: value):
    arrived = arrival(swap_dp(current, bit))
    place = sum(1 for other in done if other > bit)
    mine = my_bit(bit)
    return jnp.stack([pick(mine, current, arrived), pick(mine, arrived, current)], axis=place)


def halves(current, bit, left):
    place = left.index(bit)
    first = lax.index_in_dim(current, 0, place, keepdims=False)
    second = lax.index_in_dim(current, 1, place, keepdims=False)
    mine = my_bit(bit)
    return pick(mine, first, second), pick(mine, second, first).astype(BF16)


def by_bits(total):
    return total.reshape((2,) * dp_bits() + (-1, total.shape[-1]))


def gather_relative(value, first=lambda value, bit: value):
    current = value
    count = dp_bits()
    for bit in range(count):
        current = first(current, bit)
        if bit == 1 and count == 3:
            others = [swap_by(current, k << 1) for k in range(1, 4)]
            current = jnp.stack([current, *others])
            break
        current = jnp.stack([current, swap_dp(current, bit)])
    return current.reshape((-1,) + value.shape)


def scatter_relative(terms, first=lambda value, bit: value):
    count = dp_bits()
    current = terms.reshape((2,) * count + terms.shape[1:])
    for bit in range(count):
        current = first(current, bit)
        if bit == 1 and count == 3:
            current = current.reshape((4,) + current.shape[2:])
            return current[0] + sum(swap_by(current[k], k << 1) for k in range(1, 4))
        place = count - 1 - bit
        kept = lax.index_in_dim(current, 0, place, keepdims=False)
        sent = lax.index_in_dim(current, 1, place, keepdims=False)
        current = kept + swap_dp(sent, bit)
    return current


def document_columns(row_ref, col_s):
    for start in range(0, row_ref.shape[1], 128):
        tile = jnp.broadcast_to(row_ref[0:1, start : start + 128], (128, 128))
        col_s[start : start + 128, :] = tile.T


def token_copies(refs, place, tok_s, sems):
    rows = tok_s.shape[0] // 4
    return [
        pltpu.make_async_copy(
            ref,
            tok_s.at[pl.ds(pl.multiple_of(jnp.bitwise_xor(place, r) * rows, rows), rows), :],
            sems.at[r],
        )
        for r, ref in enumerate(refs)
    ]


def same_documents(row_ref, col_s, rows, columns, size):
    return jnp.concatenate([col_s[rows, :]] * (size // 128), axis=1) == row_ref[0:1, columns]


def attend_kernel(
    m, bq, bk, heads, lo_ref, hi_ref, place_ref, t0, t1, t2, t3, mods_ref, wq_ref, cs_ref, sn_ref,
    row_ref, normed_hbm, qkv_ref, own_ref, far_ref, lse_ref,
    tok_s, normed_s, wq_s, key_s, acc_s, att_s, col_s, sem, token_sems,
):
    length, width = tok_s.shape
    rows = length // 4
    place = place_ref[0]
    copies = token_copies((t0, t1, t2, t3), place, tok_s, token_sems)
    for copy in copies:
        copy.start()
    wq_s[...] = wq_ref[...].T
    document_columns(row_ref, col_s)
    for copy in copies:
        copy.wait()
    shift = mods_ref[m : m + 1, 0:width]
    stretch = 1.0 + mods_ref[m : m + 1, width : 2 * width]
    step = min(256, rows)

    def project(i, _):
        piece = pl.ds(pl.multiple_of(i * step, step), step)
        unit, _ = normalize(tok_s[piece, :].astype(F32))
        normed = (unit * stretch + shift).astype(BF16)
        normed_s[piece, :] = normed
        packed = dot(wq_s[...], normed, NT)
        cosine = cs_ref[:, piece]
        sine = sn_ref[:, piece]
        for h in range(heads):
            base = 3 * HD * h

            def turned(row):
                a = packed[row : row + HALF]
                b = packed[row + HALF : row + HD]
                return jnp.concatenate([a * cosine - b * sine, a * sine + b * cosine], axis=0)

            qkv_ref[base : base + HD, piece] = turned(base).astype(BF16)
            keys = turned(base + HD)
            qkv_ref[base + HD : base + 2 * HD, piece] = keys.astype(BF16)
            key_s[h, piece, :] = keys.T.astype(BF16)
            qkv_ref[base + 2 * HD : base + 3 * HD, piece] = packed[
                base + 2 * HD : base + 3 * HD
            ].astype(BF16)
        return 0

    lax.fori_loop(0, length // step, project, 0)
    copy = pltpu.make_async_copy(normed_s, normed_hbm, sem)
    copy.start()

    def query_block(i, _):
        columns = pl.ds(pl.multiple_of(i * bq, bq), bq)
        queries = [
            qkv_ref[3 * HD * h : 3 * HD * h + HD, columns] * jnp.asarray(0.125, BF16)
            for h in range(heads)
        ]
        acc_s[...] = jnp.zeros_like(acc_s)

        def key_block(j, carry):
            keys = pl.ds(pl.multiple_of(j * bk, bk), bk)
            allowed = same_documents(row_ref, col_s, keys, columns, bq)
            scores = [dot(key_s[h, keys, :], queries[h]) for h in range(heads)]
            result, fades, lows = [], [], []
            for h in range(heads):
                top, total = carry[2 * h], carry[2 * h + 1]
                masked = jnp.where(allowed, scores[h], MASKED)
                new_top = jnp.maximum(top, jnp.max(masked, axis=0, keepdims=True))
                fade = jnp.exp(top - new_top)
                chances = jnp.exp(masked - new_top)
                total = fade * total + jnp.sum(chances, axis=0, keepdims=True)
                lows.append(chances.astype(BF16))
                fades.append(fade)
                result += [new_top, total]
            for h in range(heads):
                values = qkv_ref[3 * HD * h + 2 * HD : 3 * HD * h + 3 * HD, keys]
                acc_s[h] = acc_s[h] * fades[h] + dot(values, lows[h])
            return tuple(result)

        start = (jnp.full((1, bq), MASKED, F32), jnp.zeros((1, bq), F32)) * heads
        carry = lax.fori_loop(lo_ref[i], hi_ref[i], key_block, start)
        for h in range(heads):
            top, total = carry[2 * h], carry[2 * h + 1]
            att_s[HD * h : HD * h + HD, columns] = (acc_s[h] / total).astype(BF16)
            lse_ref[h, 0:1, columns] = top + jnp.log(total)
        return 0

    lax.fori_loop(0, length // bq, query_block, 0)
    half = length // 2
    mine = pl.multiple_of(place // 2 * half, half)
    away = pl.multiple_of(half - mine, half)
    own_ref[...] = att_s[:, pl.ds(mine, half)]
    far_ref[...] = att_s[:, pl.ds(away, half)]
    copy.wait()


def attend_back_kernel(
    bq, bk, heads, lo_ref, hi_ref, place_ref, qkv_ref, own_ref, far_ref, d_own_ref, d_far_ref,
    lse_ref, cs_ref, sn_ref, row_ref, wq_hbm, t0, t1, t2, t3,
    keep_ref, send_ref, back_s, sums_ref, q_s, k_s, v_s, g_s, dat_s, dq_s, dk_s, dv_s, inner_s,
    col_s, wq_s, tok_s, sems, token_sems,
):
    place = place_ref[0]
    copies = [
        pltpu.make_async_copy(wq_hbm, wq_s, sems),
        *token_copies((t0, t1, t2, t3), place, tok_s, token_sems),
    ]
    for copy in copies:
        copy.start()
    length = qkv_ref.shape[1]
    half = length // 2
    rows = length // 4
    document_columns(row_ref, col_s)
    mine = pl.multiple_of(place // 2 * half, half)
    away = pl.multiple_of(half - mine, half)
    for start, att_ref, d_ref in ((mine, own_ref, d_own_ref), (away, far_ref, d_far_ref)):
        piece = pl.ds(start, half)
        dat_s[:, piece] = d_ref[...]
        for h in range(heads):
            head = slice(HD * h, HD * h + HD)
            inner_s[h, 0:1, piece] = jnp.sum(
                att_ref[head, :].astype(F32) * d_ref[head, :].astype(F32), axis=0, keepdims=True
            )
            g_s[h, piece, :] = d_ref[head, :].T
    for h in range(heads):
        base = 3 * HD * h
        q_s[h] = qkv_ref[base : base + HD, :].T
        k_s[h] = qkv_ref[base + HD : base + 2 * HD, :].T
        v_s[h] = qkv_ref[base + 2 * HD : base + 3 * HD, :].T
    dq_s[...] = jnp.zeros_like(dq_s)

    def key_block(j, _):
        keys = pl.ds(pl.multiple_of(j * bk, bk), bk)
        dk_s[:, keys, :] = jnp.zeros((heads, bk, HD), F32)
        dv_s[:, keys, :] = jnp.zeros((heads, bk, HD), F32)

        def query_block(i, _):
            columns = pl.ds(pl.multiple_of(i * bq, bq), bq)
            allowed = same_documents(row_ref, col_s, keys, columns, bq)
            for h in range(heads):
                base = 3 * HD * h
                head = slice(HD * h, HD * h + HD)
                scores = dot(
                    k_s[h, keys, :] * jnp.asarray(0.125, BF16), qkv_ref[base : base + HD, columns]
                )
                chances = jnp.where(
                    allowed, jnp.exp(scores - lse_ref[h, 0:1, columns]), 0.0
                )
                d_chances = dot(v_s[h, keys, :], dat_s[head, columns])
                d_scores = (chances * (d_chances - inner_s[h, 0:1, columns])).astype(BF16)
                dv_s[h, keys, :] += dot(chances.astype(BF16), g_s[h, columns, :])
                dk_s[h, keys, :] += dot(d_scores, q_s[h, columns, :])
                dq_s[head, columns] += dot(qkv_ref[base + HD : base + 2 * HD, keys], d_scores)
            return 0

        lax.fori_loop(lo_ref[j], hi_ref[j], query_block, 0)
        return 0

    lax.fori_loop(0, length // bk, key_block, 0)
    for copy in copies:
        copy.wait()
    step = min(256, rows)

    sums_ref[...] = jnp.zeros_like(sums_ref)
    for r, (ref, entry) in enumerate(
        ((keep_ref, 0), (send_ref, 0), (keep_ref, 1), (send_ref, 1))
    ):

        def finish(i, _):
            start = jnp.bitwise_xor(place, r) * rows + i * step
            piece = pl.ds(pl.multiple_of(start, step), step)
            cosine = cs_ref[:, piece] * 0.125
            sine = sn_ref[:, piece] * 0.125

            def turned_back(row, value):
                a = value[0:HALF, :]
                b = value[HALF:HD, :]
                back_s[row : row + HALF, piece] = (a * cosine + b * sine).astype(BF16)
                back_s[row + HALF : row + HD, piece] = (b * cosine - a * sine).astype(BF16)

            for h in range(heads):
                base = 3 * HD * h
                turned_back(base, dq_s[HD * h : HD * h + HD, piece])
                turned_back(base + HD, dk_s[h, piece, :].T)
                back_s[base + 2 * HD : base + 3 * HD, piece] = dv_s[h, piece, :].T.astype(BF16)
            part = dot(back_s[:, piece].T, wq_s[...], NT)
            unit, _ = normalize(tok_s[piece, :].astype(F32))
            sums_ref[0:1, :] += jnp.sum(part, axis=0, keepdims=True)
            sums_ref[1:2, :] += jnp.sum(part * unit, axis=0, keepdims=True)
            ref[entry, pl.ds(pl.multiple_of(i * step, step), step), :] = part.astype(ref.dtype)
            return 0

        lax.fori_loop(0, rows // step, finish, 0)

def project_grad_kernel(add, normed_ref, back_ref, *rest):
    if add:
        before_ref, *rest = rest
    out_ref, total_s = rest
    step = pl.program_id(0)

    @pl.when(step == 0)
    def _():
        total_s[...] = jnp.zeros_like(total_s)

    total_s[...] += dot(back_ref[...], normed_ref[...])

    @pl.when(step == pl.num_programs(0) - 1)
    def _():
        total = total_s[...].T
        out_ref[...] = total + before_ref[...] if add else total


def project_grad(normed, back, before):
    length, width = normed.shape
    size = back.shape[0]
    add = before is not None
    step = length // 4
    block = pl.BlockSpec((width, size), lambda i: (0, 0))
    return pl.pallas_call(
        functools.partial(project_grad_kernel, add),
        grid=(4,),
        in_specs=[
            pl.BlockSpec((step, width), lambda i: (i, 0)),
            pl.BlockSpec((size, step), lambda i: (0, i)),
        ]
        + [block] * add,
        out_specs=block,
        out_shape=jax.ShapeDtypeStruct((width, size), F32),
        scratch_shapes=[pltpu.VMEM((size, width), F32)],
        cost_estimate=pl.CostEstimate(
            flops=40 * length * width * size, bytes_accessed=length * width * 4, transcendentals=0
        ),
        name="project_grad",
    )(normed, back, *[before] * add)


def held(*shape):
    return pl.BlockSpec(shape, lambda i, *_: (0,) * len(shape), pipeline_mode=pl.Buffered(1))


ANYWHERE = pl.BlockSpec(memory_space=pl.ANY)


def attend(m, blocks, mods, wq, tables, doc_row, bounds, place, heads, bq, bk):
    rows, width = blocks[0].shape
    length = 4 * rows
    size = 3 * HD * heads
    return pl.pallas_call(
        functools.partial(attend_kernel, m, bq, bk, heads),
        grid_spec=pltpu.PrefetchScalarGridSpec(
            num_scalar_prefetch=3,
            grid=(1,),
            in_specs=[ANYWHERE] * 4
            + [
                held(*mods.shape),
                held(width, size),
                held(HALF, length),
                held(HALF, length),
                held(1, length),
            ],
            out_specs=[
                ANYWHERE,
                held(size, length),
                held(HD * heads, length // 2),
                held(HD * heads, length // 2),
                held(heads, 1, length),
            ],
            scratch_shapes=[
                pltpu.VMEM((length, width), BF16),
                pltpu.VMEM((length, width), BF16),
                pltpu.VMEM((size, width), BF16),
                pltpu.VMEM((heads, length, HD), BF16),
                pltpu.VMEM((heads, HD, bq), F32),
                pltpu.VMEM((HD * heads, length), BF16),
                pltpu.VMEM((length, 128), F32),
                pltpu.SemaphoreType.DMA(()),
                pltpu.SemaphoreType.DMA((4,)),
            ],
        ),
        out_shape=[
            jax.ShapeDtypeStruct((length, width), BF16),
            jax.ShapeDtypeStruct((size, length), BF16),
            jax.ShapeDtypeStruct((HD * heads, length // 2), BF16),
            jax.ShapeDtypeStruct((HD * heads, length // 2), BF16),
            jax.ShapeDtypeStruct((heads, 1, length), F32),
        ],
        cost_estimate=pl.CostEstimate(
            flops=heads * length * length * 800,
            bytes_accessed=length * width * 8,
            transcendentals=heads * length * length // 2,
        ),
        compiler_params=pltpu.CompilerParams(vmem_limit_bytes=46 * 2**20),
        name="attend",
    )(*bounds, place, *blocks, mods, wq, *tables, doc_row)


def attend_back(
    blocks, qkv, att, d_att, lse, tables, doc_row, bounds, place, wq, heads, bq, bk
):
    size, length = qkv.shape
    width = wq.shape[0]
    rows = length // 4
    half = held(HD * heads, length // 2)
    return pl.pallas_call(
        functools.partial(attend_back_kernel, bq, bk, heads),
        grid_spec=pltpu.PrefetchScalarGridSpec(
            num_scalar_prefetch=3,
            grid=(1,),
            in_specs=[
                held(size, length),
                half,
                half,
                half,
                half,
                held(heads, 1, length),
                held(HALF, length),
                held(HALF, length),
                held(1, length),
            ]
            + [ANYWHERE] * 5,
            out_specs=[
                held(2, rows, width),
                held(2, rows, width),
                held(size, length),
                held(2, width),
            ],
            scratch_shapes=[pltpu.VMEM((heads, length, HD), BF16)] * 4
            + [
                pltpu.VMEM((heads * HD, length), BF16),
                pltpu.VMEM((heads * HD, length), F32),
                pltpu.VMEM((heads, length, HD), F32),
                pltpu.VMEM((heads, length, HD), F32),
                pltpu.VMEM((heads, 8, length), F32),
                pltpu.VMEM((length, 128), F32),
                pltpu.VMEM((width, size), BF16),
                pltpu.VMEM((length, width), BF16),
                pltpu.SemaphoreType.DMA(()),
                pltpu.SemaphoreType.DMA((4,)),
            ],
        ),
        out_shape=[
            jax.ShapeDtypeStruct((2, rows, width), F32),
            jax.ShapeDtypeStruct((2, rows, width), BF16),
            jax.ShapeDtypeStruct((size, length), BF16),
            jax.ShapeDtypeStruct((2, width), F32),
        ],
        cost_estimate=pl.CostEstimate(
            flops=heads * length * length * 3600,
            bytes_accessed=length * width * 8,
            transcendentals=heads * length * length // 2,
        ),
        compiler_params=pltpu.CompilerParams(vmem_limit_bytes=50 * 2**20),
        name="attend_back",
    )(*bounds, place, qkv, *att, *d_att, lse, *tables, doc_row, wq, *blocks)


def gelu_pair(values):
    square = values * values
    bend = jnp.tanh(0.7978845608028654 * (values + 0.044715 * (square * values)))
    slope = 0.7978845608028654 * (1.0 + 3 * 0.044715 * square)
    hidden = 0.5 * values * (1.0 + bend)
    return hidden, 0.5 * (1.0 + bend) + 0.5 * values * (1.0 - bend * bend) * slope


def feed_kernel(parts, add, n0, n1, g0, g1, up_ref, down_ref, *rest):
    if add:
        before_ref, *rest = rest
    b0, b1, d0, d1, g_ref, n_s, g_s, n_t, g_t, hidden_s, pre_s, b1_s, d1_s = rest
    rows = n0.shape[0]
    up = up_ref[...].reshape(-1, up_ref.shape[-1])
    down = down_ref[...].reshape(-1, down_ref.shape[-1])

    @pl.when(pl.program_id(0) == 0)
    def _():
        for piece, n, g in ((slice(0, rows), n0, g0), (slice(rows, 2 * rows), n1, g1)):
            n_s[piece, :] = n[...]
            g_s[piece, :] = g[...]
            n_t[:, piece] = n[...].T
            g_t[:, piece] = g[...].T
        for ref in (b0, b1_s, d0, d1_s):
            ref[...] = jnp.zeros_like(ref)

    step = 2 * rows // parts
    for p in range(parts):
        piece = slice(p * step, (p + 1) * step)
        hidden, slope = gelu_pair(dot(n_s[piece, :], up))
        hidden_s[piece, :] = hidden.astype(BF16)
        pre_s[piece, :] = (dot(g_s[piece, :], down) * slope).astype(BF16)
    for first, b_ref, d_ref in ((0, b0, d0), (rows, b1_s, d1_s)):
        for start in range(0, rows, step):
            piece = slice(first + start, first + start + step)
            b_ref[start : start + step, :] += dot(hidden_s[piece, :], down, NT)
            d_ref[start : start + step, :] += dot(pre_s[piece, :], up, NT)
    chunk = up.shape[1]
    for start, left, right in ((0, n_t, pre_s), (chunk, g_t, hidden_s)):
        columns = slice(start, start + chunk)
        grad = dot(left[...], right[...])
        if add:
            grad = grad + before_ref[:, columns]
        g_ref[:, columns] = grad.astype(g_ref.dtype)

    @pl.when(pl.program_id(0) == pl.num_programs(0) - 1)
    def _():
        b1[...] = b1_s[...].astype(BF16)
        d1[...] = d1_s[...].astype(BF16)


CHUNK = 256


def feed(normed, grads, pack, hid, before, kind):
    rows, width = normed[0].shape
    count, _, height, _ = pack.shape
    chunk = CHUNK
    steps = hid // chunk
    add = before is not None

    def weight(first):
        return pl.BlockSpec(
            (count, 1, height, chunk), lambda i: (0, i // steps, 0, first * steps + i % steps)
        )

    block = pl.BlockSpec((rows, width), lambda i: (0, 0))
    columns = pl.BlockSpec((width, 2 * chunk), lambda i: (0, i))
    total = 2 * rows
    return pl.pallas_call(
        functools.partial(feed_kernel, 4, add),
        grid=(2 * steps,),
        in_specs=[block] * 4 + [weight(0), weight(1)] + [columns] * add,
        out_specs=[block] * 4 + [columns],
        out_shape=[jax.ShapeDtypeStruct((rows, width), kind) for kind in (F32, BF16, F32, BF16)]
        + [jax.ShapeDtypeStruct((width, 4 * hid), kind)],
        scratch_shapes=[pltpu.VMEM((total, width), BF16)] * 2
        + [pltpu.VMEM((width, total), BF16)] * 2
        + [pltpu.VMEM((total, chunk), BF16)] * 2
        + [pltpu.VMEM((rows, width), F32)] * 2,
        cost_estimate=pl.CostEstimate(
            flops=24 * total * width * hid,
            bytes_accessed=8 * width * hid + 12 * total * width,
            transcendentals=2 * total * hid,
        ),
        compiler_params=pltpu.CompilerParams(vmem_limit_bytes=46 * 2**20),
        name="feed",
    )(*normed, *grads, pack, pack, *[before] * add)


def terms_kernel(cond_ref, w_ref, bias_ref, out_ref):
    total = bias_ref[...] + jnp.zeros_like(out_ref)
    for r in range(w_ref.shape[0]):
        total = total + cond_ref[:, r : r + 1] * w_ref[r : r + 1, :].astype(F32)
    out_ref[...] = total


def mod_terms(cond, w_ada, bias):
    return pl.pallas_call(
        terms_kernel,
        out_shape=jax.ShapeDtypeStruct((cond.shape[0], w_ada.shape[1]), F32),
        cost_estimate=pl.CostEstimate(
            flops=2 * cond.size * w_ada.shape[1],
            bytes_accessed=4 * cond.shape[0] * w_ada.shape[1],
            transcendentals=0,
        ),
        name="mod_terms",
    )(cond.astype(F32), w_ada, bias[None, :])


def part_of(mods_ref, m, k, width):
    return mods_ref[m : m + 1, k * width : (k + 1) * width]


def out_weights(pack_ref, side, size):
    return pack_ref[:, pl.ds(side, 1), :, :].reshape(-1, size)


def out_kernel(place_ref, own_ref, far_ref, pack_ref, keep_ref, send_ref):
    size, total = own_ref.shape
    rows = total // 2
    side, near = place_ref[0] // 2, place_ref[0] % 2
    own_w = out_weights(pack_ref, side, size)
    far_w = out_weights(pack_ref, 1 - side, size)
    for ref, half in ((keep_ref, near), (send_ref, 1 - near)):
        piece = pl.ds(pl.multiple_of(half * rows, rows), rows)
        ref[...] = (
            dot(own_ref[:, piece].T, own_w, NT) + dot(far_ref[:, piece].T, far_w, NT)
        ).astype(ref.dtype)


def out_project(place, own, away, pack):
    size, total = own.shape
    rows, width = total // 2, pack.shape[0] * pack.shape[2]
    return pl.pallas_call(
        out_kernel,
        grid_spec=pltpu.PrefetchScalarGridSpec(
            num_scalar_prefetch=1,
            grid=(1,),
            in_specs=[held(size, total), held(size, total), held(*pack.shape)],
            out_specs=[held(rows, width), held(rows, width)],
        ),
        out_shape=[
            jax.ShapeDtypeStruct((rows, width), F32),
            jax.ShapeDtypeStruct((rows, width), BF16),
        ],
        cost_estimate=pl.CostEstimate(
            flops=8 * total * width * size, bytes_accessed=total * width * 4, transcendentals=0
        ),
        compiler_params=pltpu.CompilerParams(vmem_limit_bytes=20 * 2**20),
        name="out_project",
    )(place, own, away, pack)


def out_back_kernel(add, place_ref, g0_ref, g1_ref, own_ref, far_ref, pack_ref, *rest):
    if add:
        *before_refs, = rest[:2]
        rest = rest[2:]
    d_own_ref, d_far_ref, *grad_refs = rest
    size, total = own_ref.shape
    rows = total // 2
    side, near = place_ref[0] // 2, place_ref[0] % 2
    pieces = [
        pl.ds(pl.multiple_of(half * rows, rows), rows) for half in (near, 1 - near)
    ]
    grads = [g0_ref[...], g1_ref[...]]
    turned = [grad.T for grad in grads]
    for k, (att_ref, d_ref, which) in enumerate(
        ((own_ref, d_own_ref, side), (far_ref, d_far_ref, 1 - side))
    ):
        weights = out_weights(pack_ref, which, size).T
        total_grad = 0.0
        for grad, flipped, piece in zip(grads, turned, pieces):
            d_ref[:, piece] = dot(weights, grad, NT).astype(BF16)
            total_grad = total_grad + dot(flipped, att_ref[:, piece], NT)
        if add:
            total_grad = total_grad + before_refs[k][...]
        grad_refs[k][...] = total_grad.astype(grad_refs[k].dtype)


def out_back(place, grads, own, away, pack, before, last):
    size, total = own.shape
    rows, width = grads[0].shape
    add = before is not None
    half = held(size, total)
    return pl.pallas_call(
        functools.partial(out_back_kernel, add),
        grid_spec=pltpu.PrefetchScalarGridSpec(
            num_scalar_prefetch=1,
            grid=(1,),
            in_specs=[held(rows, width)] * 2
            + [half, half, held(*pack.shape)]
            + [held(width, size)] * (2 * add),
            out_specs=[half, half, held(width, size), held(width, size)],
        ),
        out_shape=[jax.ShapeDtypeStruct((size, total), BF16)] * 2
        + [
            jax.ShapeDtypeStruct((width, size), F32),
            jax.ShapeDtypeStruct((width, size), BF16 if last else F32),
        ],
        cost_estimate=pl.CostEstimate(
            flops=16 * total * width * size, bytes_accessed=total * width * 4, transcendentals=0
        ),
        compiler_params=None if last else pltpu.CompilerParams(vmem_limit_bytes=24 * 2**20),
        name="out_back",
    )(place, *grads, own, away, pack, *(before if add else ()))


def before_feed_kernel(m, mods_ref, tok_ref, cot_ref, keep_ref, arr_ref, br_ref, n_ref, g_ref):
    width = keep_ref.shape[1]
    branch = keep_ref[...] + arr_ref[...].astype(F32)
    br_ref[...] = branch
    middle = tok_ref[0].astype(F32) + part_of(mods_ref, m, 2, width) * branch
    unit, _ = normalize(middle)
    n_ref[...] = (
        unit * (1.0 + part_of(mods_ref, m, 4, width)) + part_of(mods_ref, m, 3, width)
    ).astype(BF16)
    g_ref[...] = (cot_ref[0].astype(F32) * part_of(mods_ref, m, 5, width)).astype(BF16)


def after_feed_kernel(
    m, mods_ref, tok_ref, cot_ref, br_ref, b0_ref, b1_ref, d0_ref, d1_ref, *rest
):
    out_ref, d_ref, g_ref, sums_ref = rest[-4:]
    width = br_ref.shape[1]
    branch_a = br_ref[...]
    middle = tok_ref[0].astype(F32) + part_of(mods_ref, m, 2, width) * branch_a
    unit, root = normalize(middle)
    branch_m = b0_ref[...] + b1_ref[...].astype(F32)
    out_ref[0] = (middle + part_of(mods_ref, m, 5, width) * branch_m).astype(BF16)
    d_normed = d0_ref[...] + d1_ref[...].astype(F32)
    grad = cot_ref[0].astype(F32)
    d_middle = grad + normalize_back(d_normed, unit, root, part_of(mods_ref, m, 4, width))
    d_ref[...] = d_middle
    g_ref[...] = (d_middle * part_of(mods_ref, m, 2, width)).astype(BF16)

    @pl.when(pl.program_id(0) == 0)
    def _():
        sums_ref[...] = jnp.zeros_like(sums_ref)

    for k, term in enumerate((d_middle * branch_a, d_normed, d_normed * unit, grad * branch_m)):
        sums_ref[k : k + 1, :] += jnp.sum(term, axis=0, keepdims=True)


def finish_kernel(m, mods_ref, tok_ref, keep_ref, arr_ref, crossed_ref, d_ref, *rest):
    out_ref = rest[-1]
    width = d_ref.shape[1]
    unit, root = normalize(tok_ref[0].astype(F32))
    grad = keep_ref[0] + arr_ref[0].astype(F32) + crossed_ref[...].astype(F32)
    out_ref[0] = d_ref[...] + normalize_back(grad, unit, root, part_of(mods_ref, m, 1, width))


def by_rows(name, kernel, m, mods, inputs, outputs, before=None, sums=0, weight=40):
    rows, width = inputs[-1].shape
    step = min(256, rows)
    flat = pl.BlockSpec((step, width), lambda i: (i, 0))
    entry = pl.BlockSpec((1, step, width), lambda i: (m, i, 0))
    first = pl.BlockSpec((1, step, width), lambda i: (0, i, 0))
    in_specs = [pl.BlockSpec(mods.shape, lambda i: (0, 0))]
    for value, whole_set in inputs[:-1]:
        in_specs.append(flat if value.ndim == 2 else entry if whole_set else first)
    values = [value for value, _ in inputs[:-1]] + [inputs[-1]]
    in_specs.append(flat)
    extra = [] if before is None else [before]
    in_specs += [ANYWHERE] * len(extra)
    out_specs = [flat if len(shape.shape) == 2 else entry for shape in outputs]
    if sums:
        outputs = [*outputs, jax.ShapeDtypeStruct((sums, width), F32)]
        out_specs.append(pl.BlockSpec((sums, width), lambda i: (0, 0)))
    return pl.pallas_call(
        functools.partial(kernel, m),
        grid=(rows // step,),
        in_specs=in_specs,
        out_specs=out_specs,
        out_shape=outputs,
        input_output_aliases={1 + len(values): 0} if extra else {},
        cost_estimate=pl.CostEstimate(
            flops=weight * rows * width, bytes_accessed=32 * rows * width, transcendentals=rows
        ),
        compiler_params=None
        if name == "finish"
        else pltpu.CompilerParams(vmem_limit_bytes=16 * 2**20),
        name=name,
    )(mods, *values, *extra)


def block_range(doc_ids, rows, columns):
    by_row = doc_ids.reshape(-1, rows)
    by_column = doc_ids.reshape(-1, columns)
    low = jnp.sum(by_column[:, -1][None, :] < by_row[:, 0][:, None], axis=1, dtype=jnp.int32)
    high = jnp.sum(by_column[:, 0][None, :] <= by_row[:, -1][:, None], axis=1, dtype=jnp.int32)
    return low, high


def turn_tables(length):
    freqs = jnp.exp(-math.log(10000.0) * jnp.arange(HALF, dtype=F32) / HALF)
    angles = freqs[:, None] * jnp.arange(length, dtype=F32)[None, :]
    return jnp.cos(angles), jnp.sin(angles)


def normalize(values):
    center = values - jnp.mean(values, axis=-1, keepdims=True)
    root = lax.rsqrt(jnp.mean(center * center, axis=-1, keepdims=True) + EPSILON)
    return center * root, root


def normalize_back(grad, unit, root, stretch):
    turned = grad * (1.0 + stretch)
    return root * (
        turned
        - jnp.mean(turned, axis=-1, keepdims=True)
        - unit * jnp.mean(turned * unit, axis=-1, keepdims=True)
    )


def per_device(tokens, segments, timesteps, cotangent, w_qkv, w_out, w_up, w_down, w_ada, b_ada):
    micro_count, rows, width = tokens.shape
    heads = HEADS // 4
    length = 4 * rows
    count = dp_bits()
    tensor = lax.axis_index("tensor")
    far, near = tensor // 2, tensor % 2
    device = lax.axis_index("dp") * 4 + tensor
    falling = list(range(count - 1, -1, -1))
    rising = list(range(count))

    fq, fk = min(512, length), min(512, length)
    rq, rk = min(512, length), min(256, length)
    doc_rows = segments.astype(F32)
    bounds = [
        (block_range(segments[m], fq, fk), block_range(segments[m], rk, rq))
        for m in range(micro_count)
    ]
    tables = turn_tables(length)
    pack = jnp.concatenate([w_up, w_down.T, w_out.T], axis=1)

    states = []

    def advance(value, step):
        while len(states) <= step:
            done = falling[: len(states)]
            states.append(
                gather_block(states[-1] if states else w_qkv, falling[len(done)], done)
            )
        return after(value, states[step])

    def with_stamps(value, bit):
        return advance(value, bit - 1) if bit >= 1 else value

    def with_terms(value, bit):
        return advance(value, count - 2) if bit == 0 else value

    ready = tokens[0]
    across = swap_far(ready)
    blocks = [(ready, swap_near(ready), across, swap_near(across))]

    feature_rows = w_ada.shape[0]
    half = feature_rows * lax.axis_size("dp") * 4 // 2
    stamps = gather_relative(timesteps[:, 0].astype(F32), with_stamps)
    index = device * feature_rows + jnp.arange(feature_rows)
    freqs = jnp.exp(-math.log(10000.0) * (index % half).astype(F32) / half)
    angles = stamps[:, :, None] * freqs
    cond = jnp.where(index < half, jnp.cos(angles), jnp.sin(angles)).astype(BF16)
    cond = cond.reshape(-1, feature_rows)
    bias_size = b_ada.shape[0]
    slots = w_ada.shape[1] // bias_size
    bias = jnp.where(
        jnp.arange(slots)[:, None] == device, b_ada.astype(F32)[None, :], 0.0
    ).reshape(-1)
    terms = mod_terms(after(cond, across), w_ada, bias)
    mods = scatter_relative(terms.reshape(-1, micro_count, terms.shape[1]), with_terms)

    mods = after(mods, (blocks[0][3], tables, doc_rows, bounds))
    mods = advance(mods + swap_far(mods), count - 1)
    wq = states[-1].reshape(width, -1)
    mods = mods + swap_near(mods)

    pack = after(pack, cond)
    groups = [
        [4 * i + 2 * j + c for i in range(lax.axis_size("dp")) for j in range(2)] for c in range(2)
    ]
    pack = lax.all_gather(pack, ("dp", "tensor"), axis_index_groups=groups)
    pack = pack.reshape((-1, 2) + pack.shape[1:])
    hid = w_up.shape[1]
    part = w_out.shape[0]
    if w_up.shape[0] % 16:
        pack = pack.transpose(1, 0, 2, 3).reshape(1, 2, width, -1)

    place = tensor.astype(jnp.int32).reshape(1)
    state = []
    for m in range(micro_count):
        if m > 0:
            own = after(tokens, mods)[m]
            across = after(swap_far(own), state[-1][3])
            blocks.append((own, swap_near(own), across, swap_near(across)))
        normed_a, qkv, att_own, att_away, lse = attend(
            m, blocks[m], mods, wq, tables, doc_rows[m : m + 1],
            bounds[m][0], place, heads, fq, fk,
        )
        state.append((normed_a, qkv, (att_own, att_away), lse))

    out_pack = pack[..., 2 * hid :]
    every = jax.ShapeDtypeStruct(tokens.shape, BF16)
    wide = jax.ShapeDtypeStruct((rows, width), F32)
    low = jax.ShapeDtypeStruct((rows, width), BF16)
    output = None
    grads_out = None
    grads_feed = None
    middles = []
    for m in range(micro_count):
        last = m + 1 == micro_count
        att_own, att_away = state[m][2]
        if m == 0:
            crossing = [swap_far(state[k][2][1]) for k in range(micro_count)]
        att_far = crossing[m]
        if not last:
            att_far = after(att_far, state[m + 1][2][0])
        keep, send = out_project(place, att_own, att_far, out_pack)
        branch_a, normed_m, grad_m = by_rows(
            "before_feed",
            before_feed_kernel,
            m,
            mods,
            [(tokens, True), (cotangent, True), (keep, False), swap_near(send)],
            [wide, low, low],
        )
        if m > 0:
            normed_m = after(normed_m, middles[-1][3])
        branch_own, branch_near, d_own, d_near, grads_feed = feed(
            (normed_m, swap_near(normed_m)),
            (grad_m, swap_near(grad_m)),
            pack,
            hid,
            grads_feed,
            BF16 if last else F32,
        )
        if not last:
            (branch_own, branch_near, d_own, d_near), crossing[m + 1] = lax.optimization_barrier(
                ((branch_own, branch_near, d_own, d_near), crossing[m + 1])
            )
        if m > 0:
            (branch_own, branch_near, d_own, d_near), middles[m - 1][1][1] = (
                lax.optimization_barrier(
                    ((branch_own, branch_near, d_own, d_near), middles[m - 1][1][1])
                )
            )
        output, d_middle, grad_a, sums = by_rows(
            "after_feed",
            after_feed_kernel,
            m,
            mods,
            [
                (tokens, True),
                (cotangent, True),
                (branch_a, False),
                (branch_own, False),
                (swap_near(branch_near), False),
                (d_own, False),
                swap_near(d_near),
            ],
            [every, wide, low],
            before=output,
            sums=4,
        )
        d_att_own, d_att_far, *grads_out = out_back(
            place, (grad_a, swap_near(grad_a)), att_own, att_far, out_pack, grads_out,
            last,
        )
        if m > 0:
            middles[m - 1][1][0] = after(middles[m - 1][1][0], d_att_far)
        middles.append([d_middle, [d_att_own, swap_far(d_att_far)], sums, d_att_far])

    feed_total = lax.psum_scatter(grads_feed, "dp", scatter_dimension=0, tiled=True)
    out_far = swap_far(grads_out[1])

    mod_grads = []
    g_qkv = None
    backs = []
    for m in range(micro_count):
        normed_a, qkv, att, lse = state[m]
        keep, send, back, sums = attend_back(
            blocks[m], qkv, att, middles[m][1], lse, tables, doc_rows[m : m + 1],
            bounds[m][1], place, wq, heads, rq, rk,
        )
        if m > 0:
            (keep, send, back, sums), (backs[m - 1][2], out_half) = lax.optimization_barrier(
                ((keep, send, back, sums), (backs[m - 1][2], out_half))
            )
        elif m == 0:
            (keep, send, back, sums), out_far = lax.optimization_barrier(
                ((keep, send, back, sums), out_far)
            )
            out_keep, out_send = halves(
                by_bits(grads_out[0] + out_far.astype(F32)), 0, falling
            )
            out_half = swap_dp(out_send, 0)
        arrived = swap_near(send)
        crossing = (keep[1] + arrived[1].astype(F32)).astype(BF16)
        crossed = swap_far(crossing)
        g_qkv = project_grad(normed_a, back, g_qkv)
        if m + 1 < micro_count:
            middles[m + 1][1][0] = after(
                middles[m + 1][1][0], (crossing, g_qkv, out_send)
            )
            middles[m + 1][1][1] = after(middles[m + 1][1][1], sums)
        backs.append([keep, arrived, crossed])
        mod_grads.append(jnp.concatenate([sums.reshape(-1), middles[m][2].reshape(-1)]))
    g_last = after(g_qkv, crossing)
    middles[0][0] = after(middles[0][0], g_last)
    d_tokens = None
    wide_set = jax.ShapeDtypeStruct(tokens.shape, F32)
    for m in range(micro_count):
        keep, arrived, crossing = backs[m]
        (d_tokens,) = by_rows(
            "finish",
            finish_kernel,
            m,
            mods,
            [(tokens, True), (keep, False), (arrived, False), (crossing, False), middles[m][0]],
            [wide_set],
            before=d_tokens,
        )
        if m == 0:
            d_tokens, backs[-1][2] = lax.optimization_barrier((d_tokens, backs[-1][2]))
            first_done, crossed = d_tokens, backs[-1][2]
    sides = feed_total[:, : 2 * hid], feed_total[:, 2 * hid :]
    feed_far = swap_far(after(pick(far, sides[1], sides[0]), crossed))
    total = pick(far, sides[0], sides[1]).astype(F32) + feed_far.astype(F32)
    pieces = jnp.split(total, 2 * hid // CHUNK, axis=1)
    g_up = jnp.concatenate(pieces[0::2], axis=1)
    g_down = jnp.concatenate(pieces[1::2], axis=1).T
    d_mods = jnp.stack(mod_grads)
    d_mods = after(d_mods + swap_far(d_mods), g_last)
    d_mods = d_mods + swap_near(d_mods)
    all_mods = gather_relative(d_mods).reshape(-1, d_mods.shape[1])
    current, sent = halves(by_bits(g_last), 0, falling)
    swapped = after(swap_dp(sent, 0), (first_done, all_mods))
    current = jnp.concatenate(
        [out_keep + out_half.astype(F32), current + swapped.astype(F32)], axis=-1
    )
    for bit in rising[1:]:
        if bit == 1:
            current = after(current, crossed)
        current, sent = halves(current, bit, falling[: count - bit])
        current = current + swap_dp(sent, bit).astype(F32)
    g_out = current[:, :part].T
    g_qkv = current[:, part:]

    g_ada = lax.dot_general(
        cond.astype(F32),
        all_mods,
        TN,
        precision=lax.Precision.HIGHEST,
        preferred_element_type=F32,
    )
    g_bias = lax.dynamic_slice_in_dim(jnp.sum(all_mods, axis=0), device * bias_size, bias_size)
    return (
        output,
        d_tokens,
        g_qkv,
        g_out,
        g_up,
        g_down,
        g_ada,
        g_bias,
    )


def solution(mesh):
    return jax.shard_map(
        per_device,
        mesh=mesh,
        in_specs=(
            P(None, ("dp", "tensor"), None),
            P(None, "dp"),
            P(None, "dp"),
            P(None, ("dp", "tensor"), None),
            P("dp", "tensor"),
            P("tensor", "dp"),
            P("dp", "tensor"),
            P("tensor", "dp"),
            P(("dp", "tensor"), None),
            P(("dp", "tensor")),
        ),
        out_specs=(
            P(None, ("dp", "tensor"), None),
            P(None, ("dp", "tensor"), None),
            P("dp", "tensor"),
            P("tensor", "dp"),
            P("dp", "tensor"),
            P("tensor", "dp"),
            P(("dp", "tensor"), None),
            P(("dp", "tensor")),
        ),
        check_vma=False,
    )
```

```python
import functools
import math

import jax
import jax.numpy as jnp
from jax import lax
from jax.experimental import pallas as pl
from jax.experimental.pallas import tpu as pltpu
from jax.sharding import PartitionSpec as P

HEADS = 12
HD = 64
HALF = HD // 2
EPSILON = 1e-06
MASKED = -1e30
F32 = jnp.float32
BF16 = jnp.bfloat16
NN = (((1,), (0,)), ((), ()))
NT = (((1,), (1,)), ((), ()))
TN = (((0,), (0,)), ((), ()))
TT = (((0,), (1,)), ((), ()))


def dot(left, right, dims=NN):
    return lax.dot_general(left, right, dims, preferred_element_type=F32)


def pick(bit, zero, one):
    return jnp.where(bit == 0, zero, one)


def swap_far(value):
    return lax.ppermute(value, "tensor", [(i, i ^ 2) for i in range(4)])


def swap_near(value):
    return lax.ppermute(value, "tensor", [(i, i ^ 1) for i in range(4)])


def swap_by(value, mask):
    return lax.ppermute(value, "dp", [(i, i ^ mask) for i in range(lax.axis_size("dp"))])


def swap_dp(value, bit):
    return swap_by(value, 1 << bit)


def after(value, other):
    return lax.optimization_barrier((value, other))[0]


def dp_bits():
    return lax.axis_size("dp").bit_length() - 1


def my_bit(bit):
    return (lax.axis_index("dp") >> bit) & 1


def gather_block(current, bit, done, arrival=lambda value: value):
    arrived = arrival(swap_dp(current, bit))
    place = sum(1 for other in done if other > bit)
    mine = my_bit(bit)
    return jnp.stack([pick(mine, current, arrived), pick(mine, arrived, current)], axis=place)


def halves(current, bit, left):
    place = left.index(bit)
    first = lax.index_in_dim(current, 0, place, keepdims=False)
    second = lax.index_in_dim(current, 1, place, keepdims=False)
    mine = my_bit(bit)
    return pick(mine, first, second), pick(mine, second, first).astype(BF16)


def by_bits(total):
    return total.reshape((2,) * dp_bits() + (-1, total.shape[-1]))


def gather_relative(value, first=lambda value, bit: value):
    current = value
    count = dp_bits()
    for bit in range(count):
        current = first(current, bit)
        if bit == 1 and count == 3:
            others = [swap_by(current, k << 1) for k in range(1, 4)]
            current = jnp.stack([current, *others])
            break
        current = jnp.stack([current, swap_dp(current, bit)])
    return current.reshape((-1,) + value.shape)


def scatter_relative(terms, first=lambda value, bit: value):
    count = dp_bits()
    current = terms.reshape((2,) * count + terms.shape[1:])
    for bit in range(count):
        current = first(current, bit)
        if bit == 1 and count == 3:
            current = current.reshape((4,) + current.shape[2:])
            return current[0] + sum(swap_by(current[k], k << 1) for k in range(1, 4))
        place = count - 1 - bit
        kept = lax.index_in_dim(current, 0, place, keepdims=False)
        sent = lax.index_in_dim(current, 1, place, keepdims=False)
        current = kept + swap_dp(sent, bit)
    return current


def document_columns(row_ref, col_s):
    for start in range(0, row_ref.shape[1], 128):
        tile = jnp.broadcast_to(row_ref[0:1, start : start + 128], (128, 128))
        col_s[start : start + 128, :] = tile.T


def token_copies(refs, place, tok_s, sems):
    rows = tok_s.shape[0] // 4
    return [
        pltpu.make_async_copy(
            ref,
            tok_s.at[pl.ds(pl.multiple_of(jnp.bitwise_xor(place, r) * rows, rows), rows), :],
            sems.at[r],
        )
        for r, ref in enumerate(refs)
    ]


def same_documents(row_ref, col_s, rows, columns, size):
    return jnp.concatenate([col_s[rows, :]] * (size // 128), axis=1) == row_ref[0:1, columns]


def attend_kernel(
    m, bq, bk, heads, lo_ref, hi_ref, place_ref, t0, t1, t2, t3, mods_ref, wq_ref, cs_ref, sn_ref,
    row_ref, normed_hbm, qkv_ref, own_ref, far_ref, lse_ref,
    tok_s, normed_s, wq_s, key_s, acc_s, att_s, col_s, sem, token_sems,
):
    length, width = tok_s.shape
    rows = length // 4
    place = place_ref[0]
    copies = token_copies((t0, t1, t2, t3), place, tok_s, token_sems)
    for copy in copies:
        copy.start()
    wq_s[...] = wq_ref[...].T
    document_columns(row_ref, col_s)
    for copy in copies:
        copy.wait()
    shift = mods_ref[m : m + 1, 0:width]
    stretch = 1.0 + mods_ref[m : m + 1, width : 2 * width]
    step = min(256, rows)

    def project(i, _):
        piece = pl.ds(pl.multiple_of(i * step, step), step)
        unit, _ = normalize(tok_s[piece, :].astype(F32))
        normed = (unit * stretch + shift).astype(BF16)
        normed_s[piece, :] = normed
        packed = dot(wq_s[...], normed, NT)
        cosine = cs_ref[:, piece]
        sine = sn_ref[:, piece]
        for h in range(heads):
            base = 3 * HD * h

            def turned(row):
                a = packed[row : row + HALF]
                b = packed[row + HALF : row + HD]
                return jnp.concatenate([a * cosine - b * sine, a * sine + b * cosine], axis=0)

            qkv_ref[base : base + HD, piece] = turned(base).astype(BF16)
            keys = turned(base + HD)
            qkv_ref[base + HD : base + 2 * HD, piece] = keys.astype(BF16)
            key_s[h, piece, :] = keys.T.astype(BF16)
            qkv_ref[base + 2 * HD : base + 3 * HD, piece] = packed[
                base + 2 * HD : base + 3 * HD
            ].astype(BF16)
        return 0

    lax.fori_loop(0, length // step, project, 0)
    copy = pltpu.make_async_copy(normed_s, normed_hbm, sem)
    copy.start()

    def query_block(i, _):
        columns = pl.ds(pl.multiple_of(i * bq, bq), bq)
        queries = [
            qkv_ref[3 * HD * h : 3 * HD * h + HD, columns] * jnp.asarray(0.125, BF16)
            for h in range(heads)
        ]
        acc_s[...] = jnp.zeros_like(acc_s)

        def key_block(j, carry):
            keys = pl.ds(pl.multiple_of(j * bk, bk), bk)
            allowed = same_documents(row_ref, col_s, keys, columns, bq)
            scores = [dot(key_s[h, keys, :], queries[h]) for h in range(heads)]
            result, fades, lows = [], [], []
            for h in range(heads):
                top, total = carry[2 * h], carry[2 * h + 1]
                masked = jnp.where(allowed, scores[h], MASKED)
                new_top = jnp.maximum(top, jnp.max(masked, axis=0, keepdims=True))
                fade = jnp.exp(top - new_top)
                chances = jnp.exp(masked - new_top)
                total = fade * total + jnp.sum(chances, axis=0, keepdims=True)
                lows.append(chances.astype(BF16))
                fades.append(fade)
                result += [new_top, total]
            for h in range(heads):
                values = qkv_ref[3 * HD * h + 2 * HD : 3 * HD * h + 3 * HD, keys]
                acc_s[h] = acc_s[h] * fades[h] + dot(values, lows[h])
            return tuple(result)

        start = (jnp.full((1, bq), MASKED, F32), jnp.zeros((1, bq), F32)) * heads
        carry = lax.fori_loop(lo_ref[i], hi_ref[i], key_block, start)
        for h in range(heads):
            top, total = carry[2 * h], carry[2 * h + 1]
            att_s[HD * h : HD * h + HD, columns] = (acc_s[h] / total).astype(BF16)
            lse_ref[h, 0:1, columns] = top + jnp.log(total)
        return 0

    lax.fori_loop(0, length // bq, query_block, 0)
    half = length // 2
    mine = pl.multiple_of(place // 2 * half, half)
    away = pl.multiple_of(half - mine, half)
    own_ref[...] = att_s[:, pl.ds(mine, half)]
    far_ref[...] = att_s[:, pl.ds(away, half)]
    copy.wait()


def attend_back_kernel(
    bq, bk, heads, lo_ref, hi_ref, place_ref, qkv_ref, own_ref, far_ref, d_own_ref, d_far_ref,
    lse_ref, cs_ref, sn_ref, row_ref, wq_hbm, t0, t1, t2, t3,
    keep_ref, send_ref, back_s, sums_ref, q_s, k_s, v_s, g_s, dat_s, dq_s, dk_s, dv_s, inner_s,
    col_s, wq_s, tok_s, sems, token_sems,
):
    place = place_ref[0]
    copies = [
        pltpu.make_async_copy(wq_hbm, wq_s, sems),
        *token_copies((t0, t1, t2, t3), place, tok_s, token_sems),
    ]
    for copy in copies:
        copy.start()
    length = qkv_ref.shape[1]
    half = length // 2
    rows = length // 4
    document_columns(row_ref, col_s)
    mine = pl.multiple_of(place // 2 * half, half)
    away = pl.multiple_of(half - mine, half)
    for start, att_ref, d_ref in ((mine, own_ref, d_own_ref), (away, far_ref, d_far_ref)):
        piece = pl.ds(start, half)
        dat_s[:, piece] = d_ref[...]
        for h in range(heads):
            head = slice(HD * h, HD * h + HD)
            inner_s[h, 0:1, piece] = jnp.sum(
                att_ref[head, :].astype(F32) * d_ref[head, :].astype(F32), axis=0, keepdims=True
            )
            g_s[h, piece, :] = d_ref[head, :].T
    for h in range(heads):
        base = 3 * HD * h
        q_s[h] = qkv_ref[base : base + HD, :].T
        k_s[h] = qkv_ref[base + HD : base + 2 * HD, :].T * jnp.asarray(0.125, BF16)
        v_s[h] = qkv_ref[base + 2 * HD : base + 3 * HD, :].T
    dq_s[...] = jnp.zeros_like(dq_s)

    def key_block(j, _):
        keys = pl.ds(pl.multiple_of(j * bk, bk), bk)
        dk_s[:, keys, :] = jnp.zeros((heads, bk, HD), F32)
        dv_s[:, keys, :] = jnp.zeros((heads, bk, HD), F32)

        def query_block(i, _):
            columns = pl.ds(pl.multiple_of(i * bq, bq), bq)
            allowed = same_documents(row_ref, col_s, keys, columns, bq)
            for h in range(heads):
                base = 3 * HD * h
                head = slice(HD * h, HD * h + HD)
                scores = dot(k_s[h, keys, :], qkv_ref[base : base + HD, columns])
                chances = jnp.where(
                    allowed, jnp.exp(scores - lse_ref[h, 0:1, columns]), 0.0
                )
                d_chances = dot(v_s[h, keys, :], dat_s[head, columns])
                d_scores = (chances * (d_chances - inner_s[h, 0:1, columns])).astype(BF16)
                dv_s[h, keys, :] += dot(chances.astype(BF16), g_s[h, columns, :])
                dk_s[h, keys, :] += dot(d_scores, q_s[h, columns, :])
                dq_s[head, columns] += dot(qkv_ref[base + HD : base + 2 * HD, keys], d_scores)
            return 0

        lax.fori_loop(lo_ref[j], hi_ref[j], query_block, 0)
        return 0

    lax.fori_loop(0, length // bk, key_block, 0)
    for copy in copies:
        copy.wait()
    step = min(256, rows)

    sums_ref[...] = jnp.zeros_like(sums_ref)
    for r, (ref, entry) in enumerate(
        ((keep_ref, 0), (send_ref, 0), (keep_ref, 1), (send_ref, 1))
    ):

        def finish(i, _):
            start = jnp.bitwise_xor(place, r) * rows + i * step
            piece = pl.ds(pl.multiple_of(start, step), step)
            cosine = cs_ref[:, piece] * 0.125
            sine = sn_ref[:, piece] * 0.125

            def turned_back(row, value):
                a = value[0:HALF, :]
                b = value[HALF:HD, :]
                back_s[row : row + HALF, piece] = (a * cosine + b * sine).astype(BF16)
                back_s[row + HALF : row + HD, piece] = (b * cosine - a * sine).astype(BF16)

            for h in range(heads):
                base = 3 * HD * h
                turned_back(base, dq_s[HD * h : HD * h + HD, piece])
                turned_back(base + HD, dk_s[h, piece, :].T)
                back_s[base + 2 * HD : base + 3 * HD, piece] = dv_s[h, piece, :].T.astype(BF16)
            part = dot(back_s[:, piece].T, wq_s[...], NT)
            unit, _ = normalize(tok_s[piece, :].astype(F32))
            sums_ref[0:1, :] += jnp.sum(part, axis=0, keepdims=True)
            sums_ref[1:2, :] += jnp.sum(part * unit, axis=0, keepdims=True)
            ref[entry, pl.ds(pl.multiple_of(i * step, step), step), :] = part.astype(ref.dtype)
            return 0

        lax.fori_loop(0, rows // step, finish, 0)

def project_grad_kernel(add, normed_ref, back_ref, *rest):
    if add:
        before_ref, *rest = rest
    out_ref, total_s = rest
    step = pl.program_id(0)

    @pl.when(step == 0)
    def _():
        total_s[...] = jnp.zeros_like(total_s)

    total_s[...] += dot(back_ref[...], normed_ref[...])

    @pl.when(step == pl.num_programs(0) - 1)
    def _():
        total = total_s[...].T
        out_ref[...] = total + before_ref[...] if add else total


def project_grad(normed, back, before):
    length, width = normed.shape
    size = back.shape[0]
    add = before is not None
    step = length // 4
    block = pl.BlockSpec((width, size), lambda i: (0, 0))
    return pl.pallas_call(
        functools.partial(project_grad_kernel, add),
        grid=(4,),
        in_specs=[
            pl.BlockSpec((step, width), lambda i: (i, 0)),
            pl.BlockSpec((size, step), lambda i: (0, i)),
        ]
        + [block] * add,
        out_specs=block,
        out_shape=jax.ShapeDtypeStruct((width, size), F32),
        scratch_shapes=[pltpu.VMEM((size, width), F32)],
        cost_estimate=pl.CostEstimate(
            flops=40 * length * width * size, bytes_accessed=length * width * 4, transcendentals=0
        ),
        name="project_grad",
    )(normed, back, *[before] * add)


def held(*shape):
    return pl.BlockSpec(shape, lambda i, *_: (0,) * len(shape), pipeline_mode=pl.Buffered(1))


ANYWHERE = pl.BlockSpec(memory_space=pl.ANY)


def attend(m, blocks, mods, wq, tables, doc_row, bounds, place, heads, bq, bk):
    rows, width = blocks[0].shape
    length = 4 * rows
    size = 3 * HD * heads
    return pl.pallas_call(
        functools.partial(attend_kernel, m, bq, bk, heads),
        grid_spec=pltpu.PrefetchScalarGridSpec(
            num_scalar_prefetch=3,
            grid=(1,),
            in_specs=[ANYWHERE] * 4
            + [
                held(*mods.shape),
                held(width, size),
                held(HALF, length),
                held(HALF, length),
                held(1, length),
            ],
            out_specs=[
                ANYWHERE,
                held(size, length),
                held(HD * heads, length // 2),
                held(HD * heads, length // 2),
                held(heads, 1, length),
            ],
            scratch_shapes=[
                pltpu.VMEM((length, width), BF16),
                pltpu.VMEM((length, width), BF16),
                pltpu.VMEM((size, width), BF16),
                pltpu.VMEM((heads, length, HD), BF16),
                pltpu.VMEM((heads, HD, bq), F32),
                pltpu.VMEM((HD * heads, length), BF16),
                pltpu.VMEM((length, 128), F32),
                pltpu.SemaphoreType.DMA(()),
                pltpu.SemaphoreType.DMA((4,)),
            ],
        ),
        out_shape=[
            jax.ShapeDtypeStruct((length, width), BF16),
            jax.ShapeDtypeStruct((size, length), BF16),
            jax.ShapeDtypeStruct((HD * heads, length // 2), BF16),
            jax.ShapeDtypeStruct((HD * heads, length // 2), BF16),
            jax.ShapeDtypeStruct((heads, 1, length), F32),
        ],
        cost_estimate=pl.CostEstimate(
            flops=heads * length * length * 800,
            bytes_accessed=length * width * 8,
            transcendentals=heads * length * length // 2,
        ),
        compiler_params=pltpu.CompilerParams(vmem_limit_bytes=46 * 2**20),
        name="attend",
    )(*bounds, place, *blocks, mods, wq, *tables, doc_row)


def attend_back(
    blocks, qkv, att, d_att, lse, tables, doc_row, bounds, place, wq, heads, bq, bk
):
    size, length = qkv.shape
    width = wq.shape[0]
    rows = length // 4
    half = held(HD * heads, length // 2)
    return pl.pallas_call(
        functools.partial(attend_back_kernel, bq, bk, heads),
        grid_spec=pltpu.PrefetchScalarGridSpec(
            num_scalar_prefetch=3,
            grid=(1,),
            in_specs=[
                held(size, length),
                half,
                half,
                half,
                half,
                held(heads, 1, length),
                held(HALF, length),
                held(HALF, length),
                held(1, length),
            ]
            + [ANYWHERE] * 5,
            out_specs=[
                held(2, rows, width),
                held(2, rows, width),
                held(size, length),
                held(2, width),
            ],
            scratch_shapes=[pltpu.VMEM((heads, length, HD), BF16)] * 4
            + [
                pltpu.VMEM((heads * HD, length), BF16),
                pltpu.VMEM((heads * HD, length), F32),
                pltpu.VMEM((heads, length, HD), F32),
                pltpu.VMEM((heads, length, HD), F32),
                pltpu.VMEM((heads, 8, length), F32),
                pltpu.VMEM((length, 128), F32),
                pltpu.VMEM((width, size), BF16),
                pltpu.VMEM((length, width), BF16),
                pltpu.SemaphoreType.DMA(()),
                pltpu.SemaphoreType.DMA((4,)),
            ],
        ),
        out_shape=[
            jax.ShapeDtypeStruct((2, rows, width), F32),
            jax.ShapeDtypeStruct((2, rows, width), BF16),
            jax.ShapeDtypeStruct((size, length), BF16),
            jax.ShapeDtypeStruct((2, width), F32),
        ],
        cost_estimate=pl.CostEstimate(
            flops=heads * length * length * 3600,
            bytes_accessed=length * width * 8,
            transcendentals=heads * length * length // 2,
        ),
        compiler_params=pltpu.CompilerParams(vmem_limit_bytes=50 * 2**20),
        name="attend_back",
    )(*bounds, place, qkv, *att, *d_att, lse, *tables, doc_row, wq, *blocks)


def gelu_pair(values):
    square = values * values
    bend = jnp.tanh(0.7978845608028654 * (values + 0.044715 * (square * values)))
    slope = 0.7978845608028654 * (1.0 + 3 * 0.044715 * square)
    hidden = 0.5 * values * (1.0 + bend)
    return hidden, 0.5 * (1.0 + bend) + 0.5 * values * (1.0 - bend * bend) * slope


def feed_kernel(parts, add, n0, n1, g0, g1, up_ref, down_ref, *rest):
    if add:
        before_ref, *rest = rest
    b0, b1, d0, d1, g_ref, n_s, g_s, n_t, g_t, hidden_s, pre_s, b1_s, d1_s = rest
    rows = n0.shape[0]
    up = up_ref[...].reshape(-1, up_ref.shape[-1])
    down = down_ref[...].reshape(-1, down_ref.shape[-1])

    @pl.when(pl.program_id(0) == 0)
    def _():
        for piece, n, g in ((slice(0, rows), n0, g0), (slice(rows, 2 * rows), n1, g1)):
            n_s[piece, :] = n[...]
            g_s[piece, :] = g[...]
            n_t[:, piece] = n[...].T
            g_t[:, piece] = g[...].T
        for ref in (b0, b1_s, d0, d1_s):
            ref[...] = jnp.zeros_like(ref)

    step = 2 * rows // parts
    for p in range(parts):
        piece = slice(p * step, (p + 1) * step)
        hidden, slope = gelu_pair(dot(n_s[piece, :], up))
        hidden_s[piece, :] = hidden.astype(BF16)
        pre_s[piece, :] = (dot(g_s[piece, :], down) * slope).astype(BF16)
    for first, b_ref, d_ref in ((0, b0, d0), (rows, b1_s, d1_s)):
        for start in range(0, rows, step):
            piece = slice(first + start, first + start + step)
            b_ref[start : start + step, :] += dot(hidden_s[piece, :], down, NT)
            d_ref[start : start + step, :] += dot(pre_s[piece, :], up, NT)
    chunk = up.shape[1]
    for start, left, right in ((0, n_t, pre_s), (chunk, g_t, hidden_s)):
        columns = slice(start, start + chunk)
        grad = dot(left[...], right[...])
        if add:
            grad = grad + before_ref[:, columns]
        g_ref[:, columns] = grad.astype(g_ref.dtype)

    @pl.when(pl.program_id(0) == pl.num_programs(0) - 1)
    def _():
        b1[...] = b1_s[...].astype(BF16)
        d1[...] = d1_s[...].astype(BF16)


CHUNK = 256


def feed(normed, grads, pack, hid, before, kind):
    rows, width = normed[0].shape
    count, _, height, _ = pack.shape
    chunk = CHUNK
    steps = hid // chunk
    add = before is not None

    def weight(first):
        return pl.BlockSpec(
            (count, 1, height, chunk), lambda i: (0, i // steps, 0, first * steps + i % steps)
        )

    block = pl.BlockSpec((rows, width), lambda i: (0, 0))
    columns = pl.BlockSpec((width, 2 * chunk), lambda i: (0, i))
    total = 2 * rows
    return pl.pallas_call(
        functools.partial(feed_kernel, 4, add),
        grid=(2 * steps,),
        in_specs=[block] * 4 + [weight(0), weight(1)] + [columns] * add,
        out_specs=[block] * 4 + [columns],
        out_shape=[jax.ShapeDtypeStruct((rows, width), kind) for kind in (F32, BF16, F32, BF16)]
        + [jax.ShapeDtypeStruct((width, 4 * hid), kind)],
        scratch_shapes=[pltpu.VMEM((total, width), BF16)] * 2
        + [pltpu.VMEM((width, total), BF16)] * 2
        + [pltpu.VMEM((total, chunk), BF16)] * 2
        + [pltpu.VMEM((rows, width), F32)] * 2,
        cost_estimate=pl.CostEstimate(
            flops=24 * total * width * hid,
            bytes_accessed=8 * width * hid + 12 * total * width,
            transcendentals=2 * total * hid,
        ),
        compiler_params=pltpu.CompilerParams(vmem_limit_bytes=36 * 2**20),
        name="feed",
    )(*normed, *grads, pack, pack, *[before] * add)


def terms_kernel(cond_ref, w_ref, bias_ref, out_ref):
    total = bias_ref[...] + jnp.zeros_like(out_ref)
    for r in range(w_ref.shape[0]):
        total = total + cond_ref[:, r : r + 1] * w_ref[r : r + 1, :].astype(F32)
    out_ref[...] = total


def mod_terms(cond, w_ada, bias):
    return pl.pallas_call(
        terms_kernel,
        out_shape=jax.ShapeDtypeStruct((cond.shape[0], w_ada.shape[1]), F32),
        cost_estimate=pl.CostEstimate(
            flops=2 * cond.size * w_ada.shape[1],
            bytes_accessed=4 * cond.shape[0] * w_ada.shape[1],
            transcendentals=0,
        ),
        name="mod_terms",
    )(cond.astype(F32), w_ada, bias[None, :])


def part_of(mods_ref, m, k, width):
    return mods_ref[m : m + 1, k * width : (k + 1) * width]


def out_weights(pack_ref, side, size):
    return pack_ref[:, pl.ds(side, 1), :, :].reshape(-1, size)


def out_kernel(place_ref, own_ref, far_ref, pack_ref, keep_ref, send_ref):
    size, total = own_ref.shape
    rows = total // 2
    side, near = place_ref[0] // 2, place_ref[0] % 2
    own_w = out_weights(pack_ref, side, size)
    far_w = out_weights(pack_ref, 1 - side, size)
    for ref, half in ((keep_ref, near), (send_ref, 1 - near)):
        piece = pl.ds(pl.multiple_of(half * rows, rows), rows)
        ref[...] = (
            dot(own_ref[:, piece].T, own_w, NT) + dot(far_ref[:, piece].T, far_w, NT)
        ).astype(ref.dtype)


def out_project(place, own, away, pack):
    size, total = own.shape
    rows, width = total // 2, pack.shape[0] * pack.shape[2]
    return pl.pallas_call(
        out_kernel,
        grid_spec=pltpu.PrefetchScalarGridSpec(
            num_scalar_prefetch=1,
            grid=(1,),
            in_specs=[held(size, total), held(size, total), held(*pack.shape)],
            out_specs=[held(rows, width), held(rows, width)],
        ),
        out_shape=[
            jax.ShapeDtypeStruct((rows, width), F32),
            jax.ShapeDtypeStruct((rows, width), BF16),
        ],
        cost_estimate=pl.CostEstimate(
            flops=8 * total * width * size, bytes_accessed=total * width * 4, transcendentals=0
        ),
        compiler_params=pltpu.CompilerParams(vmem_limit_bytes=20 * 2**20),
        name="out_project",
    )(place, own, away, pack)


def out_back_kernel(add, place_ref, g0_ref, g1_ref, own_ref, far_ref, pack_ref, *rest):
    if add:
        *before_refs, = rest[:2]
        rest = rest[2:]
    d_own_ref, d_far_ref, *grad_refs = rest
    size, total = own_ref.shape
    rows = total // 2
    side, near = place_ref[0] // 2, place_ref[0] % 2
    pieces = [
        pl.ds(pl.multiple_of(half * rows, rows), rows) for half in (near, 1 - near)
    ]
    grads = [g0_ref[...], g1_ref[...]]
    turned = [grad.T for grad in grads]
    for k, (att_ref, d_ref, which) in enumerate(
        ((own_ref, d_own_ref, side), (far_ref, d_far_ref, 1 - side))
    ):
        weights = out_weights(pack_ref, which, size).T
        total_grad = 0.0
        for grad, flipped, piece in zip(grads, turned, pieces):
            d_ref[:, piece] = dot(weights, grad, NT).astype(BF16)
            total_grad = total_grad + dot(flipped, att_ref[:, piece], NT)
        if add:
            total_grad = total_grad + before_refs[k][...]
        grad_refs[k][...] = total_grad.astype(grad_refs[k].dtype)


def out_back(place, grads, own, away, pack, before, last):
    size, total = own.shape
    rows, width = grads[0].shape
    add = before is not None
    half = held(size, total)
    return pl.pallas_call(
        functools.partial(out_back_kernel, add),
        grid_spec=pltpu.PrefetchScalarGridSpec(
            num_scalar_prefetch=1,
            grid=(1,),
            in_specs=[held(rows, width)] * 2
            + [half, half, held(*pack.shape)]
            + [held(width, size)] * (2 * add),
            out_specs=[half, half, held(width, size), held(width, size)],
        ),
        out_shape=[jax.ShapeDtypeStruct((size, total), BF16)] * 2
        + [
            jax.ShapeDtypeStruct((width, size), F32),
            jax.ShapeDtypeStruct((width, size), BF16 if last else F32),
        ],
        cost_estimate=pl.CostEstimate(
            flops=16 * total * width * size, bytes_accessed=total * width * 4, transcendentals=0
        ),
        compiler_params=None if last else pltpu.CompilerParams(vmem_limit_bytes=24 * 2**20),
        name="out_back",
    )(place, *grads, own, away, pack, *(before if add else ()))


def before_feed_kernel(m, mods_ref, tok_ref, cot_ref, keep_ref, arr_ref, br_ref, n_ref, g_ref):
    width = keep_ref.shape[1]
    branch = keep_ref[...] + arr_ref[...].astype(F32)
    br_ref[...] = branch
    middle = tok_ref[0].astype(F32) + part_of(mods_ref, m, 2, width) * branch
    unit, _ = normalize(middle)
    n_ref[...] = (
        unit * (1.0 + part_of(mods_ref, m, 4, width)) + part_of(mods_ref, m, 3, width)
    ).astype(BF16)
    g_ref[...] = (cot_ref[0].astype(F32) * part_of(mods_ref, m, 5, width)).astype(BF16)


def after_feed_kernel(
    m, mods_ref, tok_ref, cot_ref, br_ref, b0_ref, b1_ref, d0_ref, d1_ref, *rest
):
    out_ref, d_ref, g_ref, sums_ref = rest[-4:]
    width = br_ref.shape[1]
    branch_a = br_ref[...]
    middle = tok_ref[0].astype(F32) + part_of(mods_ref, m, 2, width) * branch_a
    unit, root = normalize(middle)
    branch_m = b0_ref[...] + b1_ref[...].astype(F32)
    out_ref[0] = (middle + part_of(mods_ref, m, 5, width) * branch_m).astype(BF16)
    d_normed = d0_ref[...] + d1_ref[...].astype(F32)
    grad = cot_ref[0].astype(F32)
    d_middle = grad + normalize_back(d_normed, unit, root, part_of(mods_ref, m, 4, width))
    d_ref[...] = d_middle
    g_ref[...] = (d_middle * part_of(mods_ref, m, 2, width)).astype(BF16)

    @pl.when(pl.program_id(0) == 0)
    def _():
        sums_ref[...] = jnp.zeros_like(sums_ref)

    for k, term in enumerate((d_middle * branch_a, d_normed, d_normed * unit, grad * branch_m)):
        sums_ref[k : k + 1, :] += jnp.sum(term, axis=0, keepdims=True)


def finish_kernel(m, mods_ref, tok_ref, keep_ref, arr_ref, crossed_ref, d_ref, *rest):
    out_ref = rest[-1]
    width = d_ref.shape[1]
    unit, root = normalize(tok_ref[0].astype(F32))
    grad = keep_ref[0] + arr_ref[0].astype(F32) + crossed_ref[...].astype(F32)
    out_ref[0] = d_ref[...] + normalize_back(grad, unit, root, part_of(mods_ref, m, 1, width))


def by_rows(name, kernel, m, mods, inputs, outputs, before=None, sums=0, weight=40):
    rows, width = inputs[-1].shape
    step = min(256, rows)
    flat = pl.BlockSpec((step, width), lambda i: (i, 0))
    entry = pl.BlockSpec((1, step, width), lambda i: (m, i, 0))
    first = pl.BlockSpec((1, step, width), lambda i: (0, i, 0))
    in_specs = [pl.BlockSpec(mods.shape, lambda i: (0, 0))]
    for value, whole_set in inputs[:-1]:
        in_specs.append(flat if value.ndim == 2 else entry if whole_set else first)
    values = [value for value, _ in inputs[:-1]] + [inputs[-1]]
    in_specs.append(flat)
    extra = [] if before is None else [before]
    in_specs += [ANYWHERE] * len(extra)
    out_specs = [flat if len(shape.shape) == 2 else entry for shape in outputs]
    if sums:
        outputs = [*outputs, jax.ShapeDtypeStruct((sums, width), F32)]
        out_specs.append(pl.BlockSpec((sums, width), lambda i: (0, 0)))
    return pl.pallas_call(
        functools.partial(kernel, m),
        grid=(rows // step,),
        in_specs=in_specs,
        out_specs=out_specs,
        out_shape=outputs,
        input_output_aliases={1 + len(values): 0} if extra else {},
        cost_estimate=pl.CostEstimate(
            flops=weight * rows * width, bytes_accessed=32 * rows * width, transcendentals=rows
        ),
        compiler_params=None
        if name == "finish"
        else pltpu.CompilerParams(vmem_limit_bytes=16 * 2**20),
        name=name,
    )(mods, *values, *extra)


def block_range(doc_ids, rows, columns):
    by_row = doc_ids.reshape(-1, rows)
    by_column = doc_ids.reshape(-1, columns)
    low = jnp.sum(by_column[:, -1][None, :] < by_row[:, 0][:, None], axis=1, dtype=jnp.int32)
    high = jnp.sum(by_column[:, 0][None, :] <= by_row[:, -1][:, None], axis=1, dtype=jnp.int32)
    return low, high


def turn_tables(length):
    freqs = jnp.exp(-math.log(10000.0) * jnp.arange(HALF, dtype=F32) / HALF)
    angles = freqs[:, None] * jnp.arange(length, dtype=F32)[None, :]
    return jnp.cos(angles), jnp.sin(angles)


def normalize(values):
    center = values - jnp.mean(values, axis=-1, keepdims=True)
    root = lax.rsqrt(jnp.mean(center * center, axis=-1, keepdims=True) + EPSILON)
    return center * root, root


def normalize_back(grad, unit, root, stretch):
    turned = grad * (1.0 + stretch)
    return root * (
        turned
        - jnp.mean(turned, axis=-1, keepdims=True)
        - unit * jnp.mean(turned * unit, axis=-1, keepdims=True)
    )


def per_device(tokens, segments, timesteps, cotangent, w_qkv, w_out, w_up, w_down, w_ada, b_ada):
    micro_count, rows, width = tokens.shape
    heads = HEADS // 4
    length = 4 * rows
    count = dp_bits()
    tensor = lax.axis_index("tensor")
    far, near = tensor // 2, tensor % 2
    device = lax.axis_index("dp") * 4 + tensor
    falling = list(range(count - 1, -1, -1))
    rising = list(range(count))

    fq, fk = min(512, length), min(512, length)
    rq, rk = min(512, length), min(256, length)
    doc_rows = segments.astype(F32)
    bounds = [
        (block_range(segments[m], fq, fk), block_range(segments[m], rk, rq))
        for m in range(micro_count)
    ]
    tables = turn_tables(length)
    pack = jnp.concatenate([w_up, w_down.T, w_out.T], axis=1)

    states = []

    def advance(value, step):
        while len(states) <= step:
            done = falling[: len(states)]
            states.append(
                gather_block(states[-1] if states else w_qkv, falling[len(done)], done)
            )
        return after(value, states[step])

    def with_stamps(value, bit):
        return advance(value, bit - 1) if bit >= 1 else value

    def with_terms(value, bit):
        return advance(value, count - 2) if bit == 0 else value

    ready = tokens[0]
    across = swap_far(ready)
    blocks = [(ready, swap_near(ready), across, swap_near(across))]

    feature_rows = w_ada.shape[0]
    half = feature_rows * lax.axis_size("dp") * 4 // 2
    stamps = gather_relative(timesteps[:, 0].astype(F32), with_stamps)
    index = device * feature_rows + jnp.arange(feature_rows)
    freqs = jnp.exp(-math.log(10000.0) * (index % half).astype(F32) / half)
    angles = stamps[:, :, None] * freqs
    cond = jnp.where(index < half, jnp.cos(angles), jnp.sin(angles)).astype(BF16)
    cond = cond.reshape(-1, feature_rows)
    bias_size = b_ada.shape[0]
    slots = w_ada.shape[1] // bias_size
    bias = jnp.where(
        jnp.arange(slots)[:, None] == device, b_ada.astype(F32)[None, :], 0.0
    ).reshape(-1)
    terms = mod_terms(after(cond, across), w_ada, bias)
    mods = scatter_relative(terms.reshape(-1, micro_count, terms.shape[1]), with_terms)

    mods = after(mods, (blocks[0][3], tables, doc_rows, bounds))
    mods = advance(mods + swap_far(mods), count - 1)
    wq = states[-1].reshape(width, -1)
    mods = mods + swap_near(mods)

    pack = after(pack, cond)
    groups = [
        [4 * i + 2 * j + c for i in range(lax.axis_size("dp")) for j in range(2)] for c in range(2)
    ]
    pack = lax.all_gather(pack, ("dp", "tensor"), axis_index_groups=groups)
    pack = pack.reshape((-1, 2) + pack.shape[1:])
    hid = w_up.shape[1]
    part = w_out.shape[0]
    if w_up.shape[0] % 16:
        pack = pack.transpose(1, 0, 2, 3).reshape(1, 2, width, -1)

    place = tensor.astype(jnp.int32).reshape(1)
    state = []
    for m in range(micro_count):
        if m > 0:
            own = after(tokens, mods)[m]
            across = after(swap_far(own), state[-1][3])
            blocks.append((own, swap_near(own), across, swap_near(across)))
        normed_a, qkv, att_own, att_away, lse = attend(
            m, blocks[m], mods, wq, tables, doc_rows[m : m + 1],
            bounds[m][0], place, heads, fq, fk,
        )
        state.append((normed_a, qkv, (att_own, att_away), lse))

    out_pack = pack[..., 2 * hid :]
    every = jax.ShapeDtypeStruct(tokens.shape, BF16)
    wide = jax.ShapeDtypeStruct((rows, width), F32)
    low = jax.ShapeDtypeStruct((rows, width), BF16)
    output = None
    grads_out = None
    grads_feed = None
    middles = []
    for m in range(micro_count):
        last = m + 1 == micro_count
        att_own, att_away = state[m][2]
        if m == 0:
            crossing = [swap_far(state[k][2][1]) for k in range(micro_count)]
        att_far = crossing[m]
        if not last:
            att_far = after(att_far, state[m + 1][2][0])
        keep, send = out_project(place, att_own, att_far, out_pack)
        branch_a, normed_m, grad_m = by_rows(
            "before_feed",
            before_feed_kernel,
            m,
            mods,
            [(tokens, True), (cotangent, True), (keep, False), swap_near(send)],
            [wide, low, low],
        )
        if m > 0:
            normed_m = after(normed_m, middles[-1][3])
        branch_own, branch_near, d_own, d_near, grads_feed = feed(
            (normed_m, swap_near(normed_m)),
            (grad_m, swap_near(grad_m)),
            pack,
            hid,
            grads_feed,
            BF16 if last else F32,
        )
        if not last:
            (branch_own, branch_near, d_own, d_near), crossing[m + 1] = lax.optimization_barrier(
                ((branch_own, branch_near, d_own, d_near), crossing[m + 1])
            )
        if m > 0:
            (branch_own, branch_near, d_own, d_near), middles[m - 1][1][1] = (
                lax.optimization_barrier(
                    ((branch_own, branch_near, d_own, d_near), middles[m - 1][1][1])
                )
            )
        output, d_middle, grad_a, sums = by_rows(
            "after_feed",
            after_feed_kernel,
            m,
            mods,
            [
                (tokens, True),
                (cotangent, True),
                (branch_a, False),
                (branch_own, False),
                (swap_near(branch_near), False),
                (d_own, False),
                swap_near(d_near),
            ],
            [every, wide, low],
            before=output,
            sums=4,
        )
        d_att_own, d_att_far, *grads_out = out_back(
            place, (grad_a, swap_near(grad_a)), att_own, att_far, out_pack, grads_out,
            last,
        )
        if m > 0:
            middles[m - 1][1][0] = after(middles[m - 1][1][0], d_att_far)
        middles.append([d_middle, [d_att_own, swap_far(d_att_far)], sums, d_att_far])

    feed_total = lax.psum_scatter(grads_feed, "dp", scatter_dimension=0, tiled=True)
    out_far = swap_far(grads_out[1])

    mod_grads = []
    g_qkv = None
    backs = []
    for m in range(micro_count):
        normed_a, qkv, att, lse = state[m]
        keep, send, back, sums = attend_back(
            blocks[m], qkv, att, middles[m][1], lse, tables, doc_rows[m : m + 1],
            bounds[m][1], place, wq, heads, rq, rk,
        )
        if m > 0:
            (keep, send, back, sums), (backs[m - 1][2], out_half) = lax.optimization_barrier(
                ((keep, send, back, sums), (backs[m - 1][2], out_half))
            )
        elif m == 0:
            (keep, send, back, sums), out_far = lax.optimization_barrier(
                ((keep, send, back, sums), out_far)
            )
            out_keep, out_send = halves(
                by_bits(grads_out[0] + out_far.astype(F32)), 0, falling
            )
            out_half = swap_dp(out_send, 0)
        arrived = swap_near(send)
        crossing = (keep[1] + arrived[1].astype(F32)).astype(BF16)
        crossed = swap_far(crossing)
        g_qkv = project_grad(normed_a, back, g_qkv)
        if m + 1 < micro_count:
            middles[m + 1][1][0] = after(
                middles[m + 1][1][0], (crossing, g_qkv, out_send)
            )
            middles[m + 1][1][1] = after(middles[m + 1][1][1], sums)
        backs.append([keep, arrived, crossed])
        mod_grads.append(jnp.concatenate([sums.reshape(-1), middles[m][2].reshape(-1)]))
    g_last = after(g_qkv, crossing)
    middles[0][0] = after(middles[0][0], g_last)
    d_tokens = None
    wide_set = jax.ShapeDtypeStruct(tokens.shape, F32)
    for m in range(micro_count):
        keep, arrived, crossing = backs[m]
        (d_tokens,) = by_rows(
            "finish",
            finish_kernel,
            m,
            mods,
            [(tokens, True), (keep, False), (arrived, False), (crossing, False), middles[m][0]],
            [wide_set],
            before=d_tokens,
        )
        if m == 0:
            d_tokens, backs[-1][2] = lax.optimization_barrier((d_tokens, backs[-1][2]))
            first_done, crossed = d_tokens, backs[-1][2]
    sides = feed_total[:, : 2 * hid], feed_total[:, 2 * hid :]
    feed_far = swap_far(after(pick(far, sides[1], sides[0]), crossed))
    total = pick(far, sides[0], sides[1]).astype(F32) + feed_far.astype(F32)
    pieces = jnp.split(total, 2 * hid // CHUNK, axis=1)
    g_up = jnp.concatenate(pieces[0::2], axis=1)
    g_down = jnp.concatenate(pieces[1::2], axis=1).T
    d_mods = jnp.stack(mod_grads)
    d_mods = after(d_mods + swap_far(d_mods), g_last)
    d_mods = d_mods + swap_near(d_mods)
    all_mods = gather_relative(d_mods).reshape(-1, d_mods.shape[1])
    current, sent = halves(by_bits(g_last), 0, falling)
    swapped = after(swap_dp(sent, 0), (first_done, all_mods))
    current = jnp.concatenate(
        [out_keep + out_half.astype(F32), current + swapped.astype(F32)], axis=-1
    )
    for bit in rising[1:]:
        if bit == 1:
            current = after(current, crossed)
        current, sent = halves(current, bit, falling[: count - bit])
        current = current + swap_dp(sent, bit).astype(F32)
    g_out = current[:, :part].T
    g_qkv = current[:, part:]

    g_ada = lax.dot_general(
        cond.astype(F32),
        all_mods,
        TN,
        precision=lax.Precision.HIGHEST,
        preferred_element_type=F32,
    )
    g_bias = lax.dynamic_slice_in_dim(jnp.sum(all_mods, axis=0), device * bias_size, bias_size)
    return (
        output,
        d_tokens,
        g_qkv,
        g_out,
        g_up,
        g_down,
        g_ada,
        g_bias,
    )


def solution(mesh):
    return jax.shard_map(
        per_device,
        mesh=mesh,
        in_specs=(
            P(None, ("dp", "tensor"), None),
            P(None, "dp"),
            P(None, "dp"),
            P(None, ("dp", "tensor"), None),
            P("dp", "tensor"),
            P("tensor", "dp"),
            P("dp", "tensor"),
            P("tensor", "dp"),
            P(("dp", "tensor"), None),
            P(("dp", "tensor")),
        ),
        out_specs=(
            P(None, ("dp", "tensor"), None),
            P(None, ("dp", "tensor"), None),
            P("dp", "tensor"),
            P("tensor", "dp"),
            P("dp", "tensor"),
            P("tensor", "dp"),
            P(("dp", "tensor"), None),
            P(("dp", "tensor")),
        ),
        check_vma=False,
    )
```
